32 devices in a mesh: grp: 4 (over y, x), seq: 8 (over z, core).
Axes of the slice: x: 2, y: 2, z: 4, core: 2. Of those that a mesh axis runs over, the one named last changes fastest.
Arguments:
- queries: bfloat16 [1024, 64, 192], P('seq', 'grp'), may hold values from -6 to 6
- key_cache: bfloat16 [4, 8192, 192], P('grp', 'seq'), may hold values from -6 to 6
- group_value_cache: bfloat16 [4, 8192, 128], P('grp', 'seq'), may hold values from -6 to 6
- coarse_keys: bfloat16 [4, 512, 192], P('grp', 'seq'), may hold values from -6 to 6
- coarse_values: bfloat16 [4, 512, 128], P('grp', 'seq'), may hold values from -6 to 6
- hidden: bfloat16 [1024, 2560], P('seq'), may hold values from -6 to 6
- gate_weight: bfloat16 [4, 2560, 32], P('grp'), may hold values from -0.125 to 0.125
- out_weight: bfloat16 [8192, 2560], P('grp'), may hold values from -0.09375 to 0.09375
- selected: int32 [4, 8, 16], P('grp', 'seq'), may hold values from 0 to 127, as said below
Outputs:
- layer_out: bfloat16 [1024, 2560], P('seq', 'grp')
The draws below stay inside these ranges and needn't reach their ends.
Inputs may be any that keep to these rules, and one draw needn't show every extreme that they name: selected[g, t] lists 16 distinct blocks of 64 positions for tile t of group g; the first is block 0; none starts after the tile's last query position; at most 4 of them lie within one index of seq's 1024 positions.
All inputs are finite; a program needn't handle non-finite values.
Results may differ from the reference program's by a relative error of at most 0.013.
Values may be sent and summed in bfloat16 or wider, within the bound.
A program may use at most 128 MiB of HBM per device.

```python
import jax
import jax.numpy as jnp
from jax import lax

D = 2560
HEADS = 64
GROUPS = 4
DQK = 192
DV = 128
BLK = 64
SEL = 16
TILE = 128
CSTRIDE = 16
CLEN = 32
HG = 16
TILES = 8
NQ = 1024
CONTEXT = 8192
NC = 512
BLK_DEV = 16
CAP = 4
N_SEQ = 8


def draw_queries(key, part):
    full_shape = (NQ, HEADS, DQK)
    return jnp.clip(jax.random.normal(jax.random.fold_in(key, 11), full_shape, jnp.float32), -6.0, 6.0).astype(jnp.bfloat16)


def draw_key_cache(key, part):
    full_shape = (GROUPS, CONTEXT, DQK)
    return jnp.clip(jax.random.normal(jax.random.fold_in(key, 21), full_shape, jnp.float32), -6.0, 6.0).astype(jnp.bfloat16)


def draw_coarse_keys(key, part):
    full_shape = (GROUPS, NC, DQK)
    return jnp.clip(jax.random.normal(jax.random.fold_in(key, 23), full_shape, jnp.float32), -6.0, 6.0).astype(jnp.bfloat16)


def draw_selected(key, part):
    tile_ids = jnp.arange(TILES, dtype=jnp.int32)
    last_block = (CONTEXT - NQ + (tile_ids + 1) * TILE - 1) // BLK
    last_owner = last_block // BLK_DEV
    owner_ids = jnp.arange(N_SEQ, dtype=jnp.int32)
    slot_ids = jnp.arange(CAP, dtype=jnp.int32)
    owned = jnp.where(owner_ids[None, :] < last_owner[:, None], BLK_DEV, jnp.where(owner_ids[None, :] == last_owner[:, None], last_block[:, None] - last_owner[:, None] * BLK_DEV + 1, 0))
    is_first = (owner_ids[None, :] == 0).astype(jnp.int32)
    usable = owned - is_first
    slot_limit = jnp.minimum(usable, CAP - is_first)
    open_slot = slot_ids[None, None, :] < slot_limit[:, :, None]
    latest_blocks = owner_ids[None, :] >= last_owner[:, None] - 1
    preferred_blocks = (owner_ids[None, :] <= 1) | (owner_ids[None, :] >= last_owner[:, None] - 6)
    preference_boost = jnp.where(latest_blocks, 2 ** 20, 0) + jnp.where(preferred_blocks, 2 ** 16, 0)
    random_noise = jax.random.randint(jax.random.fold_in(key, 31), (GROUPS, TILES, N_SEQ, CAP), 0, 2 ** 16)
    logit_scores = random_noise + preference_boost[None, :, :, None]
    flat_ids = owner_ids[:, None] * CAP + slot_ids[None, :]
    ranked = jnp.where(open_slot[None], logit_scores + 1, 0) * (N_SEQ * CAP) + flat_ids[None, None]
    ranked = ranked.reshape(GROUPS, TILES, N_SEQ * CAP)
    top_values, chosen = lax.top_k(ranked, SEL - 1)
    chosen_owner = chosen // CAP
    chosen_slot = chosen % CAP
    rotation = jax.random.randint(jax.random.fold_in(key, 37), (GROUPS, TILES, N_SEQ), 0, 2 ** 20)
    usable_all = jnp.broadcast_to(usable[None], (GROUPS, TILES, N_SEQ))
    block_span = jnp.maximum(jnp.take_along_axis(usable_all, chosen_owner, axis=2), 1)
    start_pick = jnp.take_along_axis(rotation, chosen_owner, axis=2) % block_span
    within = (start_pick + chosen_slot) % block_span + (chosen_owner == 0).astype(jnp.int32)
    blocks = chosen_owner * BLK_DEV + within
    sink_block = jnp.zeros((GROUPS, TILES, 1), jnp.int32)
    return jnp.concatenate([sink_block, blocks.astype(jnp.int32)], axis=2)


def spiked(drawn, key, source, target, shards_of, factor):
    def block_of(dim):
        return (jnp.arange(drawn.shape[dim]) // (drawn.shape[dim] // shards_of)).reshape((-1,) + (1,) * (drawn.ndim - 1 - dim))

    first = jax.random.permutation(key, shards_of)[block_of(target)]
    far = (block_of(target) + shards_of // 2) % shards_of
    return jnp.where((block_of(source) == first) | (block_of(source) == far), factor * drawn, drawn)


def shard_levels(rng, dims, cuts, smallest, high):
    level = 1.0
    for position, blocks in cuts:
        steps = jax.random.uniform(jax.random.fold_in(jax.random.fold_in(rng, 6), position), (blocks,), jnp.float32, smallest / len(cuts), high / len(cuts))
        level = level * jnp.repeat(jnp.exp(steps), dims[position] // blocks).reshape((-1,) + (1,) * (len(dims) - 1 - position))
    return level


def gaussian(key, shape, scale, most, shards=(), kind=jnp.bfloat16):
    entries = scale * jax.random.normal(key, shape, jnp.float32)
    if shards:
        entries = entries * shard_levels(key, shape, shards, -0.22, 0.18)
    return jnp.clip(entries, -most, most).astype(kind)


def gaussian_with(key, dims, scale, most, split, heavy, kind=jnp.bfloat16):
    drawn = scale * jax.random.normal(key, dims, jnp.float32)
    if split:
        drawn = drawn * shard_levels(key, dims, split, -0.22, 0.18)
    return jnp.clip(spiked(drawn, jax.random.fold_in(key, 3), *heavy), -most, most).astype(kind)


def setup_inputs(seed: int = 0) -> dict:
    streams_of = jax.random.split(jax.random.key(seed), 10)
    return {
        "queries": draw_queries(jax.random.fold_in(streams_of[9], 71), 0),
        "key_cache": draw_key_cache(jax.random.fold_in(streams_of[9], 71), 0),
        "group_value_cache": gaussian(streams_of[2], (GROUPS, CONTEXT, DV), 1.0, 6.0, ((0, 4), (1, 8))),
        "coarse_keys": draw_coarse_keys(jax.random.fold_in(streams_of[9], 71), 0),
        "coarse_values": gaussian(streams_of[4], (GROUPS, NC, DV), 1.0, 6.0, ((0, 4), (1, 8))),
        "hidden": gaussian(streams_of[5], (NQ, D), 1.0, 6.0, ((0, 8),)),
        "gate_weight": gaussian(streams_of[6], (GROUPS, D, 2 * HG), D ** -0.5, 0.125, ((0, 4),)),
        "out_weight": gaussian_with(streams_of[7], (HEADS * DV, D), (HEADS * DV) ** -0.5, 0.09375, ((0, 4),), (0, 1, 4, 2.0)),
        "selected": draw_selected(jax.random.fold_in(streams_of[9], 71), 0),
    }


def branch(query_rows, row_pos, key_rows, value_rows, key_pos):
    logit_scores = jnp.dot(query_rows, key_rows.T, preferred_element_type=jnp.float32) * (DQK ** -0.5)
    logit_scores = jnp.where(key_pos[None, :] <= row_pos[:, None], logit_scores, -jnp.inf)
    row_max = jnp.max(logit_scores, axis=1, keepdims=True)
    weights = jnp.exp(logit_scores - row_max)
    row_total = jnp.sum(weights, axis=1, keepdims=True)
    return jnp.dot(weights.astype(jnp.bfloat16), value_rows, preferred_element_type=jnp.float32) / row_total


def reference(queries, key_cache, group_value_cache, coarse_keys, coarse_values, hidden, gate_weight, out_weight, selected):
    coarse_pos = jnp.arange(NC, dtype=jnp.int32) * CSTRIDE + CLEN - 1
    offsets = jnp.arange(BLK, dtype=jnp.int32)

    def one_tile(flat_index):
        group_index = (flat_index // TILES).astype(jnp.int32)
        tile_index = (flat_index % TILES).astype(jnp.int32)
        first_row = (tile_index * TILE).astype(jnp.int32)
        query_rows = lax.dynamic_slice(queries, (first_row, (group_index * HG).astype(jnp.int32), jnp.int32(0)), (TILE, HG, DQK)).reshape(TILE * HG, DQK)
        query_pos = (CONTEXT - NQ + first_row + jnp.arange(TILE, dtype=jnp.int32)).astype(jnp.int32)
        row_pos = jnp.repeat(query_pos, HG)
        group_keys = lax.dynamic_index_in_dim(key_cache, group_index, 0, keepdims=False)
        group_values = lax.dynamic_index_in_dim(group_value_cache, group_index, 0, keepdims=False)
        coarse_k = lax.dynamic_index_in_dim(coarse_keys, group_index, 0, keepdims=False)
        coarse_v = lax.dynamic_index_in_dim(coarse_values, group_index, 0, keepdims=False)
        coarse = branch(query_rows, row_pos, coarse_k, coarse_v, coarse_pos)
        group_sel = lax.dynamic_index_in_dim(selected, group_index, 0, keepdims=False)
        blocks = lax.dynamic_index_in_dim(group_sel, tile_index, 0, keepdims=False)
        key_pos = (blocks[:, None] * BLK + offsets[None, :]).reshape(-1).astype(jnp.int32)
        picked_block_index = branch(query_rows, row_pos, group_keys[key_pos], group_values[key_pos], key_pos)
        tile_hidden = lax.dynamic_slice_in_dim(hidden, first_row, TILE, 0)
        group_gate = lax.dynamic_index_in_dim(gate_weight, group_index, 0, keepdims=False)
        gate_logits = jnp.dot(tile_hidden, group_gate, preferred_element_type=jnp.float32)
        gate_coarse = jax.nn.sigmoid(gate_logits[:, :HG])
        gate_picked = jax.nn.sigmoid(gate_logits[:, HG:])
        mixed_heads = gate_coarse[:, :, None] * coarse.reshape(TILE, HG, DV) + gate_picked[:, :, None] * picked_block_index.reshape(TILE, HG, DV)
        return mixed_heads.astype(jnp.bfloat16).reshape(TILE, HG * DV)

    tiles_out = lax.map(one_tile, jnp.arange(GROUPS * TILES, dtype=jnp.int32))
    attended = tiles_out.reshape(GROUPS, TILES, TILE, HG * DV).transpose(1, 2, 0, 3).reshape(NQ, HEADS * DV)
    return jnp.dot(attended, out_weight, preferred_element_type=jnp.float32).astype(jnp.bfloat16)
```

```python
import functools
import math

import jax
import jax.numpy as jnp
from jax import lax
from jax.experimental import pallas as pl
from jax.experimental.pallas import tpu as pltpu
from jax.sharding import PartitionSpec as P

BLK = 64
SEL = 16
TILE = 128
CSTRIDE = 16
CLEN = 32

NEGATIVE = -1e30
FAR = 1 << 28
MESH = pl.DeviceIdType.MESH
HALF = BLK // 2
UNIT = BLK + HALF + BLK
MARK = 1 << 16


def pack(keys, values, width):
    tail = keys[:, 128:width]
    folded = jnp.concatenate([tail[:HALF], tail[HALF:]], axis=1)
    return jnp.concatenate([keys[:, :128], folded, values], axis=0)


def unpack(block):
    folded = block[BLK : BLK + HALF]
    low = lax.broadcasted_iota(jnp.int32, folded.shape, 1) < 64
    zero = jnp.zeros_like(folded)
    tails = jnp.concatenate([jnp.where(low, folded, zero), jnp.where(low, zero, folded)], axis=0)
    return jnp.concatenate([block[:BLK], tails], axis=1), block[BLK + HALF :]


def bit_of(index, bit):
    return index // bit % 2 if isinstance(index, int) else lax.rem(index // bit, 2)


def flip(index, step, size):
    shared = 0
    bit = 1
    while bit < size:
        shared = shared + bit_of(index, bit) * bit_of(step, bit) * bit
        bit *= 2
    return index + step - 2 * shared


def exchanges(count):
    found = []
    p = 1
    while p < count:
        k = p
        while k >= 1:
            for j in range(k % p, count - k, 2 * k):
                for i in range(min(k, count - j - k)):
                    if (i + j) // (2 * p) == (i + j + k) // (2 * p):
                        found.append((i + j, i + j + k))
            k //= 2
        p *= 2
    return found


def picks(read, owner, blocks, cap):
    low = owner * blocks
    found = [jnp.int32(-1)] * cap
    count = jnp.int32(0)
    for entry in range(SEL):
        block = read(entry)
        here = (block >= low) & (block < low + blocks)
        for slot in range(cap):
            found[slot] = jnp.where(here & (count == slot), block, found[slot])
        count = count + here.astype(jnp.int32)
    return found


def kernel(
    n,
    groups,
    cap,
    scale,
    own_smem,
    own_table,
    query_hbm,
    key_hbm,
    value_hbm,
    ckey_hbm,
    cvalue_hbm,
    hidden_hbm,
    gate_hbm,
    weight_hbm,
    out_ref,
    query_ref,
    key_ref,
    value_ref,
    ckey_ref,
    cvalue_ref,
    hidden_ref,
    gate_ref,
    packed,
    query_wide,
    tables,
    tables_smem,
    order_smem,
    outgoing,
    early,
    late,
    coarse,
    keys_wide,
    values_wide,
    picked_top,
    picked_sum,
    picked_out,
    coarse_top,
    coarse_sum,
    coarse_out,
    attended,
    weights,
    partial,
    arrived,
    own_part,
    input_sem,
    weight_sem,
    local_sem,
    table_send,
    table_recv,
    slot_send,
    slot_recv,
    coarse_send,
    coarse_recv,
    pass_send,
    pass_recv,
    part_send,
    part_recv,
):
    me = lax.axis_index("seq")
    group = lax.axis_index("grp")
    core = lax.rem(me, 2)
    sibling = me + 1 - 2 * core
    heads, width, _ = query_ref.shape
    blocks = value_ref.shape[0]
    columns = out_ref.shape[1]
    context = blocks * BLK * n
    span = 2 * TILE
    half = n // 2
    near = half * cap
    share = SEL // cap

    barrier = pltpu.get_barrier_semaphore()

    def greet(step, carry):
        pl.semaphore_signal(
            barrier, inc=1, device_id={"seq": flip(me, step, n)}, device_id_type=MESH
        )
        return carry

    lax.fori_loop(1, n, greet, 0)
    for step in range(1, groups):
        pl.semaphore_signal(
            barrier, inc=1, device_id={"grp": flip(group, step, groups)}, device_id_type=MESH
        )

    loads = [
        pltpu.make_async_copy(source, target, input_sem.at[index])
        for index, (source, target) in enumerate(
            [
                (ckey_hbm, ckey_ref),
                (cvalue_hbm, cvalue_ref),
                (key_hbm, key_ref),
                (value_hbm, value_ref),
                (query_hbm, query_ref),
                (hidden_hbm, hidden_ref),
                (gate_hbm, gate_ref),
            ]
        )
    ]
    for load in loads:
        load.start()

    def weight_copy(step):
        target = flip(group, step, groups)
        return pltpu.make_async_copy(
            weight_hbm.at[:, pl.ds(pl.multiple_of(target * columns, 128), columns)],
            weights.at[step],
            weight_sem.at[step],
        )

    for step in reversed(range(groups)):
        weight_copy(step).start()

    loads[0].wait()
    loads[1].wait()
    coarse[me] = pack(ckey_ref[...], cvalue_ref[...], width)
    loads[2].wait()
    loads[3].wait()
    for pair in range(blocks // 2):
        both = key_ref[:, pair * 128 : (pair + 1) * 128].T
        packed[2 * pair] = pack(both[:BLK], value_ref[2 * pair], width)
        packed[2 * pair + 1] = pack(both[BLK:], value_ref[2 * pair + 1], width)
    pl.semaphore_wait(barrier, n - 1 + groups - 1)

    def table_copy(step):
        return pltpu.make_async_remote_copy(
            src_ref=own_table,
            dst_ref=tables.at[step],
            send_sem=table_send.at[step],
            recv_sem=table_recv.at[step],
            device_id={"seq": flip(me, step, n)},
            device_id_type=MESH,
        )

    def coarse_copy(step):
        return pltpu.make_async_remote_copy(
            src_ref=coarse.at[me],
            dst_ref=coarse.at[me],
            send_sem=coarse_send.at[step],
            recv_sem=coarse_recv.at[step],
            device_id={"seq": flip(me, 2 * step, n)},
            device_id_type=MESH,
        )

    def pass_copy(step):
        origin = flip(me, 2 * step, n)
        return pltpu.make_async_remote_copy(
            src_ref=coarse.at[origin],
            dst_ref=coarse.at[origin],
            send_sem=pass_send.at[step],
            recv_sem=pass_recv.at[step],
            device_id={"seq": sibling},
            device_id_type=MESH,
        )

    def slot_copy(step, slot, across):
        if not across:
            target = early.at[step * cap + slot]
        elif slot == 0:
            target = early.at[near + step - half]
        else:
            target = late[slot - 1].at[step - half]
        return pltpu.make_async_remote_copy(
            src_ref=outgoing.at[step, slot],
            dst_ref=target,
            send_sem=slot_send.at[step, slot],
            recv_sem=slot_recv.at[step, slot],
            device_id={"seq": flip(me, step, n)},
            device_id_type=MESH,
        )

    def send_table(step, carry):
        table_copy(step).start()
        return carry

    lax.fori_loop(1, n, send_table, 0)

    def send_coarse(step, carry):
        coarse_copy(step).start()
        return carry

    lax.fori_loop(1, n // 2, send_coarse, 0)
    pass_copy(0).start()

    def wait_table(step, carry):
        table_copy(step).wait_recv()
        return carry

    lax.fori_loop(1, n, wait_table, 0)
    to_smem = pltpu.make_async_copy(tables, tables_smem, local_sem)
    to_smem.start()
    to_smem.wait()

    def fill_slots(step):
        wanted = picks(lambda entry: tables_smem[step, 0, 0, entry], me, blocks, cap)
        for slot in range(cap):
            outgoing[step, slot] = packed[jnp.maximum(wanted[slot] - me * blocks, 0)]

    def send_near(index, carry):
        step = half - index
        fill_slots(step)
        for slot in range(cap):
            slot_copy(step, slot, False).start()
        return carry

    side = me // half

    def far_step(phase, index):
        place = half - 2 - 2 * index + phase
        return flip(me, half - side + (1 - 2 * side) * place, n)

    def send_far(phase):
        def fill_far(index, carry):
            fill_slots(far_step(phase, index))
            return carry

        lax.fori_loop(0, half // 2, fill_far, 0)
        for slot in range(cap):

            def send_one(index, carry):
                slot_copy(far_step(phase, index), slot, True).start()
                return carry

            lax.fori_loop(0, half // 2, send_one, 0)

    lax.fori_loop(1, half - 1, send_near, 0)
    send_far(0)
    lax.fori_loop(half - 1, half, send_near, 0)
    send_far(1)

    def rank(step, carry):
        near_one = step < half
        owner = flip(me, step, n)
        order_smem[0, owner] = jnp.where(near_one, step * cap, near + step - half)
        order_smem[1, owner] = jnp.where(near_one, 1, half)
        return carry

    lax.fori_loop(0, n, rank, 0)
    entries = [own_smem[0, 0, entry] for entry in range(SEL)]
    owners = [entry // blocks for entry in entries]
    marks = []
    for entry in range(SEL):
        slot = jnp.int32(0)
        for other in range(entry):
            slot = slot + (owners[other] == owners[entry]).astype(jnp.int32)
        place = order_smem[0, owners[entry]] + order_smem[1, owners[entry]] * slot
        marks.append(place * MARK + entries[entry])
    for low, high in exchanges(SEL):
        marks[low], marks[high] = (
            jnp.minimum(marks[low], marks[high]),
            jnp.maximum(marks[low], marks[high]),
        )
    for entry in range(SEL):
        order_smem[2, entry] = marks[entry]
    mine = picks(lambda entry: own_smem[0, 0, entry], me, blocks, cap)
    for slot in range(cap):
        early[slot] = packed[jnp.maximum(mine[slot] - me * blocks, 0)]

    loads[4].wait()
    for head in range(heads):
        one = query_ref[head]
        query_wide[:width, head * 128 : (head + 1) * 128] = one
        query_wide[width:, head * 128 : (head + 1) * 128] = one[128:]

    first_pos = context - TILE * n + me * TILE
    row = lax.broadcasted_iota(jnp.int32, (BLK, span), 0)
    query = lax.rem(lax.broadcasted_iota(jnp.int32, (BLK, span), 1), TILE)

    def fill(place, block):
        keys, values = unpack(block)
        keys_wide[place * BLK : (place + 1) * BLK] = keys
        return values

    def attend(count, bounds, stride, top_ref, sum_ref, out, first):
        lag = row * stride - query

        def chunk(index, carry):
            here = pl.ds(pl.multiple_of(index * span, span), span)
            scores = jnp.dot(
                keys_wide[: count * BLK], query_wide[:, here], preferred_element_type=jnp.float32
            )
            scores = jnp.concatenate(
                [
                    jnp.where(lag <= bounds[block], scores[block * BLK : (block + 1) * BLK], -jnp.inf)
                    for block in range(count)
                ],
                axis=0,
            )
            top = jnp.max(scores, axis=0, keepdims=True)
            if first:
                new = jnp.maximum(top, NEGATIVE)
            else:
                old = top_ref[:, here]
                new = jnp.maximum(old, top)
                factor = jnp.exp2((old - new) * scale)
            exponents = jnp.exp2((scores - new) * scale).astype(jnp.bfloat16)
            added = jnp.dot(
                values_wide[:, : count * BLK], exponents, preferred_element_type=jnp.float32
            )
            if first:
                out[:, here] = added[:128]
                sum_ref[:, here] = added[128:129]
            else:
                out[:, here] = out[:, here] * factor + added[:128]
                sum_ref[:, here] = sum_ref[:, here] * factor + added[128:129]
            top_ref[:, here] = new
            return carry

        lax.fori_loop(0, heads * TILE // span, chunk, 0, unroll=8)

    values_wide[128:, :] = jnp.ones_like(values_wide[128:, :])

    def gather(mark, turn):
        place = mark // MARK
        block = early[jnp.minimum(place, near + half - 1)]
        for slot in range(1, turn + 1):
            start = near + slot * half
            other = late[slot - 1][jnp.clip(place - start, 0, half - 1)]
            block = jnp.where(place >= start, other, block)
        return block

    def attend_picked(turn):
        count = min(share, 4)
        for part in range(share // count):
            marks = [order_smem[2, turn * share + part * count + index] for index in range(count)]
            values = [fill(index, gather(mark, turn)) for index, mark in enumerate(marks)]
            values_wide[:128, : count * BLK] = jnp.concatenate(values, axis=0).T
            bounds = [first_pos - lax.rem(mark, MARK) * BLK for mark in marks]
            attend(count, bounds, 1, picked_top, picked_sum, picked_out, turn + part == 0)

    loads[5].wait()
    loads[6].wait()
    gates = jax.nn.sigmoid(
        lax.dot_general(
            gate_ref[...],
            hidden_ref[...],
            (((1,), (1,)), ((), ())),
            preferred_element_type=jnp.float32,
        )
    )

    def forward(step, carry):
        coarse_copy(step).wait_recv()
        pass_copy(step).start()
        return carry

    lax.fori_loop(1, n // 2, forward, 0)

    def passed(step, carry):
        pass_copy(step).wait_recv()
        return carry

    lax.fori_loop(0, n // 2, passed, 0)

    pieces = min(n, 8)

    def coarse_step(index, first):
        values = [fill(piece, coarse[index * pieces + piece]) for piece in range(pieces)]
        values_wide[:128, : pieces * BLK] = jnp.concatenate(values, axis=0).T
        start = first_pos - (CLEN - 1) - index * (pieces * BLK * CSTRIDE)
        bounds = [start - piece * (BLK * CSTRIDE) for piece in range(pieces)]
        attend(pieces, bounds, CSTRIDE, coarse_top, coarse_sum, coarse_out, first)

    coarse_step(0, True)
    if n > pieces:

        def coarse_more(index, carry):
            coarse_step(index, False)
            return carry

        lax.fori_loop(1, n // pieces, coarse_more, 0)

    def wait_near(step, carry):
        for slot in range(cap):
            slot_copy(step, slot, False).wait_recv()
        return carry

    lax.fori_loop(1, half, wait_near, 0)
    for turn in range(cap):

        def wait_far(step, carry):
            slot_copy(step, turn, True).wait_recv()
            return carry

        lax.fori_loop(half, n, wait_far, 0)
        attend_picked(turn)

    for head in range(heads):
        here = slice(head * 128, (head + 1) * 128)
        of_coarse = gates[head : head + 1] / coarse_sum[:, here]
        of_picked = gates[heads + head : heads + head + 1] / picked_sum[:, here]
        mixed = coarse_out[:, here] * of_coarse + picked_out[:, here] * of_picked
        attended[:, here] = mixed.T.astype(jnp.bfloat16)

    def part_copy(step):
        return pltpu.make_async_remote_copy(
            src_ref=partial.at[step],
            dst_ref=arrived.at[step],
            send_sem=part_send.at[step],
            recv_sem=part_recv.at[step],
            device_id={"grp": flip(group, step, groups)},
            device_id_type=MESH,
        )

    for step in reversed(range(1, groups)):
        weight_copy(step).wait()
        partial[step] = jnp.dot(
            attended[...], weights[step], preferred_element_type=jnp.float32
        ).astype(jnp.bfloat16)
        part_copy(step).start()
    weight_copy(0).wait()
    own_part[...] = jnp.dot(attended[...], weights[0], preferred_element_type=jnp.float32)

    def sent(step, carry):
        table_copy(step).wait_send()
        return carry

    lax.fori_loop(1, n, sent, 0)

    def sent_slots(across):
        def sent_one(step, carry):
            for slot in range(cap):
                slot_copy(step, slot, across).wait_send()
            return carry

        return sent_one

    lax.fori_loop(1, half, sent_slots(False), 0)
    lax.fori_loop(half, n, sent_slots(True), 0)

    def sent_coarse(step, carry):
        coarse_copy(step).wait_send()
        pass_copy(step).wait_send()
        return carry

    lax.fori_loop(1, n // 2, sent_coarse, 0)
    pass_copy(0).wait_send()
    total = own_part[...]
    for step in range(1, groups):
        part_copy(step).wait_recv()
        total = total + arrived[step].astype(jnp.float32)
    out_ref[...] = total.astype(out_ref.dtype)
    for step in range(1, groups):
        part_copy(step).wait_send()


def shards(
    queries,
    key_cache,
    group_value_cache,
    coarse_keys,
    coarse_values,
    hidden,
    gate_weight,
    out_weight,
    selected,
):
    n = lax.axis_size("seq")
    groups = lax.axis_size("grp")
    ctx_dev = key_cache.shape[1]
    heads = queries.shape[1]
    width = queries.shape[2]
    vwidth = group_value_cache.shape[2]
    rows = TILE * heads
    blocks = ctx_dev // BLK
    cap = max(1, 2 * SEL // n)
    columns = out_weight.shape[1] // groups
    pieces = min(n, 8)
    wide = max(pieces, 4) * BLK

    vmem = pl.BlockSpec(memory_space=pltpu.VMEM)
    hbm = pl.BlockSpec(memory_space=pl.ANY)
    dma = pltpu.SemaphoreType.DMA
    bf16, f32 = jnp.bfloat16, jnp.float32
    inputs = (
        queries.transpose(1, 2, 0),
        key_cache[0].T,
        group_value_cache.reshape(blocks, BLK, vwidth),
        coarse_keys[0],
        coarse_values[0],
        hidden,
        gate_weight[0].T,
    )
    return pl.pallas_call(
        functools.partial(kernel, n, groups, cap, width**-0.5 * math.log2(math.e)),
        out_shape=jax.ShapeDtypeStruct((TILE, columns), bf16),
        in_specs=[pl.BlockSpec(memory_space=pltpu.SMEM), vmem] + [hbm] * (len(inputs) + 1),
        out_specs=vmem,
        scratch_shapes=[pltpu.VMEM(one.shape, bf16) for one in inputs]
        + [
            pltpu.VMEM((blocks, UNIT, 128), bf16),
            pltpu.VMEM((256, rows), bf16),
            pltpu.VMEM((n, 1, 1, SEL), jnp.int32),
            pltpu.SMEM((n, 1, 1, SEL), jnp.int32),
            pltpu.SMEM((3, max(n, SEL)), jnp.int32),
            pltpu.VMEM((n, cap, UNIT, 128), bf16),
            pltpu.VMEM((n // 2 * (cap + 1), UNIT, 128), bf16),
            [pltpu.VMEM((n // 2, UNIT, 128), bf16) for _ in range(cap - 1)],
            pltpu.VMEM((n, UNIT, 128), bf16),
            pltpu.VMEM((wide, 256), bf16),
            pltpu.VMEM((144, wide), bf16),
            pltpu.VMEM((1, rows), f32),
            pltpu.VMEM((1, rows), f32),
            pltpu.VMEM((vwidth, rows), f32),
            pltpu.VMEM((1, rows), f32),
            pltpu.VMEM((1, rows), f32),
            pltpu.VMEM((vwidth, rows), f32),
            pltpu.VMEM((TILE, heads * vwidth), bf16),
            pltpu.VMEM((groups, heads * vwidth, columns), bf16),
            pltpu.VMEM((groups, TILE, columns), bf16),
            pltpu.VMEM((groups, TILE, columns), bf16),
            pltpu.VMEM((TILE, columns), f32),
            dma((len(inputs),)),
            dma((groups,)),
            dma,
            dma((n,)),
            dma((n,)),
            dma((n, cap)),
            dma((n, cap)),
            dma((n // 2,)),
            dma((n // 2,)),
            dma((n // 2,)),
            dma((n // 2,)),
            dma((groups,)),
            dma((groups,)),
        ],
        compiler_params=pltpu.CompilerParams(
            collective_id=0, has_side_effects=True, vmem_limit_bytes=60 * 1024 * 1024
        ),
    )(selected, selected, *inputs, out_weight)


def solution(mesh):
    return jax.shard_map(
        shards,
        mesh=mesh,
        in_specs=(
            P("seq", "grp", None),
            P("grp", "seq", None),
            P("grp", "seq", None),
            P("grp", "seq", None),
            P("grp", "seq", None),
            P("seq", None),
            P("grp", None, None),
            P("grp", None),
            P("grp", "seq", None),
        ),
        out_specs=P("seq", "grp"),
        check_vma=False,
    )
```

```python
import functools
import math

import jax
import jax.numpy as jnp
from jax import lax
from jax.experimental import pallas as pl
from jax.experimental.pallas import tpu as pltpu
from jax.sharding import PartitionSpec as P

BLK = 64
SEL = 16
TILE = 128
CSTRIDE = 16
CLEN = 32

NEGATIVE = -1e30
FAR = 1 << 28
MESH = pl.DeviceIdType.MESH
HALF = BLK // 2
UNIT = BLK + HALF + BLK
MARK = 1 << 16
PART = SEL // 4


def pack(keys, values, width):
    tail = keys[:, 128:width]
    folded = jnp.concatenate([tail[:HALF], tail[HALF:]], axis=1)
    return jnp.concatenate([keys[:, :128], folded, values], axis=0)


def unpack(block):
    folded = block[BLK : BLK + HALF]
    low = lax.broadcasted_iota(jnp.int32, folded.shape, 1) < 64
    zero = jnp.zeros_like(folded)
    tails = jnp.concatenate([jnp.where(low, folded, zero), jnp.where(low, zero, folded)], axis=0)
    return jnp.concatenate([block[:BLK], tails], axis=1), block[BLK + HALF :]


def bit_of(index, bit):
    return index // bit % 2 if isinstance(index, int) else lax.rem(index // bit, 2)


def flip(index, step, size):
    shared = 0
    bit = 1
    while bit < size:
        shared = shared + bit_of(index, bit) * bit_of(step, bit) * bit
        bit *= 2
    return index + step - 2 * shared


def exchanges(count):
    found = []
    p = 1
    while p < count:
        k = p
        while k >= 1:
            for j in range(k % p, count - k, 2 * k):
                for i in range(min(k, count - j - k)):
                    if (i + j) // (2 * p) == (i + j + k) // (2 * p):
                        found.append((i + j, i + j + k))
            k //= 2
        p *= 2
    return found


def picks(read, owner, blocks, cap):
    low = owner * blocks
    found = [jnp.int32(-1)] * cap
    count = jnp.int32(0)
    for entry in range(SEL):
        block = read(entry)
        here = (block >= low) & (block < low + blocks)
        for slot in range(cap):
            found[slot] = jnp.where(here & (count == slot), block, found[slot])
        count = count + here.astype(jnp.int32)
    return found


def kernel(
    n,
    groups,
    cap,
    scale,
    own_smem,
    own_table,
    query_hbm,
    key_hbm,
    value_hbm,
    ckey_hbm,
    cvalue_hbm,
    hidden_hbm,
    gate_hbm,
    weight_hbm,
    out_ref,
    query_ref,
    key_ref,
    value_ref,
    ckey_ref,
    cvalue_ref,
    hidden_ref,
    gate_ref,
    packed,
    query_wide,
    tables,
    tables_smem,
    order_smem,
    outgoing,
    early,
    late,
    coarse,
    keys_wide,
    values_wide,
    picked_top,
    picked_sum,
    picked_out,
    coarse_top,
    coarse_sum,
    coarse_out,
    attended,
    weights,
    partial,
    arrived,
    own_part,
    input_sem,
    weight_sem,
    local_sem,
    table_send,
    table_recv,
    slot_send,
    slot_recv,
    coarse_send,
    coarse_recv,
    pass_send,
    pass_recv,
    part_send,
    part_recv,
):
    me = lax.axis_index("seq")
    group = lax.axis_index("grp")
    core = lax.rem(me, 2)
    sibling = me + 1 - 2 * core
    heads, width, _ = query_ref.shape
    blocks = value_ref.shape[0]
    columns = out_ref.shape[1]
    context = blocks * BLK * n
    span = 2 * TILE
    half = n // 2
    chips = n // 2
    ahead = n if cap == 1 else half + half // 2
    ready = n if cap == 1 else ahead * cap
    batch = half // 2 * (cap // 2)

    barrier = pltpu.get_barrier_semaphore()

    def greet(step, carry):
        pl.semaphore_signal(
            barrier, inc=1, device_id={"seq": flip(me, step, n)}, device_id_type=MESH
        )
        return carry

    lax.fori_loop(1, n, greet, 0)
    for step in range(1, groups):
        pl.semaphore_signal(
            barrier, inc=1, device_id={"grp": flip(group, step, groups)}, device_id_type=MESH
        )

    loads = [
        pltpu.make_async_copy(source, target, input_sem.at[index])
        for index, (source, target) in enumerate(
            [
                (ckey_hbm, ckey_ref),
                (cvalue_hbm, cvalue_ref),
                (key_hbm, key_ref),
                (value_hbm, value_ref),
                (query_hbm, query_ref),
                (hidden_hbm, hidden_ref),
                (gate_hbm, gate_ref),
            ]
        )
    ]
    for load in loads:
        load.start()

    def weight_copy(step):
        target = flip(group, step, groups)
        return pltpu.make_async_copy(
            weight_hbm.at[:, pl.ds(pl.multiple_of(target * columns, 128), columns)],
            weights.at[step],
            weight_sem.at[step],
        )

    for step in reversed(range(groups)):
        weight_copy(step).start()

    loads[0].wait()
    loads[1].wait()
    coarse[me] = pack(ckey_ref[...], cvalue_ref[...], width)
    loads[2].wait()
    loads[3].wait()
    for pair in range(blocks // 2):
        both = key_ref[:, pair * 128 : (pair + 1) * 128].T
        packed[2 * pair] = pack(both[:BLK], value_ref[2 * pair], width)
        packed[2 * pair + 1] = pack(both[BLK:], value_ref[2 * pair + 1], width)
    pl.semaphore_wait(barrier, n - 1 + groups - 1)

    def table_copy(step):
        return pltpu.make_async_remote_copy(
            src_ref=own_table,
            dst_ref=tables.at[step],
            send_sem=table_send.at[step],
            recv_sem=table_recv.at[step],
            device_id={"seq": flip(me, step, n)},
            device_id_type=MESH,
        )

    def coarse_copy(held, bit):
        unit = coarse.at[flip(me, 2 * held, n)]
        return pltpu.make_async_remote_copy(
            src_ref=unit,
            dst_ref=unit,
            send_sem=coarse_send.at[held + bit],
            recv_sem=coarse_recv.at[held + bit],
            device_id={"seq": flip(me, 2 * bit, n)},
            device_id_type=MESH,
        )

    def coarse_wait(held):
        coarse_copy(0, held).wait_recv()

    def pass_copy(step):
        unit = coarse.at[flip(me, 2 * step, n)]
        return pltpu.make_async_remote_copy(
            src_ref=unit,
            dst_ref=unit,
            send_sem=pass_send.at[step],
            recv_sem=pass_recv.at[step],
            device_id={"seq": sibling},
            device_id_type=MESH,
        )

    def bits_below(bit):
        while bit > 1:
            bit //= 2
            yield bit

    def slot_copy(step, slot, late_one):
        if cap == 1:
            target = early.at[step]
        elif late_one:
            target = late[slot // (cap // 2)].at[(step - half) * (cap // 2) + slot % (cap // 2)]
        else:
            target = early.at[(step - jnp.where(step < half, 0, half // 2)) * cap + slot]
        return pltpu.make_async_remote_copy(
            src_ref=outgoing.at[step, slot],
            dst_ref=target,
            send_sem=slot_send.at[step, slot],
            recv_sem=slot_recv.at[step, slot],
            device_id={"seq": flip(me, step, n)},
            device_id_type=MESH,
        )

    def send_table(step, carry):
        table_copy(step).start()
        return carry

    lax.fori_loop(1, n, send_table, 0)

    for bit in bits_below(chips):
        coarse_copy(0, bit).start()
    pass_copy(0).start()

    def wait_table(step, carry):
        table_copy(step).wait_recv()
        return carry

    lax.fori_loop(1, n, wait_table, 0)
    to_smem = pltpu.make_async_copy(tables, tables_smem, local_sem)
    to_smem.start()
    to_smem.wait()

    def fill_slots(step):
        wanted = picks(lambda entry: tables_smem[step, 0, 0, entry], me, blocks, cap)
        for slot in range(cap):
            outgoing[step, slot] = packed[jnp.maximum(wanted[slot] - me * blocks, 0)]

    def send_near(step, carry):
        fill_slots(step)
        for slot in range(cap):
            slot_copy(step, slot, False).start()
        return carry

    side = me // half

    def far_step(phase, chip):
        return flip(me, half - side + (1 - 2 * side) * (2 * chip + phase), n)

    def send_far(phase):
        def fill_far(chip, carry):
            fill_slots(far_step(phase, chip))
            return carry

        lax.fori_loop(0, half // 2, fill_far, 0)
        if cap == 1:

            def send_single(index, carry):
                slot_copy(far_step(phase, half // 2 - 1 - index), 0, False).start()
                return carry

            lax.fori_loop(0, half // 2, send_single, 0)
            return
        lag = 2.5 if phase else -0.1
        order = [
            (slot + lag * (half // 2 - 1 - chip), chip, slot)
            for chip in range(half // 2)
            for slot in range(cap)
        ]
        for _, chip, slot in sorted(order):
            step = far_step(phase, chip)

            @pl.when(step < half + half // 2)
            def _():
                slot_copy(step, slot, True).start()

            @pl.when(step >= half + half // 2)
            def _():
                slot_copy(step, slot, False).start()

    send_far(0)
    for low in bits_below(chips):
        for held in range(low, chips, 2 * low):
            if low > 1:
                coarse_wait(held)
                for bit in bits_below(low):
                    coarse_copy(held, bit).start()
                pass_copy(held).start()
    lax.fori_loop(2, half, send_near, 0)
    lax.fori_loop(1, 2, send_near, 0)
    send_far(1)
    for held in range(1, chips, 2):
        coarse_wait(held)
        pass_copy(held).start()

    def rank(step, carry):
        owner = flip(me, step, n)
        if cap == 1:
            order_smem[0, owner] = step
            order_smem[1, owner] = 0
        else:
            last = (step >= half) & (step < half + half // 2)
            order_smem[0, owner] = jnp.where(
                last,
                ready + (step - half) * (cap // 2),
                (step - jnp.where(step < half, 0, half // 2)) * cap,
            )
            order_smem[1, owner] = jnp.where(last, batch - cap // 2, 0)
        return carry

    lax.fori_loop(0, n, rank, 0)
    entries = [own_smem[0, 0, entry] for entry in range(SEL)]
    owners = [entry // blocks for entry in entries]
    marks = []
    for entry in range(SEL):
        slot = jnp.int32(0)
        for other in range(entry):
            slot = slot + (owners[other] == owners[entry]).astype(jnp.int32)
        place = order_smem[0, owners[entry]] + slot
        place = place + jnp.where(slot >= cap // 2, order_smem[1, owners[entry]], 0)
        marks.append(place * MARK + entries[entry])
    for low, high in exchanges(SEL):
        marks[low], marks[high] = (
            jnp.minimum(marks[low], marks[high]),
            jnp.maximum(marks[low], marks[high]),
        )
    for entry in range(SEL):
        order_smem[2, entry] = marks[entry]
    mine = picks(lambda entry: own_smem[0, 0, entry], me, blocks, cap)
    for slot in range(cap):
        early[slot] = packed[jnp.maximum(mine[slot] - me * blocks, 0)]

    loads[4].wait()
    for head in range(heads):
        one = query_ref[head]
        query_wide[:width, head * 128 : (head + 1) * 128] = one
        query_wide[width:, head * 128 : (head + 1) * 128] = one[128:]

    first_pos = context - TILE * n + me * TILE
    row = lax.broadcasted_iota(jnp.int32, (BLK, span), 0)
    query = lax.rem(lax.broadcasted_iota(jnp.int32, (BLK, span), 1), TILE)

    def fill(place, block):
        keys, values = unpack(block)
        keys_wide[place * BLK : (place + 1) * BLK] = keys
        return values

    def attend(count, bounds, stride, top_ref, sum_ref, out, first):
        lag = row * stride - query
        total = heads * TILE // span

        def score(index):
            here = slice(index * span, (index + 1) * span)
            return jnp.dot(
                keys_wide[: count * BLK], query_wide[:, here], preferred_element_type=jnp.float32
            )

        def soft(index, scores):
            here = slice(index * span, (index + 1) * span)
            scores = jnp.concatenate(
                [
                    jnp.where(lag <= bounds[block], scores[block * BLK : (block + 1) * BLK], -jnp.inf)
                    for block in range(count)
                ],
                axis=0,
            )
            top = jnp.max(scores, axis=0, keepdims=True)
            if first:
                new = jnp.maximum(top, NEGATIVE)
                factor = None
            else:
                old = top_ref[:, here]
                new = jnp.maximum(old, top)
                factor = jnp.exp2((old - new) * scale)
            top_ref[:, here] = new
            return jnp.exp2((scores - new) * scale).astype(jnp.bfloat16), factor

        def value(index, exponents, factor):
            here = slice(index * span, (index + 1) * span)
            added = jnp.dot(
                values_wide[:, : count * BLK], exponents, preferred_element_type=jnp.float32
            )
            if first:
                out[:, here] = added[:128]
                sum_ref[:, here] = added[128:129]
            else:
                out[:, here] = out[:, here] * factor + added[:128]
                sum_ref[:, here] = sum_ref[:, here] * factor + added[128:129]

        ready = score(0)
        for index in range(total):
            later = score(index + 1) if index + 1 < total else None
            value(index, *soft(index, ready))
            ready = later

    values_wide[128:, :] = jnp.ones_like(values_wide[128:, :])

    def gather(mark, turn):
        place = mark // MARK
        block = early[jnp.minimum(place, ready - 1)]
        for index in range(turn):
            start = ready + index * batch
            other = late[index][jnp.clip(place - start, 0, batch - 1)]
            block = jnp.where(place >= start, other, block)
        return block

    def attend_picked(turn, start):
        marks = [order_smem[2, start + index] for index in range(PART)]
        values = [fill(index, gather(mark, turn)) for index, mark in enumerate(marks)]
        values_wide[:128, : PART * BLK] = jnp.concatenate(values, axis=0).T
        bounds = [first_pos - lax.rem(mark, MARK) * BLK for mark in marks]
        attend(PART, bounds, 1, picked_top, picked_sum, picked_out, start == 0)

    loads[5].wait()
    loads[6].wait()
    gates = jax.nn.sigmoid(
        lax.dot_general(
            gate_ref[...],
            hidden_ref[...],
            (((1,), (1,)), ((), ())),
            preferred_element_type=jnp.float32,
        )
    )

    def passed(step, carry):
        pass_copy(step).wait_recv()
        return carry

    lax.fori_loop(0, n // 2, passed, 0)

    pieces = min(n, 8)

    def coarse_step(index, first):
        values = [fill(piece, coarse[index * pieces + piece]) for piece in range(pieces)]
        values_wide[:128, : pieces * BLK] = jnp.concatenate(values, axis=0).T
        start = first_pos - (CLEN - 1) - index * (pieces * BLK * CSTRIDE)
        bounds = [start - piece * (BLK * CSTRIDE) for piece in range(pieces)]
        attend(pieces, bounds, CSTRIDE, coarse_top, coarse_sum, coarse_out, first)

    coarse_step(0, True)
    if n > pieces:

        def coarse_more(index, carry):
            coarse_step(index, False)
            return carry

        lax.fori_loop(1, n // pieces, coarse_more, 0)

    def wait_slots(start, stop, slots, late_one):
        def wait_one(step, carry):
            for slot in slots:
                slot_copy(step, slot, late_one).wait_recv()
            return carry

        lax.fori_loop(start, stop, wait_one, 0)

    if cap == 1:
        wait_slots(1, n, [0], False)
        for start in range(0, SEL, PART):
            attend_picked(0, start)
    else:
        wait_slots(1, half, range(cap), False)
        wait_slots(half + half // 2, n, range(cap), False)
        for start in range(0, SEL // 2, PART):
            attend_picked(0, start)
        for turn in range(2):
            wait_slots(half, half + half // 2, range(turn * cap // 2, (turn + 1) * cap // 2), True)
            attend_picked(turn + 1, SEL // 2 + turn * PART)

    for head in range(heads):
        here = slice(head * 128, (head + 1) * 128)
        of_coarse = gates[head : head + 1] / coarse_sum[:, here]
        of_picked = gates[heads + head : heads + head + 1] / picked_sum[:, here]
        mixed = coarse_out[:, here] * of_coarse + picked_out[:, here] * of_picked
        attended[:, here] = mixed.T.astype(jnp.bfloat16)

    def part_copy(step):
        return pltpu.make_async_remote_copy(
            src_ref=partial.at[step],
            dst_ref=arrived.at[step],
            send_sem=part_send.at[step],
            recv_sem=part_recv.at[step],
            device_id={"grp": flip(group, step, groups)},
            device_id_type=MESH,
        )

    for step in reversed(range(1, groups)):
        weight_copy(step).wait()
        partial[step] = jnp.dot(
            attended[...], weights[step], preferred_element_type=jnp.float32
        ).astype(jnp.bfloat16)
        part_copy(step).start()
    weight_copy(0).wait()
    own_part[...] = jnp.dot(attended[...], weights[0], preferred_element_type=jnp.float32)

    def sent(step, carry):
        table_copy(step).wait_send()
        return carry

    lax.fori_loop(1, n, sent, 0)

    def sent_slots(step, carry):
        for slot in range(cap):
            slot_copy(step, slot, False).wait_send()
        return carry

    lax.fori_loop(1, n, sent_slots, 0)
    for held in range(chips):
        if held:
            coarse_copy(0, held).wait_send()
        pass_copy(held).wait_send()
    total = own_part[...]
    for step in range(1, groups):
        part_copy(step).wait_recv()
        total = total + arrived[step].astype(jnp.float32)
    out_ref[...] = total.astype(out_ref.dtype)
    for step in range(1, groups):
        part_copy(step).wait_send()


def shards(
    queries,
    key_cache,
    group_value_cache,
    coarse_keys,
    coarse_values,
    hidden,
    gate_weight,
    out_weight,
    selected,
):
    n = lax.axis_size("seq")
    groups = lax.axis_size("grp")
    ctx_dev = key_cache.shape[1]
    heads = queries.shape[1]
    width = queries.shape[2]
    vwidth = group_value_cache.shape[2]
    rows = TILE * heads
    blocks = ctx_dev // BLK
    cap = max(1, 2 * SEL // n)
    columns = out_weight.shape[1] // groups
    pieces = min(n, 8)
    wide = max(pieces, PART) * BLK

    vmem = pl.BlockSpec(memory_space=pltpu.VMEM)
    hbm = pl.BlockSpec(memory_space=pl.ANY)
    dma = pltpu.SemaphoreType.DMA
    bf16, f32 = jnp.bfloat16, jnp.float32
    inputs = (
        queries.transpose(1, 2, 0),
        key_cache[0].T,
        group_value_cache.reshape(blocks, BLK, vwidth),
        coarse_keys[0],
        coarse_values[0],
        hidden,
        gate_weight[0].T,
    )
    return pl.pallas_call(
        functools.partial(kernel, n, groups, cap, width**-0.5 * math.log2(math.e)),
        out_shape=pltpu.VMEM((TILE, columns), bf16),
        in_specs=[pl.BlockSpec(memory_space=pltpu.SMEM), vmem] + [hbm] * (len(inputs) + 1),
        out_specs=vmem,
        scratch_shapes=[pltpu.VMEM(one.shape, bf16) for one in inputs]
        + [
            pltpu.VMEM((blocks, UNIT, 128), bf16),
            pltpu.VMEM((256, rows), bf16),
            pltpu.VMEM((n, 1, 1, SEL), jnp.int32),
            pltpu.SMEM((n, 1, 1, SEL), jnp.int32),
            pltpu.SMEM((3, max(n, SEL)), jnp.int32),
            pltpu.VMEM((n, cap, UNIT, 128), bf16),
            pltpu.VMEM((n if cap == 1 else n * cap * 3 // 4, UNIT, 128), bf16),
            [pltpu.VMEM((n * cap // 8, UNIT, 128), bf16) for _ in range(2 if cap > 1 else 0)],
            pltpu.VMEM((n, UNIT, 128), bf16),
            pltpu.VMEM((wide, 256), bf16),
            pltpu.VMEM((144, wide), bf16),
            pltpu.VMEM((1, rows), f32),
            pltpu.VMEM((1, rows), f32),
            pltpu.VMEM((vwidth, rows), f32),
            pltpu.VMEM((1, rows), f32),
            pltpu.VMEM((1, rows), f32),
            pltpu.VMEM((vwidth, rows), f32),
            pltpu.VMEM((TILE, heads * vwidth), bf16),
            pltpu.VMEM((groups, heads * vwidth, columns), bf16),
            pltpu.VMEM((groups, TILE, columns), bf16),
            pltpu.VMEM((groups, TILE, columns), bf16),
            pltpu.VMEM((TILE, columns), f32),
            dma((len(inputs),)),
            dma((groups,)),
            dma,
            dma((n,)),
            dma((n,)),
            dma((n, cap)),
            dma((n, cap)),
            dma((n // 2,)),
            dma((n // 2,)),
            dma((n // 2,)),
            dma((n // 2,)),
            dma((groups,)),
            dma((groups,)),
        ],
        compiler_params=pltpu.CompilerParams(
            collective_id=0, has_side_effects=True, vmem_limit_bytes=60 * 1024 * 1024
        ),
    )(selected, selected, *inputs, out_weight)


def solution(mesh):
    return jax.shard_map(
        shards,
        mesh=mesh,
        in_specs=(
            P("seq", "grp", None),
            P("grp", "seq", None),
            P("grp", "seq", None),
            P("grp", "seq", None),
            P("grp", "seq", None),
            P("seq", None),
            P("grp", None, None),
            P("grp", None),
            P("grp", "seq", None),
        ),
        out_specs=P("seq", "grp"),
        check_vma=False,
    )
```

```python
import functools
import math

import jax
import jax.numpy as jnp
from jax import lax
from jax.experimental import pallas as pl
from jax.experimental.pallas import tpu as pltpu
from jax.sharding import PartitionSpec as P

BLK = 64
SEL = 16
TILE = 128
CSTRIDE = 16
CLEN = 32

NEGATIVE = -1e30
FAR = 1 << 28
MESH = pl.DeviceIdType.MESH
HALF = BLK // 2
UNIT = BLK + HALF + BLK
MARK = 1 << 16
PART = SEL // 4


def pack(keys, values, width):
    tail = keys[:, 128:width]
    folded = jnp.concatenate([tail[:HALF], tail[HALF:]], axis=1)
    return jnp.concatenate([keys[:, :128], folded, values], axis=0)


def unpack(block):
    folded = block[BLK : BLK + HALF]
    low = lax.broadcasted_iota(jnp.int32, folded.shape, 1) < 64
    zero = jnp.zeros_like(folded)
    tails = jnp.concatenate([jnp.where(low, folded, zero), jnp.where(low, zero, folded)], axis=0)
    return jnp.concatenate([block[:BLK], tails], axis=1), block[BLK + HALF :]


def bit_of(index, bit):
    return index // bit % 2 if isinstance(index, int) else lax.rem(index // bit, 2)


def flip(index, step, size):
    shared = 0
    bit = 1
    while bit < size:
        shared = shared + bit_of(index, bit) * bit_of(step, bit) * bit
        bit *= 2
    return index + step - 2 * shared


def exchanges(count):
    found = []
    p = 1
    while p < count:
        k = p
        while k >= 1:
            for j in range(k % p, count - k, 2 * k):
                for i in range(min(k, count - j - k)):
                    if (i + j) // (2 * p) == (i + j + k) // (2 * p):
                        found.append((i + j, i + j + k))
            k //= 2
        p *= 2
    return found


def picks(read, owner, blocks, cap):
    low = owner * blocks
    found = [jnp.int32(-1)] * cap
    count = jnp.int32(0)
    for entry in range(SEL):
        block = read(entry)
        here = (block >= low) & (block < low + blocks)
        for slot in range(cap):
            found[slot] = jnp.where(here & (count == slot), block, found[slot])
        count = count + here.astype(jnp.int32)
    return found


def kernel(
    n,
    groups,
    cap,
    scale,
    own_smem,
    own_table,
    query_hbm,
    key_hbm,
    value_hbm,
    ckey_hbm,
    cvalue_hbm,
    hidden_hbm,
    gate_hbm,
    weight_hbm,
    out_ref,
    query_ref,
    key_ref,
    value_ref,
    ckey_ref,
    cvalue_ref,
    hidden_ref,
    gate_ref,
    packed,
    query_wide,
    tables_smem,
    order_smem,
    outgoing,
    early,
    late,
    coarse,
    keys_wide,
    values_wide,
    picked_top,
    picked_sum,
    picked_out,
    coarse_top,
    coarse_sum,
    coarse_out,
    attended,
    weights,
    partial,
    arrived,
    own_part,
    input_sem,
    weight_sem,
    table_send,
    table_recv,
    slot_send,
    slot_recv,
    coarse_send,
    coarse_recv,
    pass_send,
    pass_recv,
    part_send,
    part_recv,
):
    me = lax.axis_index("seq")
    group = lax.axis_index("grp")
    core = lax.rem(me, 2)
    sibling = me + 1 - 2 * core
    heads, width, _ = query_ref.shape
    blocks = value_ref.shape[0]
    columns = out_ref.shape[1]
    context = blocks * BLK * n
    span = 2 * TILE
    half = n // 2
    chips = n // 2
    staged = len(late) == 2
    ready = early.shape[0]
    batch = ready // 6
    side = me // half
    outer = (me < half - 2) | (me >= half + 2)

    barrier = pltpu.get_barrier_semaphore()

    def greet(step, carry):
        pl.semaphore_signal(
            barrier, inc=1, device_id={"seq": flip(me, step, n)}, device_id_type=MESH
        )
        return carry

    lax.fori_loop(1, n, greet, 0)
    for step in range(1, groups):
        pl.semaphore_signal(
            barrier, inc=1, device_id={"grp": flip(group, step, groups)}, device_id_type=MESH
        )

    loads = [
        pltpu.make_async_copy(source, target, input_sem.at[index])
        for index, (source, target) in enumerate(
            [
                (ckey_hbm, ckey_ref),
                (cvalue_hbm, cvalue_ref),
                (key_hbm, key_ref),
                (value_hbm, value_ref),
                (query_hbm, query_ref),
                (hidden_hbm, hidden_ref),
                (gate_hbm, gate_ref),
            ]
        )
    ]
    for load in loads:
        load.start()

    def weight_copy(step):
        target = flip(group, step, groups)
        return pltpu.make_async_copy(
            weight_hbm.at[:, pl.ds(pl.multiple_of(target * columns, 128), columns)],
            weights.at[step],
            weight_sem.at[step],
        )

    for step in reversed(range(groups)):
        weight_copy(step).start()

    loads[0].wait()
    loads[1].wait()
    coarse[me] = pack(ckey_ref[...], cvalue_ref[...], width)
    loads[2].wait()
    loads[3].wait()
    for pair in range(blocks // 2):
        both = key_ref[:, pair * 128 : (pair + 1) * 128].T
        packed[2 * pair] = pack(both[:BLK], value_ref[2 * pair], width)
        packed[2 * pair + 1] = pack(both[BLK:], value_ref[2 * pair + 1], width)
    pl.semaphore_wait(barrier, n - 1 + groups - 1)

    def table_copy(step):
        return pltpu.make_async_remote_copy(
            src_ref=own_table,
            dst_ref=tables_smem.at[step],
            send_sem=table_send.at[step],
            recv_sem=table_recv.at[step],
            device_id={"seq": flip(me, step, n)},
            device_id_type=MESH,
        )

    def coarse_copy(held, bit):
        unit = coarse.at[flip(me, 2 * held, n)]
        return pltpu.make_async_remote_copy(
            src_ref=unit,
            dst_ref=unit,
            send_sem=coarse_send.at[held + bit],
            recv_sem=coarse_recv.at[held + bit],
            device_id={"seq": flip(me, 2 * bit, n)},
            device_id_type=MESH,
        )

    def coarse_wait(held):
        coarse_copy(0, held).wait_recv()

    def pass_copy(step):
        unit = coarse.at[flip(me, 2 * step, n)]
        return pltpu.make_async_remote_copy(
            src_ref=unit,
            dst_ref=unit,
            send_sem=pass_send.at[step],
            recv_sem=pass_recv.at[step],
            device_id={"seq": sibling},
            device_id_type=MESH,
        )

    def bits_below(bit):
        while bit > 1:
            bit //= 2
            yield bit

    def slot_copy(step, slot, late_one):
        if not staged:
            target = early.at[step * cap + slot]
        elif late_one:
            target = late[slot // 2].at[lax.rem(step, 2) * 2 + slot % 2]
        else:
            place = jnp.where(step < half, step, half + lax.rem(step, 2))
            target = early.at[place * cap + slot]
        return pltpu.make_async_remote_copy(
            src_ref=outgoing.at[step, slot],
            dst_ref=target,
            send_sem=slot_send.at[step, slot],
            recv_sem=slot_recv.at[step, slot],
            device_id={"seq": flip(me, step, n)},
            device_id_type=MESH,
        )

    def send_table(step, carry):
        table_copy(step).start()
        return carry

    lax.fori_loop(1, n, send_table, 0)

    for bit in bits_below(chips):
        coarse_copy(0, bit).start()
    pass_copy(0).start()

    def fill_slots(step):
        table_copy(step).wait_recv()
        wanted = picks(lambda entry: tables_smem[step, 0, 0, entry], me, blocks, cap)
        for slot in range(cap):
            outgoing[step, slot] = packed[jnp.maximum(wanted[slot] - me * blocks, 0)]

    def send_near(step, carry):
        fill_slots(step)
        for slot in range(cap):
            slot_copy(step, slot, False).start()
        return carry

    def far_step(phase, chip):
        return flip(me, half - side + (1 - 2 * side) * (2 * chip + phase), n)

    def send_far(phase):
        def fill_far(chip, carry):
            fill_slots(far_step(phase, chip))
            return carry

        lax.fori_loop(0, half // 2, fill_far, 0)
        if not staged:

            def send_single(index, carry):
                step = far_step(phase, half // 2 - 1 - index)
                for slot in range(cap):
                    slot_copy(step, slot, False).start()
                return carry

            lax.fori_loop(0, half // 2, send_single, 0)
            return
        lag = 1.5 if phase else -0.1
        order = [
            (slot + lag * (half // 2 - 1 - chip), chip, slot)
            for chip in range(half // 2)
            for slot in range(cap)
        ]
        for _, chip, slot in sorted(order):
            step = far_step(phase, chip)

            @pl.when(outer)
            def _():
                slot_copy(step, slot, False).start()

            @pl.when(jnp.logical_not(outer))
            def _():
                slot_copy(step, slot, True).start()

    def send_chip(start, stop):
        lax.fori_loop(start, stop, send_near, 0)

    @pl.when(outer)
    def _():
        send_chip(2, half)

    @pl.when(jnp.logical_not(outer))
    def _():
        send_far(0)

    for low in bits_below(chips):
        for held in range(low, chips, 2 * low):
            if low > 1:
                coarse_wait(held)
                for bit in bits_below(low):
                    coarse_copy(held, bit).start()
                pass_copy(held).start()

    @pl.when(outer)
    def _():
        send_far(0)

    @pl.when(jnp.logical_not(outer))
    def _():
        send_chip(2, half)

    send_chip(1, 2)
    send_far(1)
    for held in range(1, chips, 2):
        coarse_wait(held)
        pass_copy(held).start()

    def rank(step, carry):
        owner = flip(me, step, n)
        if not staged:
            order_smem[0, owner] = step * cap
            order_smem[1, owner] = 0
        else:
            inner = (owner >= half - 2) & (owner < half + 2)
            last = (step >= half) & inner
            place = jnp.where(step < half, step, half + lax.rem(step, 2))
            order_smem[0, owner] = jnp.where(last, ready + lax.rem(step, 2) * 2, place * cap)
            order_smem[1, owner] = jnp.where(last, batch - 2, 0)
        return carry

    lax.fori_loop(0, n, rank, 0)
    entries = [own_smem[0, 0, entry] for entry in range(SEL)]
    owners = [entry // blocks for entry in entries]
    marks = []
    for entry in range(SEL):
        slot = jnp.int32(0)
        for other in range(entry):
            slot = slot + (owners[other] == owners[entry]).astype(jnp.int32)
        place = order_smem[0, owners[entry]] + slot
        place = place + jnp.where(slot >= 2, order_smem[1, owners[entry]], 0)
        marks.append(place * MARK + entries[entry])
    for low, high in exchanges(SEL):
        marks[low], marks[high] = (
            jnp.minimum(marks[low], marks[high]),
            jnp.maximum(marks[low], marks[high]),
        )
    for entry in range(SEL):
        order_smem[2, entry] = marks[entry]
    mine = picks(lambda entry: own_smem[0, 0, entry], me, blocks, cap)
    for slot in range(cap):
        early[slot] = packed[jnp.maximum(mine[slot] - me * blocks, 0)]

    loads[4].wait()
    for head in range(heads):
        one = query_ref[head]
        query_wide[:width, head * 128 : (head + 1) * 128] = one
        query_wide[width:, head * 128 : (head + 1) * 128] = one[128:]

    first_pos = context - TILE * n + me * TILE
    row = lax.broadcasted_iota(jnp.int32, (BLK, span), 0)
    query = lax.rem(lax.broadcasted_iota(jnp.int32, (BLK, span), 1), TILE)

    def fill(place, block):
        keys, values = unpack(block)
        keys_wide[place * BLK : (place + 1) * BLK] = keys
        return values

    def attend(count, bounds, stride, top_ref, sum_ref, out, first):
        lag = row * stride - query
        total = heads * TILE // span

        def score(index):
            here = slice(index * span, (index + 1) * span)
            return jnp.dot(
                keys_wide[: count * BLK], query_wide[:, here], preferred_element_type=jnp.float32
            )

        def soft(index, scores):
            here = slice(index * span, (index + 1) * span)
            scores = jnp.concatenate(
                [
                    jnp.where(lag <= bounds[block], scores[block * BLK : (block + 1) * BLK], -jnp.inf)
                    for block in range(count)
                ],
                axis=0,
            )
            top = jnp.max(scores, axis=0, keepdims=True)
            if first:
                new = jnp.maximum(top, NEGATIVE)
                factor = None
            else:
                old = top_ref[:, here]
                new = jnp.maximum(old, top)
                factor = jnp.exp2((old - new) * scale)
            top_ref[:, here] = new
            return jnp.exp2((scores - new) * scale).astype(jnp.bfloat16), factor

        def value(index, exponents, factor):
            here = slice(index * span, (index + 1) * span)
            added = jnp.dot(
                values_wide[:, : count * BLK], exponents, preferred_element_type=jnp.float32
            )
            if first:
                out[:, here] = added[:128]
                sum_ref[:, here] = added[128:129]
            else:
                out[:, here] = out[:, here] * factor + added[:128]
                sum_ref[:, here] = sum_ref[:, here] * factor + added[128:129]

        ready = score(0)
        for index in range(total):
            later = score(index + 1) if index + 1 < total else None
            value(index, *soft(index, ready))
            ready = later

    values_wide[128:, :] = jnp.ones_like(values_wide[128:, :])

    def gather(mark, turn):
        place = mark // MARK
        block = early[jnp.minimum(place, ready - 1)]
        for index in range(turn):
            start = ready + index * batch
            other = late[index][jnp.clip(place - start, 0, batch - 1)]
            block = jnp.where(place >= start, other, block)
        return block

    def attend_picked(turn, start):
        marks = [order_smem[2, start + index] for index in range(PART)]
        values = [fill(index, gather(mark, turn)) for index, mark in enumerate(marks)]
        values_wide[:128, : PART * BLK] = jnp.concatenate(values, axis=0).T
        bounds = [first_pos - lax.rem(mark, MARK) * BLK for mark in marks]
        attend(PART, bounds, 1, picked_top, picked_sum, picked_out, start == 0)

    loads[5].wait()
    loads[6].wait()
    gates = jax.nn.sigmoid(
        lax.dot_general(
            gate_ref[...],
            hidden_ref[...],
            (((1,), (1,)), ((), ())),
            preferred_element_type=jnp.float32,
        )
    )

    def passed(step, carry):
        pass_copy(step).wait_recv()
        return carry

    lax.fori_loop(0, n // 2, passed, 0)

    pieces = min(n, 8)

    def coarse_step(index, first):
        values = [fill(piece, coarse[index * pieces + piece]) for piece in range(pieces)]
        values_wide[:128, : pieces * BLK] = jnp.concatenate(values, axis=0).T
        start = first_pos - (CLEN - 1) - index * (pieces * BLK * CSTRIDE)
        bounds = [start - piece * (BLK * CSTRIDE) for piece in range(pieces)]
        attend(pieces, bounds, CSTRIDE, coarse_top, coarse_sum, coarse_out, first)

    coarse_step(0, True)
    if n > pieces:

        def coarse_more(index, carry):
            coarse_step(index, False)
            return carry

        lax.fori_loop(1, n // pieces, coarse_more, 0)

    def wait_slots(start, stop, slots, late_one, base=None):
        def wait_one(index, carry):
            step = index if base is None else flip(me, base + index, n)
            for slot in slots:
                slot_copy(step, slot, late_one).wait_recv()
            return carry

        lax.fori_loop(start, stop, wait_one, 0)

    if not staged:
        wait_slots(1, n, range(cap), False)
        for start in range(0, SEL, PART):
            attend_picked(0, start)
    else:
        wait_slots(1, half, range(cap), False)
        wait_slots(0, 2, range(cap), False, (n - 2) * (1 - side))
        for start in range(0, SEL // 2, PART):
            attend_picked(0, start)
        for turn in range(2):
            wait_slots(0, 2, range(turn * 2, turn * 2 + 2), True, half - 2 * side)
            attend_picked(turn + 1, SEL // 2 + turn * PART)

    for head in range(heads):
        here = slice(head * 128, (head + 1) * 128)
        of_coarse = gates[head : head + 1] / coarse_sum[:, here]
        of_picked = gates[heads + head : heads + head + 1] / picked_sum[:, here]
        mixed = coarse_out[:, here] * of_coarse + picked_out[:, here] * of_picked
        attended[:, here] = mixed.T.astype(jnp.bfloat16)

    def part_copy(step):
        return pltpu.make_async_remote_copy(
            src_ref=partial.at[step],
            dst_ref=arrived.at[step],
            send_sem=part_send.at[step],
            recv_sem=part_recv.at[step],
            device_id={"grp": flip(group, step, groups)},
            device_id_type=MESH,
        )

    for step in reversed(range(1, groups)):
        weight_copy(step).wait()
        partial[step] = jnp.dot(
            attended[...], weights[step], preferred_element_type=jnp.float32
        ).astype(jnp.bfloat16)
        part_copy(step).start()
    weight_copy(0).wait()
    own_part[...] = jnp.dot(attended[...], weights[0], preferred_element_type=jnp.float32)

    def sent(step, carry):
        table_copy(step).wait_send()
        return carry

    lax.fori_loop(1, n, sent, 0)

    def sent_slots(step, carry):
        for slot in range(cap):
            slot_copy(step, slot, False).wait_send()
        return carry

    lax.fori_loop(1, n, sent_slots, 0)
    for held in range(chips):
        if held:
            coarse_copy(0, held).wait_send()
        pass_copy(held).wait_send()
    total = own_part[...]
    for step in range(1, groups):
        part_copy(step).wait_recv()
        total = total + arrived[step].astype(jnp.float32)
    out_ref[...] = total.astype(out_ref.dtype)
    for step in range(1, groups):
        part_copy(step).wait_send()


def shards(
    queries,
    key_cache,
    group_value_cache,
    coarse_keys,
    coarse_values,
    hidden,
    gate_weight,
    out_weight,
    selected,
):
    n = lax.axis_size("seq")
    groups = lax.axis_size("grp")
    ctx_dev = key_cache.shape[1]
    heads = queries.shape[1]
    width = queries.shape[2]
    vwidth = group_value_cache.shape[2]
    rows = TILE * heads
    blocks = ctx_dev // BLK
    cap = max(1, 2 * SEL // n)
    columns = out_weight.shape[1] // groups
    pieces = min(n, 8)
    wide = max(pieces, PART) * BLK
    staged = n == 8 and cap == 4

    vmem = pl.BlockSpec(memory_space=pltpu.VMEM)
    hbm = pl.BlockSpec(memory_space=pl.ANY)
    dma = pltpu.SemaphoreType.DMA
    bf16, f32 = jnp.bfloat16, jnp.float32
    inputs = (
        queries.transpose(1, 2, 0),
        key_cache[0].T,
        group_value_cache.reshape(blocks, BLK, vwidth),
        coarse_keys[0],
        coarse_values[0],
        hidden,
        gate_weight[0].T,
    )
    return pl.pallas_call(
        functools.partial(kernel, n, groups, cap, width**-0.5 * math.log2(math.e)),
        out_shape=pltpu.VMEM((TILE, columns), bf16),
        in_specs=[pl.BlockSpec(memory_space=pltpu.SMEM), vmem] + [hbm] * (len(inputs) + 1),
        out_specs=vmem,
        scratch_shapes=[pltpu.VMEM(one.shape, bf16) for one in inputs]
        + [
            pltpu.VMEM((blocks, UNIT, 128), bf16),
            pltpu.VMEM((256, rows), bf16),
            pltpu.SMEM((n, 1, 1, SEL), jnp.int32),
            pltpu.SMEM((3, max(n, SEL)), jnp.int32),
            pltpu.VMEM((n, cap, UNIT, 128), bf16),
            pltpu.VMEM(((n - 2 * staged) * cap, UNIT, 128), bf16),
            [pltpu.VMEM((cap, UNIT, 128), bf16) for _ in range(2 * staged)],
            pltpu.VMEM((n, UNIT, 128), bf16),
            pltpu.VMEM((wide, 256), bf16),
            pltpu.VMEM((144, wide), bf16),
            pltpu.VMEM((1, rows), f32),
            pltpu.VMEM((1, rows), f32),
            pltpu.VMEM((vwidth, rows), f32),
            pltpu.VMEM((1, rows), f32),
            pltpu.VMEM((1, rows), f32),
            pltpu.VMEM((vwidth, rows), f32),
            pltpu.VMEM((TILE, heads * vwidth), bf16),
            pltpu.VMEM((groups, heads * vwidth, columns), bf16),
            pltpu.VMEM((groups, TILE, columns), bf16),
            pltpu.VMEM((groups, TILE, columns), bf16),
            pltpu.VMEM((TILE, columns), f32),
            dma((len(inputs),)),
            dma((groups,)),
            dma((n,)),
            dma((n,)),
            dma((n, cap)),
            dma((n, cap)),
            dma((n // 2,)),
            dma((n // 2,)),
            dma((n // 2,)),
            dma((n // 2,)),
            dma((groups,)),
            dma((groups,)),
        ],
        compiler_params=pltpu.CompilerParams(
            collective_id=0, has_side_effects=True, vmem_limit_bytes=60 * 1024 * 1024
        ),
    )(selected, selected, *inputs, out_weight)


def solution(mesh):
    return jax.shard_map(
        shards,
        mesh=mesh,
        in_specs=(
            P("seq", "grp", None),
            P("grp", "seq", None),
            P("grp", "seq", None),
            P("grp", "seq", None),
            P("grp", "seq", None),
            P("seq", None),
            P("grp", None, None),
            P("grp", None),
            P("grp", "seq", None),
        ),
        out_specs=P("seq", "grp"),
        check_vma=False,
    )
```

```python
import functools
import math

import jax
import jax.numpy as jnp
from jax import lax
from jax.experimental import pallas as pl
from jax.experimental.pallas import tpu as pltpu
from jax.sharding import PartitionSpec as P

BLK = 64
SEL = 16
TILE = 128
CSTRIDE = 16
CLEN = 32

NEGATIVE = -1e30
FAR = 1 << 28
MESH = pl.DeviceIdType.MESH
HALF = BLK // 2
UNIT = BLK + HALF + BLK
MARK = 1 << 16
PART = SEL // 4


def pack(keys, values, width):
    tail = keys[:, 128:width]
    folded = jnp.concatenate([tail[:HALF], tail[HALF:]], axis=1)
    return jnp.concatenate([keys[:, :128], folded, values], axis=0)


def unpack(block):
    folded = block[BLK : BLK + HALF]
    low = lax.broadcasted_iota(jnp.int32, folded.shape, 1) < 64
    zero = jnp.zeros_like(folded)
    tails = jnp.concatenate([jnp.where(low, folded, zero), jnp.where(low, zero, folded)], axis=0)
    return jnp.concatenate([block[:BLK], tails], axis=1), block[BLK + HALF :]


def bit_of(index, bit):
    return index // bit % 2 if isinstance(index, int) else lax.rem(index // bit, 2)


def flip(index, step, size):
    shared = 0
    bit = 1
    while bit < size:
        shared = shared + bit_of(index, bit) * bit_of(step, bit) * bit
        bit *= 2
    return index + step - 2 * shared


def exchanges(count):
    found = []
    p = 1
    while p < count:
        k = p
        while k >= 1:
            for j in range(k % p, count - k, 2 * k):
                for i in range(min(k, count - j - k)):
                    if (i + j) // (2 * p) == (i + j + k) // (2 * p):
                        found.append((i + j, i + j + k))
            k //= 2
        p *= 2
    return found


def picks(read, owner, blocks, cap):
    low = owner * blocks
    found = [jnp.int32(-1)] * cap
    count = jnp.int32(0)
    for entry in range(SEL):
        block = read(entry)
        here = (block >= low) & (block < low + blocks)
        for slot in range(cap):
            found[slot] = jnp.where(here & (count == slot), block, found[slot])
        count = count + here.astype(jnp.int32)
    return found


def kernel(
    n,
    groups,
    cap,
    scale,
    own_smem,
    own_table,
    query_hbm,
    key_hbm,
    value_hbm,
    ckey_hbm,
    cvalue_hbm,
    hidden_hbm,
    gate_hbm,
    weight_hbm,
    out_ref,
    query_ref,
    key_ref,
    value_ref,
    ckey_ref,
    cvalue_ref,
    hidden_ref,
    gate_ref,
    packed,
    query_wide,
    tables_smem,
    order_smem,
    outgoing,
    early,
    late,
    coarse,
    keys_wide,
    values_wide,
    picked_top,
    picked_sum,
    picked_out,
    coarse_top,
    coarse_sum,
    coarse_out,
    attended,
    weights,
    partial,
    arrived,
    own_part,
    input_sem,
    weight_sem,
    table_send,
    table_recv,
    slot_send,
    slot_recv,
    coarse_send,
    coarse_recv,
    pass_send,
    pass_recv,
    part_send,
    part_recv,
    hello,
):
    me = lax.axis_index("seq")
    group = lax.axis_index("grp")
    core = lax.rem(me, 2)
    sibling = me + 1 - 2 * core
    heads, width, _ = query_ref.shape
    blocks = value_ref.shape[0]
    columns = out_ref.shape[1]
    context = blocks * BLK * n
    span = 2 * TILE
    half = n // 2
    chips = n // 2
    staged = len(late) == 2
    ready = early.shape[0]
    batch = ready // 6
    side = me // half
    outer = (me < half - 2) | (me >= half + 2)

    barrier = pltpu.get_barrier_semaphore()

    def greet(step, carry):
        pl.semaphore_signal(
            barrier, inc=1, device_id={"seq": flip(me, step, n)}, device_id_type=MESH
        )
        return carry

    inner = jnp.logical_not(outer)
    lax.fori_loop(1, half if staged else n, greet, 0)
    if staged:

        @pl.when(inner)
        def _():
            lax.fori_loop(n - 2, n, greet, 0)

    for step in range(1, groups):
        pl.semaphore_signal(
            barrier, inc=1, device_id={"grp": flip(group, step, groups)}, device_id_type=MESH
        )

    loads = [
        pltpu.make_async_copy(source, target, input_sem.at[index])
        for index, (source, target) in enumerate(
            [
                (ckey_hbm, ckey_ref),
                (cvalue_hbm, cvalue_ref),
                (key_hbm, key_ref),
                (value_hbm, value_ref),
                (query_hbm, query_ref),
                (hidden_hbm, hidden_ref),
                (gate_hbm, gate_ref),
            ]
        )
    ]
    for load in loads:
        load.start()

    def weight_copy(step):
        target = flip(group, step, groups)
        return pltpu.make_async_copy(
            weight_hbm.at[:, pl.ds(pl.multiple_of(target * columns, 128), columns)],
            weights.at[step],
            weight_sem.at[step],
        )

    for step in reversed(range(groups)):
        weight_copy(step).start()

    loads[0].wait()
    loads[1].wait()
    coarse[me] = pack(ckey_ref[...], cvalue_ref[...], width)
    loads[2].wait()
    loads[3].wait()
    for pair in range(blocks // 2):
        both = key_ref[:, pair * 128 : (pair + 1) * 128].T
        packed[2 * pair] = pack(both[:BLK], value_ref[2 * pair], width)
        packed[2 * pair + 1] = pack(both[BLK:], value_ref[2 * pair + 1], width)
    if not staged:
        pl.semaphore_wait(barrier, n - 1 + groups - 1)
    else:

        @pl.when(inner)
        def _():
            pl.semaphore_wait(barrier, half + 1 + groups - 1)

        @pl.when(outer)
        def _():
            pl.semaphore_wait(barrier, half - 1 + groups - 1)

    def say(kind, step):
        pl.semaphore_signal(
            hello.at[kind], inc=1, device_id={"seq": flip(me, step, n)}, device_id_type=MESH
        )


    def table_copy(step):
        return pltpu.make_async_remote_copy(
            src_ref=own_table,
            dst_ref=tables_smem.at[step],
            send_sem=table_send.at[step],
            recv_sem=table_recv.at[step],
            device_id={"seq": flip(me, step, n)},
            device_id_type=MESH,
        )

    def coarse_copy(held, bit, index=None):
        unit = coarse.at[flip(me, 2 * held, n)]
        landing = flip(held, bit, chips)
        return pltpu.make_async_remote_copy(
            src_ref=unit,
            dst_ref=unit,
            send_sem=coarse_send.at[landing if index is None else index],
            recv_sem=coarse_recv.at[landing],
            device_id={"seq": flip(me, 2 * bit, n)},
            device_id_type=MESH,
        )

    hops = [(0, 3), (0, 1), (1, 3), (3, 1), (2, 1)]

    def hop(index):
        return coarse_copy(*hops[index], index)

    def coarse_pass(held):
        coarse_wait(held)
        pass_copy(held).start()

    def coarse_wait(held):
        coarse_copy(0, held).wait_recv()

    def pass_copy(step):
        unit = coarse.at[flip(me, 2 * step, n)]
        return pltpu.make_async_remote_copy(
            src_ref=unit,
            dst_ref=unit,
            send_sem=pass_send.at[step],
            recv_sem=pass_recv.at[step],
            device_id={"seq": sibling},
            device_id_type=MESH,
        )

    def bits_below(bit):
        while bit > 1:
            bit //= 2
            yield bit

    def slot_copy(step, slot, late_one):
        if not staged:
            target = early.at[step * cap + slot]
        elif late_one:
            target = late[slot // 2].at[lax.rem(step, 2) * 2 + slot % 2]
        else:
            place = jnp.where(step < half, step, half + lax.rem(step, 2))
            target = early.at[place * cap + slot]
        return pltpu.make_async_remote_copy(
            src_ref=outgoing.at[step, slot],
            dst_ref=target,
            send_sem=slot_send.at[step, slot],
            recv_sem=slot_recv.at[step, slot],
            device_id={"seq": flip(me, step, n)},
            device_id_type=MESH,
        )

    def send_table(step, carry):
        table_copy(step).start()
        return carry

    lax.fori_loop(1, half if staged else n, send_table, 0)

    if staged:

        @pl.when(inner)
        def _():
            say(0, n - 2)
            say(0, 2)
            lax.fori_loop(n - 2, n, send_table, 0)
            hop(0).start()

        hop(1).start()
    else:
        for bit in bits_below(chips):
            coarse_copy(0, bit).start()
    pass_copy(0).start()

    def fill_slots(step):
        table_copy(step).wait_recv()
        wanted = picks(lambda entry: tables_smem[step, 0, 0, entry], me, blocks, cap)
        for slot in range(cap):
            outgoing[step, slot] = packed[jnp.maximum(wanted[slot] - me * blocks, 0)]

    def send_near(step, carry):
        fill_slots(step)
        for slot in range(cap):
            slot_copy(step, slot, False).start()
        return carry

    def far_step(phase, chip):
        return flip(me, half - side + (1 - 2 * side) * (2 * chip + phase), n)

    def send_far(phase, first, last):
        def fill_far(chip, carry):
            fill_slots(far_step(phase, chip))
            return carry

        lax.fori_loop(first, last, fill_far, 0)
        if not staged:

            def send_single(index, carry):
                step = far_step(phase, half // 2 - 1 - index)
                for slot in range(cap):
                    slot_copy(step, slot, False).start()
                return carry

            lax.fori_loop(0, half // 2, send_single, 0)
            return
        lag = 1.5 if phase else -0.1
        order = [
            (slot + lag * (half // 2 - 1 - chip), chip, slot)
            for chip in range(first, last)
            for slot in range(cap)
        ]
        for _, chip, slot in sorted(order):
            step = far_step(phase, chip)

            @pl.when(outer)
            def _():
                slot_copy(step, slot, False).start()

            @pl.when(inner)
            def _():
                slot_copy(step, slot, True).start()

    def send_chip(start, stop):
        lax.fori_loop(start, stop, send_near, 0)

    if staged:

        @pl.when(inner)
        def _():
            @pl.when(side == 0)
            def _():
                send_chip(2, half)

            send_far(0, 0, 1)
            pl.semaphore_wait(hello.at[0], 1)
            say(1, 2)
            lax.fori_loop(half, n - 2, send_table, 0)

            @pl.when(side == 1)
            def _():
                send_chip(2, half)

            coarse_pass(3)
            hop(3).start()
            coarse_pass(1)
            hop(2).start()
            send_far(0, 1, 2)
            coarse_pass(2)
            hop(4).start()

        @pl.when(outer)
        def _():
            pl.semaphore_wait(hello.at[0], 1)
            lax.fori_loop(half, n - 2, send_table, 0)
            pl.semaphore_wait(hello.at[1], 1)
            lax.fori_loop(n - 2, n, send_table, 0)
            send_chip(2, half)
            send_far(0, 0, 2)

        send_chip(1, 2)
        send_far(1, 0, 2)

        @pl.when(outer)
        def _():
            for held in (1, 2, 3):
                coarse_pass(held)
    else:
        for low in bits_below(chips):
            for held in range(low, chips, 2 * low):
                if low > 1:
                    coarse_pass(held)
                    for bit in bits_below(low):
                        coarse_copy(held, bit).start()
        send_chip(1, half)
        send_far(0, 0, half // 2)
        send_far(1, 0, half // 2)
        for held in range(1, chips, 2):
            coarse_pass(held)

    def rank(step, carry):
        owner = flip(me, step, n)
        if not staged:
            order_smem[0, owner] = step * cap
            order_smem[1, owner] = 0
        else:
            inner = (owner >= half - 2) & (owner < half + 2)
            last = (step >= half) & inner
            place = jnp.where(step < half, step, half + lax.rem(step, 2))
            order_smem[0, owner] = jnp.where(last, ready + lax.rem(step, 2) * 2, place * cap)
            order_smem[1, owner] = jnp.where(last, batch - 2, 0)
        return carry

    lax.fori_loop(0, n, rank, 0)
    entries = [own_smem[0, 0, entry] for entry in range(SEL)]
    owners = [entry // blocks for entry in entries]
    marks = []
    for entry in range(SEL):
        slot = jnp.int32(0)
        for other in range(entry):
            slot = slot + (owners[other] == owners[entry]).astype(jnp.int32)
        place = order_smem[0, owners[entry]] + slot
        place = place + jnp.where(slot >= 2, order_smem[1, owners[entry]], 0)
        marks.append(place * MARK + entries[entry])
    for low, high in exchanges(SEL):
        marks[low], marks[high] = (
            jnp.minimum(marks[low], marks[high]),
            jnp.maximum(marks[low], marks[high]),
        )
    for entry in range(SEL):
        order_smem[2, entry] = marks[entry]
    mine = picks(lambda entry: own_smem[0, 0, entry], me, blocks, cap)
    for slot in range(cap):
        early[slot] = packed[jnp.maximum(mine[slot] - me * blocks, 0)]

    loads[4].wait()
    for head in range(heads):
        one = query_ref[head]
        query_wide[:width, head * 128 : (head + 1) * 128] = one
        query_wide[width:, head * 128 : (head + 1) * 128] = one[128:]

    first_pos = context - TILE * n + me * TILE
    row = lax.broadcasted_iota(jnp.int32, (BLK, span), 0)
    query = lax.rem(lax.broadcasted_iota(jnp.int32, (BLK, span), 1), TILE)

    def fill(place, block):
        keys, values = unpack(block)
        keys_wide[place * BLK : (place + 1) * BLK] = keys
        return values

    def attend(count, bounds, stride, top_ref, sum_ref, out, first):
        lag = row * stride - query
        total = heads * TILE // span

        def score(index):
            here = slice(index * span, (index + 1) * span)
            return jnp.dot(
                keys_wide[: count * BLK], query_wide[:, here], preferred_element_type=jnp.float32
            )

        def soft(index, scores):
            here = slice(index * span, (index + 1) * span)
            scores = jnp.concatenate(
                [
                    jnp.where(lag <= bounds[block], scores[block * BLK : (block + 1) * BLK], -jnp.inf)
                    for block in range(count)
                ],
                axis=0,
            )
            top = jnp.max(scores, axis=0, keepdims=True)
            if first:
                new = jnp.maximum(top, NEGATIVE)
                factor = None
            else:
                old = top_ref[:, here]
                new = jnp.maximum(old, top)
                factor = jnp.exp2((old - new) * scale)
            top_ref[:, here] = new
            return jnp.exp2((scores - new) * scale).astype(jnp.bfloat16), factor

        def value(index, exponents, factor):
            here = slice(index * span, (index + 1) * span)
            added = jnp.dot(
                values_wide[:, : count * BLK], exponents, preferred_element_type=jnp.float32
            )
            if first:
                out[:, here] = added[:128]
                sum_ref[:, here] = added[128:129]
            else:
                out[:, here] = out[:, here] * factor + added[:128]
                sum_ref[:, here] = sum_ref[:, here] * factor + added[128:129]

        ready = score(0)
        for index in range(total):
            later = score(index + 1) if index + 1 < total else None
            value(index, *soft(index, ready))
            ready = later

    values_wide[128:, :] = jnp.ones_like(values_wide[128:, :])

    def gather(mark, turn):
        place = mark // MARK
        block = early[jnp.minimum(place, ready - 1)]
        for index in range(turn):
            start = ready + index * batch
            other = late[index][jnp.clip(place - start, 0, batch - 1)]
            block = jnp.where(place >= start, other, block)
        return block

    def attend_picked(turn, start):
        marks = [order_smem[2, start + index] for index in range(PART)]
        values = [fill(index, gather(mark, turn)) for index, mark in enumerate(marks)]
        values_wide[:128, : PART * BLK] = jnp.concatenate(values, axis=0).T
        bounds = [first_pos - lax.rem(mark, MARK) * BLK for mark in marks]
        attend(PART, bounds, 1, picked_top, picked_sum, picked_out, start == 0)

    loads[5].wait()
    loads[6].wait()
    gates = jax.nn.sigmoid(
        lax.dot_general(
            gate_ref[...],
            hidden_ref[...],
            (((1,), (1,)), ((), ())),
            preferred_element_type=jnp.float32,
        )
    )

    def passed(step, carry):
        pass_copy(step).wait_recv()
        return carry

    lax.fori_loop(0, n // 2, passed, 0)

    pieces = min(n, 8)

    def coarse_step(index, first):
        values = [fill(piece, coarse[index * pieces + piece]) for piece in range(pieces)]
        values_wide[:128, : pieces * BLK] = jnp.concatenate(values, axis=0).T
        start = first_pos - (CLEN - 1) - index * (pieces * BLK * CSTRIDE)
        bounds = [start - piece * (BLK * CSTRIDE) for piece in range(pieces)]
        attend(pieces, bounds, CSTRIDE, coarse_top, coarse_sum, coarse_out, first)

    coarse_step(0, True)
    if n > pieces:

        def coarse_more(index, carry):
            coarse_step(index, False)
            return carry

        lax.fori_loop(1, n // pieces, coarse_more, 0)

    def wait_slots(start, stop, slots, late_one, base=None):
        def wait_one(index, carry):
            step = index if base is None else flip(me, base + index, n)
            for slot in slots:
                slot_copy(step, slot, late_one).wait_recv()
            return carry

        lax.fori_loop(start, stop, wait_one, 0)

    if not staged:
        wait_slots(1, n, range(cap), False)
        for start in range(0, SEL, PART):
            attend_picked(0, start)
    else:
        wait_slots(1, half, range(cap), False)
        wait_slots(0, 2, range(cap), False, (n - 2) * (1 - side))
        for start in range(0, SEL // 2, PART):
            attend_picked(0, start)
        for turn in range(2):
            wait_slots(0, 2, range(turn * 2, turn * 2 + 2), True, half - 2 * side)
            attend_picked(turn + 1, SEL // 2 + turn * PART)

    for head in range(heads):
        here = slice(head * 128, (head + 1) * 128)
        of_coarse = gates[head : head + 1] / coarse_sum[:, here]
        of_picked = gates[heads + head : heads + head + 1] / picked_sum[:, here]
        mixed = coarse_out[:, here] * of_coarse + picked_out[:, here] * of_picked
        attended[:, here] = mixed.T.astype(jnp.bfloat16)

    def part_copy(step):
        return pltpu.make_async_remote_copy(
            src_ref=partial.at[step],
            dst_ref=arrived.at[step],
            send_sem=part_send.at[step],
            recv_sem=part_recv.at[step],
            device_id={"grp": flip(group, step, groups)},
            device_id_type=MESH,
        )

    for step in reversed(range(1, groups)):
        weight_copy(step).wait()
        partial[step] = jnp.dot(
            attended[...], weights[step], preferred_element_type=jnp.float32
        ).astype(jnp.bfloat16)
        part_copy(step).start()
    weight_copy(0).wait()
    own_part[...] = jnp.dot(attended[...], weights[0], preferred_element_type=jnp.float32)

    def sent(step, carry):
        table_copy(step).wait_send()
        return carry

    lax.fori_loop(1, n, sent, 0)

    def sent_slots(step, carry):
        for slot in range(cap):
            slot_copy(step, slot, False).wait_send()
        return carry

    lax.fori_loop(1, n, sent_slots, 0)
    for held in range(chips):
        if held and not staged:
            coarse_copy(0, held).wait_send()
        pass_copy(held).wait_send()
    if staged:
        hop(1).wait_send()

        @pl.when(inner)
        def _():
            for index in (0, 2, 3, 4):
                hop(index).wait_send()

    total = own_part[...]
    for step in range(1, groups):
        part_copy(step).wait_recv()
        total = total + arrived[step].astype(jnp.float32)
    out_ref[...] = total.astype(out_ref.dtype)
    for step in range(1, groups):
        part_copy(step).wait_send()


def shards(
    queries,
    key_cache,
    group_value_cache,
    coarse_keys,
    coarse_values,
    hidden,
    gate_weight,
    out_weight,
    selected,
):
    n = lax.axis_size("seq")
    groups = lax.axis_size("grp")
    ctx_dev = key_cache.shape[1]
    heads = queries.shape[1]
    width = queries.shape[2]
    vwidth = group_value_cache.shape[2]
    rows = TILE * heads
    blocks = ctx_dev // BLK
    cap = max(1, 2 * SEL // n)
    columns = out_weight.shape[1] // groups
    pieces = min(n, 8)
    wide = max(pieces, PART) * BLK
    staged = n == 8 and cap == 4

    vmem = pl.BlockSpec(memory_space=pltpu.VMEM)
    hbm = pl.BlockSpec(memory_space=pl.ANY)
    dma = pltpu.SemaphoreType.DMA
    bf16, f32 = jnp.bfloat16, jnp.float32
    inputs = (
        queries.transpose(1, 2, 0),
        key_cache[0].T,
        group_value_cache.reshape(blocks, BLK, vwidth),
        coarse_keys[0],
        coarse_values[0],
        hidden,
        gate_weight[0].T,
    )
    return pl.pallas_call(
        functools.partial(kernel, n, groups, cap, width**-0.5 * math.log2(math.e)),
        out_shape=pltpu.VMEM((TILE, columns), bf16),
        in_specs=[pl.BlockSpec(memory_space=pltpu.SMEM), vmem] + [hbm] * (len(inputs) + 1),
        out_specs=vmem,
        scratch_shapes=[pltpu.VMEM(one.shape, bf16) for one in inputs]
        + [
            pltpu.VMEM((blocks, UNIT, 128), bf16),
            pltpu.VMEM((256, rows), bf16),
            pltpu.SMEM((n, 1, 1, SEL), jnp.int32),
            pltpu.SMEM((3, max(n, SEL)), jnp.int32),
            pltpu.VMEM((n, cap, UNIT, 128), bf16),
            pltpu.VMEM(((n - 2 * staged) * cap, UNIT, 128), bf16),
            [pltpu.VMEM((cap, UNIT, 128), bf16) for _ in range(2 * staged)],
            pltpu.VMEM((n, UNIT, 128), bf16),
            pltpu.VMEM((wide, 256), bf16),
            pltpu.VMEM((144, wide), bf16),
            pltpu.VMEM((1, rows), f32),
            pltpu.VMEM((1, rows), f32),
            pltpu.VMEM((vwidth, rows), f32),
            pltpu.VMEM((1, rows), f32),
            pltpu.VMEM((1, rows), f32),
            pltpu.VMEM((vwidth, rows), f32),
            pltpu.VMEM((TILE, heads * vwidth), bf16),
            pltpu.VMEM((groups, heads * vwidth, columns), bf16),
            pltpu.VMEM((groups, TILE, columns), bf16),
            pltpu.VMEM((groups, TILE, columns), bf16),
            pltpu.VMEM((TILE, columns), f32),
            dma((len(inputs),)),
            dma((groups,)),
            dma((n,)),
            dma((n,)),
            dma((n, cap)),
            dma((n, cap)),
            dma((n // 2 + 1,)),
            dma((n // 2,)),
            dma((n // 2,)),
            dma((n // 2,)),
            dma((groups,)),
            dma((groups,)),
            pltpu.SemaphoreType.REGULAR((2,)),
        ],
        compiler_params=pltpu.CompilerParams(
            collective_id=0, has_side_effects=True, vmem_limit_bytes=60 * 1024 * 1024
        ),
    )(selected, selected, *inputs, out_weight)


def solution(mesh):
    return jax.shard_map(
        shards,
        mesh=mesh,
        in_specs=(
            P("seq", "grp", None),
            P("grp", "seq", None),
            P("grp", "seq", None),
            P("grp", "seq", None),
            P("grp", "seq", None),
            P("seq", None),
            P("grp", None, None),
            P("grp", None),
            P("grp", "seq", None),
        ),
        out_specs=P("seq", "grp"),
        check_vma=False,
    )
```

```python
import functools
import math

import jax
import jax.numpy as jnp
from jax import lax
from jax.experimental import pallas as pl
from jax.experimental.pallas import tpu as pltpu
from jax.sharding import PartitionSpec as P

BLK = 64
SEL = 16
TILE = 128
CSTRIDE = 16
CLEN = 32

NEGATIVE = -1e30
FAR = 1 << 28
MESH = pl.DeviceIdType.MESH
HALF = BLK // 2
UNIT = BLK + HALF + BLK
MARK = 1 << 16
PART = SEL // 4


def pack(keys, values, width):
    tail = keys[:, 128:width]
    folded = jnp.concatenate([tail[:HALF], tail[HALF:]], axis=1)
    return jnp.concatenate([keys[:, :128], folded, values], axis=0)


def unpack(block):
    folded = block[BLK : BLK + HALF]
    low = lax.broadcasted_iota(jnp.int32, folded.shape, 1) < 64
    zero = jnp.zeros_like(folded)
    tails = jnp.concatenate([jnp.where(low, folded, zero), jnp.where(low, zero, folded)], axis=0)
    return jnp.concatenate([block[:BLK], tails], axis=1), block[BLK + HALF :]


def bit_of(index, bit):
    return index // bit % 2 if isinstance(index, int) else lax.rem(index // bit, 2)


def flip(index, step, size):
    shared = 0
    bit = 1
    while bit < size:
        shared = shared + bit_of(index, bit) * bit_of(step, bit) * bit
        bit *= 2
    return index + step - 2 * shared


def exchanges(count):
    found = []
    p = 1
    while p < count:
        k = p
        while k >= 1:
            for j in range(k % p, count - k, 2 * k):
                for i in range(min(k, count - j - k)):
                    if (i + j) // (2 * p) == (i + j + k) // (2 * p):
                        found.append((i + j, i + j + k))
            k //= 2
        p *= 2
    return found


def picks(read, owner, blocks, cap):
    low = owner * blocks
    found = [jnp.int32(-1)] * cap
    count = jnp.int32(0)
    for entry in range(SEL):
        block = read(entry)
        here = (block >= low) & (block < low + blocks)
        for slot in range(cap):
            found[slot] = jnp.where(here & (count == slot), block, found[slot])
        count = count + here.astype(jnp.int32)
    return found


def kernel(
    n,
    groups,
    cap,
    scale,
    own_smem,
    own_table,
    query_hbm,
    key_hbm,
    value_hbm,
    ckey_hbm,
    cvalue_hbm,
    hidden_hbm,
    gate_hbm,
    weight_hbm,
    out_ref,
    query_ref,
    key_ref,
    value_ref,
    ckey_ref,
    cvalue_ref,
    hidden_ref,
    gate_ref,
    packed,
    query_wide,
    tables_smem,
    order_smem,
    outgoing,
    early,
    late,
    coarse,
    keys_wide,
    values_wide,
    picked_top,
    picked_sum,
    picked_out,
    coarse_top,
    coarse_sum,
    coarse_out,
    attended,
    weights,
    partial,
    arrived,
    own_part,
    input_sem,
    weight_sem,
    table_send,
    table_recv,
    slot_send,
    slot_recv,
    coarse_send,
    coarse_recv,
    pass_send,
    pass_recv,
    part_send,
    part_recv,
    hello,
):
    me = lax.axis_index("seq")
    group = lax.axis_index("grp")
    core = lax.rem(me, 2)
    sibling = me + 1 - 2 * core
    heads, width, _ = query_ref.shape
    blocks = value_ref.shape[0]
    columns = out_ref.shape[1]
    context = blocks * BLK * n
    span = 2 * TILE
    half = n // 2
    chips = n // 2
    staged = len(late) > 0
    ready = early.shape[0]
    starts = [ready, ready + 4, ready + 6]
    side = me // half
    outer = (me < half - 2) | (me >= half + 2)

    barrier = pltpu.get_barrier_semaphore()

    def greet(step, carry):
        pl.semaphore_signal(
            barrier, inc=1, device_id={"seq": flip(me, step, n)}, device_id_type=MESH
        )
        return carry

    inner = jnp.logical_not(outer)
    lax.fori_loop(1, half if staged else n, greet, 0)
    if staged:

        @pl.when(inner)
        def _():
            lax.fori_loop(n - 2, n, greet, 0)

    for step in range(1, groups):
        pl.semaphore_signal(
            barrier, inc=1, device_id={"grp": flip(group, step, groups)}, device_id_type=MESH
        )

    loads = [
        pltpu.make_async_copy(source, target, input_sem.at[index])
        for index, (source, target) in enumerate(
            [
                (ckey_hbm, ckey_ref),
                (cvalue_hbm, cvalue_ref),
                (key_hbm, key_ref),
                (value_hbm, value_ref),
                (query_hbm, query_ref),
                (hidden_hbm, hidden_ref),
                (gate_hbm, gate_ref),
            ]
        )
    ]
    for load in loads:
        load.start()

    def weight_copy(step):
        target = flip(group, step, groups)
        return pltpu.make_async_copy(
            weight_hbm.at[:, pl.ds(pl.multiple_of(target * columns, 128), columns)],
            weights.at[step],
            weight_sem.at[step],
        )

    for step in reversed(range(groups)):
        weight_copy(step).start()

    loads[0].wait()
    loads[1].wait()
    coarse[me] = pack(ckey_ref[...], cvalue_ref[...], width)
    loads[2].wait()
    loads[3].wait()
    for pair in range(blocks // 2):
        both = key_ref[:, pair * 128 : (pair + 1) * 128].T
        packed[2 * pair] = pack(both[:BLK], value_ref[2 * pair], width)
        packed[2 * pair + 1] = pack(both[BLK:], value_ref[2 * pair + 1], width)
    if not staged:
        pl.semaphore_wait(barrier, n - 1 + groups - 1)
    else:

        @pl.when(inner)
        def _():
            pl.semaphore_wait(barrier, half + 1 + groups - 1)

        @pl.when(outer)
        def _():
            pl.semaphore_wait(barrier, half - 1 + groups - 1)

    def say(kind, step):
        pl.semaphore_signal(
            hello.at[kind], inc=1, device_id={"seq": flip(me, step, n)}, device_id_type=MESH
        )


    def table_copy(step):
        return pltpu.make_async_remote_copy(
            src_ref=own_table,
            dst_ref=tables_smem.at[step],
            send_sem=table_send.at[step],
            recv_sem=table_recv.at[step],
            device_id={"seq": flip(me, step, n)},
            device_id_type=MESH,
        )

    def coarse_copy(held, bit, index=None):
        unit = coarse.at[flip(me, 2 * held, n)]
        landing = flip(held, bit, chips)
        return pltpu.make_async_remote_copy(
            src_ref=unit,
            dst_ref=unit,
            send_sem=coarse_send.at[landing if index is None else index],
            recv_sem=coarse_recv.at[landing],
            device_id={"seq": flip(me, 2 * bit, n)},
            device_id_type=MESH,
        )

    hops = [(0, 3), (0, 1), (1, 3), (3, 1), (2, 1)]

    def hop(index):
        return coarse_copy(*hops[index], index)

    def coarse_pass(held):
        coarse_wait(held)
        pass_copy(held).start()

    def coarse_wait(held):
        coarse_copy(0, held).wait_recv()

    def pass_copy(step):
        unit = coarse.at[flip(me, 2 * step, n)]
        return pltpu.make_async_remote_copy(
            src_ref=unit,
            dst_ref=unit,
            send_sem=pass_send.at[step],
            recv_sem=pass_recv.at[step],
            device_id={"seq": sibling},
            device_id_type=MESH,
        )

    def bits_below(bit):
        while bit > 1:
            bit //= 2
            yield bit

    def slot_copy(step, slot, late_one):
        if not staged:
            target = early.at[step * cap + slot]
        elif late_one:
            odd = lax.rem(step, 2)
            target = late[0].at[odd * 2 + slot] if slot < 2 else late[slot - 1].at[odd]
        else:
            place = jnp.where(step < half, step, half + lax.rem(step, 2))
            target = early.at[place * cap + slot]
        return pltpu.make_async_remote_copy(
            src_ref=outgoing.at[step, slot],
            dst_ref=target,
            send_sem=slot_send.at[step, slot],
            recv_sem=slot_recv.at[step, slot],
            device_id={"seq": flip(me, step, n)},
            device_id_type=MESH,
        )

    def send_table(step, carry):
        table_copy(step).start()
        return carry

    lax.fori_loop(1, half if staged else n, send_table, 0)

    if staged:

        @pl.when(inner)
        def _():
            say(0, n - 2)
            say(0, 2)
            lax.fori_loop(n - 2, n, send_table, 0)
            hop(0).start()

        hop(1).start()
    else:
        for bit in bits_below(chips):
            coarse_copy(0, bit).start()
    pass_copy(0).start()

    def fill_slots(step):
        table_copy(step).wait_recv()
        wanted = picks(lambda entry: tables_smem[step, 0, 0, entry], me, blocks, cap)
        for slot in range(cap):
            outgoing[step, slot] = packed[jnp.maximum(wanted[slot] - me * blocks, 0)]

    def send_near(step, carry):
        fill_slots(step)
        for slot in range(cap):
            slot_copy(step, slot, False).start()
        return carry

    def far_step(phase, chip):
        return flip(me, half - side + (1 - 2 * side) * (2 * chip + phase), n)

    def send_far(phase, first, last):
        def fill_far(chip, carry):
            fill_slots(far_step(phase, chip))
            return carry

        lax.fori_loop(first, last, fill_far, 0)
        if not staged:

            def send_single(index, carry):
                step = far_step(phase, half // 2 - 1 - index)
                for slot in range(cap):
                    slot_copy(step, slot, False).start()
                return carry

            lax.fori_loop(0, half // 2, send_single, 0)
            return
        lag = 1.5 if phase else -0.1
        order = [
            (slot + lag * (half // 2 - 1 - chip), chip, slot)
            for chip in range(first, last)
            for slot in range(cap)
        ]
        for _, chip, slot in sorted(order):
            step = far_step(phase, chip)

            @pl.when(outer)
            def _():
                slot_copy(step, slot, False).start()

            @pl.when(inner)
            def _():
                slot_copy(step, slot, True).start()

    def send_chip(start, stop):
        lax.fori_loop(start, stop, send_near, 0)

    if staged:

        @pl.when(inner)
        def _():
            @pl.when(side == 0)
            def _():
                send_chip(2, half)

            send_far(0, 0, 1)
            pl.semaphore_wait(hello.at[0], 1)
            say(1, 2)
            lax.fori_loop(half, n - 2, send_table, 0)

            @pl.when(side == 1)
            def _():
                send_chip(2, half)

            coarse_pass(3)
            hop(3).start()
            coarse_pass(1)
            hop(2).start()
            send_far(0, 1, 2)
            coarse_pass(2)
            hop(4).start()

        @pl.when(outer)
        def _():
            pl.semaphore_wait(hello.at[0], 1)
            lax.fori_loop(half, n - 2, send_table, 0)
            pl.semaphore_wait(hello.at[1], 1)
            lax.fori_loop(n - 2, n, send_table, 0)
            send_chip(2, half)
            send_far(0, 0, 2)

        send_chip(1, 2)
        send_far(1, 0, 2)

        @pl.when(outer)
        def _():
            for held in (1, 2, 3):
                coarse_pass(held)
    else:
        for low in bits_below(chips):
            for held in range(low, chips, 2 * low):
                if low > 1:
                    coarse_pass(held)
                    for bit in bits_below(low):
                        coarse_copy(held, bit).start()
        send_chip(1, half)
        send_far(0, 0, half // 2)
        send_far(1, 0, half // 2)
        for held in range(1, chips, 2):
            coarse_pass(held)

    def rank(step, carry):
        owner = flip(me, step, n)
        if not staged:
            for line, value in enumerate([step * cap, step * cap, 1]):
                order_smem[line, owner] = value
        else:
            central = (owner >= half - 2) & (owner < half + 2)
            last = (step >= half) & central
            odd = lax.rem(step, 2)
            place = jnp.where(step < half, step, half + odd) * cap
            order_smem[0, owner] = jnp.where(last, ready + odd * 2, place)
            order_smem[1, owner] = jnp.where(last, ready + odd, place)
            order_smem[2, owner] = jnp.where(last, 2, 1)
        return carry

    lax.fori_loop(0, n, rank, 0)
    newest = (context - TILE * n + me * TILE) // (blocks * BLK)
    entries = [own_smem[0, 0, entry] for entry in range(SEL)]
    owners = [entry // blocks for entry in entries]
    marks = []
    for entry in range(SEL):
        slot = jnp.int32(0)
        for other in range(entry):
            slot = slot + (owners[other] == owners[entry]).astype(jnp.int32)
        place = jnp.where(
            slot < 2,
            order_smem[0, owners[entry]] + slot,
            order_smem[1, owners[entry]] + slot * order_smem[2, owners[entry]],
        )
        place = jnp.where(owners[entry] == newest, place, place + n * cap)
        marks.append(place * MARK + entries[entry])
    for low, high in exchanges(SEL):
        marks[low], marks[high] = (
            jnp.minimum(marks[low], marks[high]),
            jnp.maximum(marks[low], marks[high]),
        )
    for entry in range(SEL):
        order_smem[3, entry] = marks[entry]
    mine = picks(lambda entry: own_smem[0, 0, entry], me, blocks, cap)
    for slot in range(cap):
        early[slot] = packed[jnp.maximum(mine[slot] - me * blocks, 0)]

    loads[4].wait()
    for head in range(heads):
        one = query_ref[head]
        query_wide[:width, head * 128 : (head + 1) * 128] = one
        query_wide[width:, head * 128 : (head + 1) * 128] = one[128:]

    first_pos = context - TILE * n + me * TILE
    row = lax.broadcasted_iota(jnp.int32, (BLK, span), 0)
    query = lax.rem(lax.broadcasted_iota(jnp.int32, (BLK, span), 1), TILE)

    def fill(place, block):
        keys, values = unpack(block)
        keys_wide[place * BLK : (place + 1) * BLK] = keys
        return values

    def gate_row(index, kind):
        first_head = kind * heads + index * (span // TILE)
        return jnp.concatenate(
            [gates[first_head + other : first_head + other + 1] for other in range(span // TILE)],
            axis=1,
        )

    def close(index, picked, total):
        here = slice(index * span, (index + 1) * span)
        mixed = coarse_out[:, here] + picked * (gate_row(index, 1) / total)
        mixed = mixed.astype(jnp.bfloat16)
        for other in range(span // TILE):
            start = index * span + other * TILE
            attended[:, start : start + TILE] = mixed[:, other * TILE : (other + 1) * TILE].T

    def attend(count, bounds, stride, top_ref, sum_ref, out, first, closing=False):
        lag = row * stride - query
        total = heads * TILE // span

        def score(index):
            here = slice(index * span, (index + 1) * span)
            return jnp.dot(
                keys_wide[: count * BLK], query_wide[:, here], preferred_element_type=jnp.float32
            )

        def soft(index, scores):
            here = slice(index * span, (index + 1) * span)
            if bounds is not None:
                scores = jnp.concatenate(
                    [
                        jnp.where(lag <= bounds[block], scores[block * BLK : (block + 1) * BLK], -jnp.inf)
                        for block in range(count)
                    ],
                    axis=0,
                )
            top = jnp.max(scores, axis=0, keepdims=True)
            if first:
                new = jnp.maximum(top, NEGATIVE)
                factor = None
            else:
                old = top_ref[:, here]
                new = jnp.maximum(old, top)
                factor = jnp.exp2((old - new) * scale)
            if not closing:
                top_ref[:, here] = new
            return jnp.exp2((scores - new) * scale).astype(jnp.bfloat16), factor

        def value(index, exponents, factor):
            here = slice(index * span, (index + 1) * span)
            added = jnp.dot(
                values_wide[:, : count * BLK], exponents, preferred_element_type=jnp.float32
            )
            if first:
                out[:, here] = added[:128]
                sum_ref[:, here] = added[128:129]
            elif closing:
                close(
                    index,
                    out[:, here] * factor + added[:128],
                    sum_ref[:, here] * factor + added[128:129],
                )
            else:
                out[:, here] = out[:, here] * factor + added[:128]
                sum_ref[:, here] = sum_ref[:, here] * factor + added[128:129]

        ready = score(0)
        for index in range(total):
            later = score(index + 1) if index + 1 < total else None
            value(index, *soft(index, ready))
            ready = later

    values_wide[128:, :] = jnp.ones_like(values_wide[128:, :])

    def gather(mark, turn):
        place = lax.rem(mark // MARK, n * cap)
        block = early[jnp.minimum(place, ready - 1)]
        for index in range(turn):
            other = late[index]
            start = starts[index]
            block = jnp.where(
                place >= start, other[jnp.clip(place - start, 0, other.shape[0] - 1)], block
            )
        return block

    def attend_picked(turn, start, count, closing=False):
        marks = [order_smem[3, start + index] for index in range(count)]
        values = [fill(index, gather(mark, turn)) for index, mark in enumerate(marks)]
        values_wide[:128, : count * BLK] = jnp.concatenate(values, axis=0).T
        bounds = None
        if start == 0:
            bounds = [first_pos - lax.rem(mark, MARK) * BLK for mark in marks]
        attend(
            count, bounds, 1, picked_top, picked_sum, picked_out, start == 0, closing
        )

    loads[5].wait()
    loads[6].wait()
    gates = jax.nn.sigmoid(
        lax.dot_general(
            gate_ref[...],
            hidden_ref[...],
            (((1,), (1,)), ((), ())),
            preferred_element_type=jnp.float32,
        )
    )

    def passed(step, carry):
        pass_copy(step).wait_recv()
        return carry

    lax.fori_loop(0, n // 2, passed, 0)

    pieces = min(n, 8)

    def coarse_step(index, first):
        values = [fill(piece, coarse[index * pieces + piece]) for piece in range(pieces)]
        values_wide[:128, : pieces * BLK] = jnp.concatenate(values, axis=0).T
        start = first_pos - (CLEN - 1) - index * (pieces * BLK * CSTRIDE)
        bounds = [start - piece * (BLK * CSTRIDE) for piece in range(pieces)]
        attend(pieces, bounds, CSTRIDE, coarse_top, coarse_sum, coarse_out, first)

    coarse_step(0, True)
    if n > pieces:

        def coarse_more(index, carry):
            coarse_step(index, False)
            return carry

        lax.fori_loop(1, n // pieces, coarse_more, 0)

    for index in range(heads * TILE // span):
        here = slice(index * span, (index + 1) * span)
        coarse_out[:, here] = coarse_out[:, here] * (gate_row(index, 0) / coarse_sum[:, here])

    def wait_slots(start, stop, slots, late_one, base=None):
        def wait_one(index, carry):
            step = index if base is None else flip(me, base + index, n)
            for slot in slots:
                slot_copy(step, slot, late_one).wait_recv()
            return carry

        lax.fori_loop(start, stop, wait_one, 0)

    if not staged:
        wait_slots(1, n, range(cap), False)
        for start in range(0, SEL, PART):
            attend_picked(0, start, PART, start + PART == SEL)
    else:
        wait_slots(1, half, range(cap), False)
        wait_slots(0, 2, range(cap), False, (n - 2) * (1 - side))
        for start in range(0, SEL // 2, PART):
            attend_picked(0, start, PART)
        start = SEL // 2
        for turn, slots in enumerate([range(2), range(2, 3), range(3, 4)]):
            wait_slots(0, 2, slots, True, half - 2 * side)
            count = 2 * len(slots)
            attend_picked(turn + 1, start, count, turn == 2)
            start += count

    def part_copy(step):
        return pltpu.make_async_remote_copy(
            src_ref=partial.at[step],
            dst_ref=arrived.at[step],
            send_sem=part_send.at[step],
            recv_sem=part_recv.at[step],
            device_id={"grp": flip(group, step, groups)},
            device_id_type=MESH,
        )

    for step in reversed(range(1, groups)):
        weight_copy(step).wait()
        partial[step] = jnp.dot(
            attended[...], weights[step], preferred_element_type=jnp.float32
        ).astype(jnp.bfloat16)
        part_copy(step).start()
    weight_copy(0).wait()
    own_part[...] = jnp.dot(attended[...], weights[0], preferred_element_type=jnp.float32)

    def sent(step, carry):
        table_copy(step).wait_send()
        return carry

    lax.fori_loop(1, n, sent, 0)

    def sent_slots(step, carry):
        for slot in range(cap):
            slot_copy(step, slot, False).wait_send()
        return carry

    lax.fori_loop(1, n, sent_slots, 0)
    for held in range(chips):
        if held and not staged:
            coarse_copy(0, held).wait_send()
        pass_copy(held).wait_send()
    if staged:
        hop(1).wait_send()

        @pl.when(inner)
        def _():
            for index in (0, 2, 3, 4):
                hop(index).wait_send()

    total = own_part[...]
    for step in range(1, groups):
        part_copy(step).wait_recv()
        total = total + arrived[step].astype(jnp.float32)
    out_ref[...] = total.astype(out_ref.dtype)
    for step in range(1, groups):
        part_copy(step).wait_send()


def shards(
    queries,
    key_cache,
    group_value_cache,
    coarse_keys,
    coarse_values,
    hidden,
    gate_weight,
    out_weight,
    selected,
):
    n = lax.axis_size("seq")
    groups = lax.axis_size("grp")
    ctx_dev = key_cache.shape[1]
    heads = queries.shape[1]
    width = queries.shape[2]
    vwidth = group_value_cache.shape[2]
    rows = TILE * heads
    blocks = ctx_dev // BLK
    cap = max(1, 2 * SEL // n)
    columns = out_weight.shape[1] // groups
    pieces = min(n, 8)
    wide = max(pieces, PART) * BLK
    staged = n == 8 and cap == 4 and n * TILE <= ctx_dev

    vmem = pl.BlockSpec(memory_space=pltpu.VMEM)
    hbm = pl.BlockSpec(memory_space=pl.ANY)
    dma = pltpu.SemaphoreType.DMA
    bf16, f32 = jnp.bfloat16, jnp.float32
    inputs = (
        queries.transpose(1, 2, 0),
        key_cache[0].T,
        group_value_cache.reshape(blocks, BLK, vwidth),
        coarse_keys[0],
        coarse_values[0],
        hidden,
        gate_weight[0].T,
    )
    return pl.pallas_call(
        functools.partial(kernel, n, groups, cap, width**-0.5 * math.log2(math.e)),
        out_shape=pltpu.VMEM((TILE, columns), bf16),
        in_specs=[pl.BlockSpec(memory_space=pltpu.SMEM), vmem] + [hbm] * (len(inputs) + 1),
        out_specs=vmem,
        scratch_shapes=[pltpu.VMEM(one.shape, bf16) for one in inputs]
        + [
            pltpu.VMEM((blocks, UNIT, 128), bf16),
            pltpu.VMEM((256, rows), bf16),
            pltpu.SMEM((n, 1, 1, SEL), jnp.int32),
            pltpu.SMEM((4, max(n, SEL)), jnp.int32),
            pltpu.VMEM((n, cap, UNIT, 128), bf16),
            pltpu.VMEM(((n - 2 * staged) * cap, UNIT, 128), bf16),
            [pltpu.VMEM((size, UNIT, 128), bf16) for size in ([4, 2, 2] if staged else [])],
            pltpu.VMEM((n, UNIT, 128), bf16),
            pltpu.VMEM((wide, 256), bf16),
            pltpu.VMEM((144, wide), bf16),
            pltpu.VMEM((1, rows), f32),
            pltpu.VMEM((1, rows), f32),
            pltpu.VMEM((vwidth, rows), f32),
            pltpu.VMEM((1, rows), f32),
            pltpu.VMEM((1, rows), f32),
            pltpu.VMEM((vwidth, rows), f32),
            pltpu.VMEM((TILE, heads * vwidth), bf16),
            pltpu.VMEM((groups, heads * vwidth, columns), bf16),
            pltpu.VMEM((groups, TILE, columns), bf16),
            pltpu.VMEM((groups, TILE, columns), bf16),
            pltpu.VMEM((TILE, columns), f32),
            dma((len(inputs),)),
            dma((groups,)),
            dma((n,)),
            dma((n,)),
            dma((n, cap)),
            dma((n, cap)),
            dma((n // 2 + 1,)),
            dma((n // 2,)),
            dma((n // 2,)),
            dma((n // 2,)),
            dma((groups,)),
            dma((groups,)),
            pltpu.SemaphoreType.REGULAR((2,)),
        ],
        compiler_params=pltpu.CompilerParams(
            collective_id=0, has_side_effects=True, vmem_limit_bytes=60 * 1024 * 1024
        ),
    )(selected, selected, *inputs, out_weight)


def solution(mesh):
    return jax.shard_map(
        shards,
        mesh=mesh,
        in_specs=(
            P("seq", "grp", None),
            P("grp", "seq", None),
            P("grp", "seq", None),
            P("grp", "seq", None),
            P("grp", "seq", None),
            P("seq", None),
            P("grp", None, None),
            P("grp", None),
            P("grp", "seq", None),
        ),
        out_specs=P("seq", "grp"),
        check_vma=False,
    )
```

```python
import functools
import math

import jax
import jax.numpy as jnp
from jax import lax
from jax.experimental import pallas as pl
from jax.experimental.pallas import tpu as pltpu
from jax.sharding import PartitionSpec as P

BLK = 64
SEL = 16
TILE = 128
CSTRIDE = 16
CLEN = 32

NEGATIVE = -1e30
FAR = 1 << 28
MESH = pl.DeviceIdType.MESH
HALF = BLK // 2
UNIT = BLK + HALF + BLK
MARK = 1 << 16
PART = SEL // 4


def pack(keys, values, width):
    tail = keys[:, 128:width]
    folded = jnp.concatenate([tail[:HALF], tail[HALF:]], axis=1)
    return jnp.concatenate([keys[:, :128], folded, values], axis=0)


def unpack(block):
    folded = block[BLK : BLK + HALF]
    low = lax.broadcasted_iota(jnp.int32, folded.shape, 1) < 64
    zero = jnp.zeros_like(folded)
    tails = jnp.concatenate([jnp.where(low, folded, zero), jnp.where(low, zero, folded)], axis=0)
    return jnp.concatenate([block[:BLK], tails], axis=1), block[BLK + HALF :]


def bit_of(index, bit):
    return index // bit % 2 if isinstance(index, int) else lax.rem(index // bit, 2)


def flip(index, step, size):
    shared = 0
    bit = 1
    while bit < size:
        shared = shared + bit_of(index, bit) * bit_of(step, bit) * bit
        bit *= 2
    return index + step - 2 * shared


def exchanges(count):
    found = []
    p = 1
    while p < count:
        k = p
        while k >= 1:
            for j in range(k % p, count - k, 2 * k):
                for i in range(min(k, count - j - k)):
                    if (i + j) // (2 * p) == (i + j + k) // (2 * p):
                        found.append((i + j, i + j + k))
            k //= 2
        p *= 2
    return found


def picks(read, owner, blocks, cap):
    low = owner * blocks
    found = [jnp.int32(-1)] * cap
    count = jnp.int32(0)
    for entry in range(SEL):
        block = read(entry)
        here = (block >= low) & (block < low + blocks)
        for slot in range(cap):
            found[slot] = jnp.where(here & (count == slot), block, found[slot])
        count = count + here.astype(jnp.int32)
    return found


def kernel(
    n,
    groups,
    cap,
    scale,
    own_smem,
    own_table,
    query_hbm,
    key_hbm,
    value_hbm,
    ckey_hbm,
    cvalue_hbm,
    hidden_hbm,
    gate_hbm,
    weight_hbm,
    out_ref,
    query_ref,
    key_ref,
    value_ref,
    ckey_ref,
    cvalue_ref,
    hidden_ref,
    gate_ref,
    packed,
    query_wide,
    tables_smem,
    order_smem,
    outgoing,
    early,
    late,
    coarse,
    keys_wide,
    values_wide,
    picked_top,
    picked_sum,
    picked_out,
    coarse_top,
    coarse_sum,
    coarse_out,
    attended,
    weights,
    partial,
    arrived,
    own_part,
    input_sem,
    weight_sem,
    table_send,
    table_recv,
    slot_send,
    slot_recv,
    coarse_send,
    coarse_recv,
    pass_send,
    pass_recv,
    part_send,
    part_recv,
    hello,
):
    me = lax.axis_index("seq")
    group = lax.axis_index("grp")
    core = lax.rem(me, 2)
    sibling = me + 1 - 2 * core
    heads, width, _ = query_ref.shape
    blocks = value_ref.shape[0]
    columns = out_ref.shape[1]
    context = blocks * BLK * n
    span = 2 * TILE
    half = n // 2
    chips = n // 2
    staged = len(late) > 0
    ready = early.shape[0]
    starts = [ready, ready + 4, ready + 6]
    side = me // half
    outer = (me < half - 2) | (me >= half + 2)

    barrier = pltpu.get_barrier_semaphore()

    def greet(step, carry):
        pl.semaphore_signal(
            barrier, inc=1, device_id={"seq": flip(me, step, n)}, device_id_type=MESH
        )
        return carry

    inner = jnp.logical_not(outer)
    lax.fori_loop(1, half if staged else n, greet, 0)
    if staged:

        @pl.when(inner)
        def _():
            lax.fori_loop(n - 2, n, greet, 0)

    for step in range(1, groups):
        pl.semaphore_signal(
            barrier, inc=1, device_id={"grp": flip(group, step, groups)}, device_id_type=MESH
        )

    loads = [
        pltpu.make_async_copy(source, target, input_sem.at[index])
        for index, (source, target) in enumerate(
            [
                (ckey_hbm, ckey_ref),
                (cvalue_hbm, cvalue_ref),
                (key_hbm, key_ref),
                (value_hbm, value_ref),
                (query_hbm, query_ref),
                (hidden_hbm, hidden_ref),
                (gate_hbm, gate_ref),
            ]
        )
    ]
    for load in loads:
        load.start()

    def weight_copy(step):
        target = flip(group, step, groups)
        return pltpu.make_async_copy(
            weight_hbm.at[:, pl.ds(pl.multiple_of(target * columns, 128), columns)],
            weights.at[step],
            weight_sem.at[step],
        )

    for step in reversed(range(groups)):
        weight_copy(step).start()

    loads[0].wait()
    loads[1].wait()
    coarse[me] = pack(ckey_ref[...], cvalue_ref[...], width)
    loads[2].wait()
    loads[3].wait()
    for pair in range(blocks // 2):
        both = key_ref[:, pair * 128 : (pair + 1) * 128].T
        packed[2 * pair] = pack(both[:BLK], value_ref[2 * pair], width)
        packed[2 * pair + 1] = pack(both[BLK:], value_ref[2 * pair + 1], width)
    if not staged:
        pl.semaphore_wait(barrier, n - 1 + groups - 1)
    else:

        @pl.when(inner)
        def _():
            pl.semaphore_wait(barrier, half + 1 + groups - 1)

        @pl.when(outer)
        def _():
            pl.semaphore_wait(barrier, half - 1 + groups - 1)

    def say(kind, step):
        pl.semaphore_signal(
            hello.at[kind], inc=1, device_id={"seq": flip(me, step, n)}, device_id_type=MESH
        )


    def table_copy(step):
        return pltpu.make_async_remote_copy(
            src_ref=own_table,
            dst_ref=tables_smem.at[step],
            send_sem=table_send.at[step],
            recv_sem=table_recv.at[step],
            device_id={"seq": flip(me, step, n)},
            device_id_type=MESH,
        )

    def coarse_copy(held, bit, index=None):
        unit = coarse.at[flip(me, 2 * held, n)]
        landing = flip(held, bit, chips)
        return pltpu.make_async_remote_copy(
            src_ref=unit,
            dst_ref=unit,
            send_sem=coarse_send.at[landing if index is None else index],
            recv_sem=coarse_recv.at[landing],
            device_id={"seq": flip(me, 2 * bit, n)},
            device_id_type=MESH,
        )

    hops = [(0, 3), (0, 1), (1, 3), (3, 1), (2, 1)]

    def hop(index):
        return coarse_copy(*hops[index], index)

    def coarse_pass(held):
        coarse_wait(held)
        pass_copy(held).start()

    def coarse_wait(held):
        coarse_copy(0, held).wait_recv()

    def pass_copy(step):
        unit = coarse.at[flip(me, 2 * step, n)]
        return pltpu.make_async_remote_copy(
            src_ref=unit,
            dst_ref=unit,
            send_sem=pass_send.at[step],
            recv_sem=pass_recv.at[step],
            device_id={"seq": sibling},
            device_id_type=MESH,
        )

    def bits_below(bit):
        while bit > 1:
            bit //= 2
            yield bit

    def slot_copy(step, slot, late_one):
        if not staged:
            target = early.at[step * cap + slot]
        elif late_one:
            odd = lax.rem(step, 2)
            target = late[0].at[odd * 2 + slot] if slot < 2 else late[slot - 1].at[odd]
        else:
            place = jnp.where(step < half, step, half + lax.rem(step, 2))
            target = early.at[place * cap + slot]
        return pltpu.make_async_remote_copy(
            src_ref=outgoing.at[step, slot],
            dst_ref=target,
            send_sem=slot_send.at[step, slot],
            recv_sem=slot_recv.at[step, slot],
            device_id={"seq": flip(me, step, n)},
            device_id_type=MESH,
        )

    def send_table(step, carry):
        table_copy(step).start()
        return carry

    lax.fori_loop(1, half if staged else n, send_table, 0)

    if staged:

        @pl.when(inner)
        def _():
            say(0, n - 2)
            say(0, 2)
            lax.fori_loop(n - 2, n, send_table, 0)
            hop(0).start()

        hop(1).start()
    else:
        for bit in bits_below(chips):
            coarse_copy(0, bit).start()
    pass_copy(0).start()

    def fill_slots(step):
        table_copy(step).wait_recv()
        wanted = picks(lambda entry: tables_smem[step, 0, 0, entry], me, blocks, cap)
        for slot in range(cap):
            outgoing[step, slot] = packed[jnp.maximum(wanted[slot] - me * blocks, 0)]

    def send_near(step, carry):
        fill_slots(step)
        for slot in range(cap):
            slot_copy(step, slot, False).start()
        return carry

    def far_step(phase, chip):
        return flip(me, half - side + (1 - 2 * side) * (2 * chip + phase), n)

    def useful(owner, tile, slot):
        return (owner * blocks + slot) * BLK < context - TILE * n + (tile + 1) * TILE

    def send_far(phase, first, last):
        def fill_far(chip, carry):
            fill_slots(far_step(phase, chip))
            return carry

        lax.fori_loop(first, last, fill_far, 0)
        if not staged:

            def send_single(index, carry):
                step = far_step(phase, half // 2 - 1 - index)
                for slot in range(cap):
                    slot_copy(step, slot, False).start()
                return carry

            lax.fori_loop(0, half // 2, send_single, 0)
            return
        def send_order(lag, late_one):
            order = [
                (slot + lag * (half // 2 - 1 - chip), chip, slot)
                for chip in range(first, last)
                for slot in range(cap)
            ]
            for _, chip, slot in sorted(order):
                step = far_step(phase, chip)
                copy = slot_copy(step, slot, late_one)
                if slot < 2 or late_one:
                    copy.start()
                else:
                    pl.when(useful(me, flip(me, step, n), slot))(copy.start)

        @pl.when(outer)
        def _():
            send_order(1.5 if phase else -0.1, False)

        @pl.when(inner & (side == 0))
        def _():
            send_order(0.7 if phase else -0.1, True)

        @pl.when(inner & (side == 1))
        def _():
            send_order(1.5 if phase else -0.1, True)

    def send_chip(start, stop):
        lax.fori_loop(start, stop, send_near, 0)

    if staged:

        @pl.when(inner)
        def _():
            @pl.when(side == 0)
            def _():
                send_chip(2, half)

            send_far(0, 0, 1)
            pl.semaphore_wait(hello.at[0], 1)
            say(1, 2)
            lax.fori_loop(half, n - 2, send_table, 0)

            @pl.when(side == 1)
            def _():
                send_chip(2, half)

            coarse_pass(3)
            hop(3).start()
            coarse_pass(1)
            hop(2).start()
            send_far(0, 1, 2)
            coarse_pass(2)
            hop(4).start()

        @pl.when(outer)
        def _():
            pl.semaphore_wait(hello.at[0], 1)
            lax.fori_loop(half, n - 2, send_table, 0)
            pl.semaphore_wait(hello.at[1], 1)
            lax.fori_loop(n - 2, n, send_table, 0)
            send_chip(2, half)
            send_far(0, 0, 2)

        send_chip(1, 2)
        send_far(1, 0, 2)

        @pl.when(outer)
        def _():
            for held in (1, 2, 3):
                coarse_pass(held)
    else:
        for low in bits_below(chips):
            for held in range(low, chips, 2 * low):
                if low > 1:
                    coarse_pass(held)
                    for bit in bits_below(low):
                        coarse_copy(held, bit).start()
        send_chip(1, half)
        send_far(0, 0, half // 2)
        send_far(1, 0, half // 2)
        for held in range(1, chips, 2):
            coarse_pass(held)

    def rank(step, carry):
        owner = flip(me, step, n)
        if not staged:
            for line, value in enumerate([step * cap, step * cap, 1]):
                order_smem[line, owner] = value
        else:
            central = (owner >= half - 2) & (owner < half + 2)
            last = (step >= half) & central
            odd = lax.rem(step, 2)
            place = jnp.where(step < half, step, half + odd) * cap
            order_smem[0, owner] = jnp.where(last, ready + odd * 2, place)
            order_smem[1, owner] = jnp.where(last, ready + odd, place)
            order_smem[2, owner] = jnp.where(last, 2, 1)
        return carry

    lax.fori_loop(0, n, rank, 0)
    newest = (context - TILE * n + me * TILE) // (blocks * BLK)
    entries = [own_smem[0, 0, entry] for entry in range(SEL)]
    owners = [entry // blocks for entry in entries]
    marks = []
    for entry in range(SEL):
        slot = jnp.int32(0)
        for other in range(entry):
            slot = slot + (owners[other] == owners[entry]).astype(jnp.int32)
        place = jnp.where(
            slot < 2,
            order_smem[0, owners[entry]] + slot,
            order_smem[1, owners[entry]] + slot * order_smem[2, owners[entry]],
        )
        place = jnp.where(owners[entry] == newest, place, place + n * cap)
        marks.append(place * MARK + entries[entry])
    for low, high in exchanges(SEL):
        marks[low], marks[high] = (
            jnp.minimum(marks[low], marks[high]),
            jnp.maximum(marks[low], marks[high]),
        )
    for entry in range(SEL):
        order_smem[3, entry] = marks[entry]
    mine = picks(lambda entry: own_smem[0, 0, entry], me, blocks, cap)
    for slot in range(cap):
        early[slot] = packed[jnp.maximum(mine[slot] - me * blocks, 0)]

    loads[4].wait()
    for head in range(heads):
        one = query_ref[head]
        query_wide[:width, head * 128 : (head + 1) * 128] = one
        query_wide[width:, head * 128 : (head + 1) * 128] = one[128:]

    first_pos = context - TILE * n + me * TILE
    row = lax.broadcasted_iota(jnp.int32, (BLK, span), 0)
    query = lax.rem(lax.broadcasted_iota(jnp.int32, (BLK, span), 1), TILE)

    def fill(place, block):
        keys, values = unpack(block)
        keys_wide[place * BLK : (place + 1) * BLK] = keys
        return values

    def gate_row(index, kind):
        first_head = kind * heads + index * (span // TILE)
        return jnp.concatenate(
            [gates[first_head + other : first_head + other + 1] for other in range(span // TILE)],
            axis=1,
        )

    def close(index, picked, total):
        here = slice(index * span, (index + 1) * span)
        mixed = coarse_out[:, here] + picked * (gate_row(index, 1) / total)
        mixed = mixed.astype(jnp.bfloat16)
        for other in range(span // TILE):
            start = index * span + other * TILE
            attended[:, start : start + TILE] = mixed[:, other * TILE : (other + 1) * TILE].T

    def attend(count, bounds, stride, top_ref, sum_ref, out, first, closing=False):
        lag = row * stride - query
        total = heads * TILE // span

        def score(index):
            here = slice(index * span, (index + 1) * span)
            return jnp.dot(
                keys_wide[: count * BLK], query_wide[:, here], preferred_element_type=jnp.float32
            )

        def soft(index, scores):
            here = slice(index * span, (index + 1) * span)
            if bounds is not None:
                scores = jnp.concatenate(
                    [
                        jnp.where(lag <= bounds[block], scores[block * BLK : (block + 1) * BLK], -jnp.inf)
                        for block in range(count)
                    ],
                    axis=0,
                )
            top = jnp.max(scores, axis=0, keepdims=True)
            if first:
                new = jnp.maximum(top, NEGATIVE)
                factor = None
            else:
                old = top_ref[:, here]
                new = jnp.maximum(old, top)
                factor = jnp.exp2((old - new) * scale)
            if not closing:
                top_ref[:, here] = new
            return jnp.exp2((scores - new) * scale).astype(jnp.bfloat16), factor

        def value(index, exponents, factor):
            here = slice(index * span, (index + 1) * span)
            added = jnp.dot(
                values_wide[:, : count * BLK], exponents, preferred_element_type=jnp.float32
            )
            if first:
                out[:, here] = added[:128]
                sum_ref[:, here] = added[128:129]
            elif closing:
                close(
                    index,
                    out[:, here] * factor + added[:128],
                    sum_ref[:, here] * factor + added[128:129],
                )
            else:
                out[:, here] = out[:, here] * factor + added[:128]
                sum_ref[:, here] = sum_ref[:, here] * factor + added[128:129]

        ready = score(0)
        for index in range(total):
            later = score(index + 1) if index + 1 < total else None
            value(index, *soft(index, ready))
            ready = later

    values_wide[128:, :] = jnp.ones_like(values_wide[128:, :])

    def gather(mark, turn):
        place = lax.rem(mark // MARK, n * cap)
        block = early[jnp.where(place < ready, place, 0)]
        for index in range(turn):
            other = late[index]
            start = starts[index]
            block = jnp.where(
                place >= start, other[jnp.clip(place - start, 0, other.shape[0] - 1)], block
            )
        return block

    def attend_picked(turn, start, count, closing=False):
        marks = [order_smem[3, start + index] for index in range(count)]
        values = [fill(index, gather(mark, turn)) for index, mark in enumerate(marks)]
        values_wide[:128, : count * BLK] = jnp.concatenate(values, axis=0).T
        bounds = None
        if start == 0:
            bounds = [first_pos - lax.rem(mark, MARK) * BLK for mark in marks]
        attend(
            count, bounds, 1, picked_top, picked_sum, picked_out, start == 0, closing
        )

    loads[5].wait()
    loads[6].wait()
    gates = jax.nn.sigmoid(
        lax.dot_general(
            gate_ref[...],
            hidden_ref[...],
            (((1,), (1,)), ((), ())),
            preferred_element_type=jnp.float32,
        )
    )

    def passed(step, carry):
        pass_copy(step).wait_recv()
        return carry

    lax.fori_loop(0, n // 2, passed, 0)

    pieces = min(n, 8)

    def coarse_step(index, first):
        values = [fill(piece, coarse[index * pieces + piece]) for piece in range(pieces)]
        values_wide[:128, : pieces * BLK] = jnp.concatenate(values, axis=0).T
        start = first_pos - (CLEN - 1) - index * (pieces * BLK * CSTRIDE)
        bounds = [start - piece * (BLK * CSTRIDE) for piece in range(pieces)]
        attend(pieces, bounds, CSTRIDE, coarse_top, coarse_sum, coarse_out, first)

    coarse_step(0, True)
    if n > pieces:

        def coarse_more(index, carry):
            coarse_step(index, False)
            return carry

        lax.fori_loop(1, n // pieces, coarse_more, 0)

    for index in range(heads * TILE // span):
        here = slice(index * span, (index + 1) * span)
        coarse_out[:, here] = coarse_out[:, here] * (gate_row(index, 0) / coarse_sum[:, here])

    def wait_slots(start, stop, slots, late_one, base=None):
        def wait_one(index, carry):
            step = index if base is None else flip(me, base + index, n)
            for slot in slots:
                copy = slot_copy(step, slot, late_one)
                if base is None or slot < 2 or late_one:
                    copy.wait_recv()
                else:
                    pl.when(useful(flip(me, step, n), me, slot))(copy.wait_recv)
            return carry

        lax.fori_loop(start, stop, wait_one, 0)

    if not staged:
        wait_slots(1, n, range(cap), False)
        for start in range(0, SEL, PART):
            attend_picked(0, start, PART, start + PART == SEL)
    else:
        wait_slots(1, half, range(cap), False)
        wait_slots(0, 2, range(cap), False, (n - 2) * (1 - side))
        for start in range(0, SEL // 2, PART):
            attend_picked(0, start, PART)
        start = SEL // 2
        for turn, slots in enumerate([range(2), range(2, 3), range(3, 4)]):
            wait_slots(0, 2, slots, True, half - 2 * side)
            count = 2 * len(slots)
            attend_picked(turn + 1, start, count, turn == 2)
            start += count

    halves = [(0, columns // 256 * 128), (columns // 256 * 128, columns)]

    def part_copy(step, half_of):
        here = slice(*halves[half_of])
        return pltpu.make_async_remote_copy(
            src_ref=partial.at[step, :, here],
            dst_ref=arrived.at[step, :, here],
            send_sem=part_send.at[step, half_of],
            recv_sem=part_recv.at[step, half_of],
            device_id={"grp": flip(group, step, groups)},
            device_id_type=MESH,
        )

    for step in reversed(range(1, groups)):
        weight_copy(step).wait()
        for half_of in range(2):
            here = slice(*halves[half_of])
            partial[step, :, here] = jnp.dot(
                attended[...], weights[step, :, here], preferred_element_type=jnp.float32
            ).astype(jnp.bfloat16)
            part_copy(step, half_of).start()
    weight_copy(0).wait()
    own_part[...] = jnp.dot(attended[...], weights[0], preferred_element_type=jnp.float32)

    def sent(step, carry):
        table_copy(step).wait_send()
        return carry

    lax.fori_loop(1, n, sent, 0)

    def sent_slots(step, carry):
        for slot in range(cap):
            copy = slot_copy(step, slot, False)
            if slot < 2 or not staged:
                copy.wait_send()
            else:
                pl.when(useful(me, flip(me, step, n), slot))(copy.wait_send)
        return carry

    lax.fori_loop(1, n, sent_slots, 0)
    for held in range(chips):
        if held and not staged:
            coarse_copy(0, held).wait_send()
        pass_copy(held).wait_send()
    if staged:
        hop(1).wait_send()

        @pl.when(inner)
        def _():
            for index in (0, 2, 3, 4):
                hop(index).wait_send()

    total = own_part[...]
    for step in range(1, groups):
        for half_of in range(2):
            part_copy(step, half_of).wait_recv()
        total = total + arrived[step].astype(jnp.float32)
    out_ref[...] = total.astype(out_ref.dtype)
    for step in range(1, groups):
        for half_of in range(2):
            part_copy(step, half_of).wait_send()


def shards(
    queries,
    key_cache,
    group_value_cache,
    coarse_keys,
    coarse_values,
    hidden,
    gate_weight,
    out_weight,
    selected,
):
    n = lax.axis_size("seq")
    groups = lax.axis_size("grp")
    ctx_dev = key_cache.shape[1]
    heads = queries.shape[1]
    width = queries.shape[2]
    vwidth = group_value_cache.shape[2]
    rows = TILE * heads
    blocks = ctx_dev // BLK
    cap = max(1, 2 * SEL // n)
    columns = out_weight.shape[1] // groups
    pieces = min(n, 8)
    wide = max(pieces, PART) * BLK
    staged = n == 8 and cap == 4 and n * TILE <= ctx_dev

    vmem = pl.BlockSpec(memory_space=pltpu.VMEM)
    hbm = pl.BlockSpec(memory_space=pl.ANY)
    dma = pltpu.SemaphoreType.DMA
    bf16, f32 = jnp.bfloat16, jnp.float32
    inputs = (
        queries.transpose(1, 2, 0),
        key_cache[0].T,
        group_value_cache.reshape(blocks, BLK, vwidth),
        coarse_keys[0],
        coarse_values[0],
        hidden,
        gate_weight[0].T,
    )
    return pl.pallas_call(
        functools.partial(kernel, n, groups, cap, width**-0.5 * math.log2(math.e)),
        out_shape=pltpu.VMEM((TILE, columns), bf16),
        in_specs=[pl.BlockSpec(memory_space=pltpu.SMEM), vmem] + [hbm] * (len(inputs) + 1),
        out_specs=vmem,
        scratch_shapes=[pltpu.VMEM(one.shape, bf16) for one in inputs]
        + [
            pltpu.VMEM((blocks, UNIT, 128), bf16),
            pltpu.VMEM((256, rows), bf16),
            pltpu.SMEM((n, 1, 1, SEL), jnp.int32),
            pltpu.SMEM((4, max(n, SEL)), jnp.int32),
            pltpu.VMEM((n, cap, UNIT, 128), bf16),
            pltpu.VMEM(((n - 2 * staged) * cap, UNIT, 128), bf16),
            [pltpu.VMEM((size, UNIT, 128), bf16) for size in ([4, 2, 2] if staged else [])],
            pltpu.VMEM((n, UNIT, 128), bf16),
            pltpu.VMEM((wide, 256), bf16),
            pltpu.VMEM((144, wide), bf16),
            pltpu.VMEM((1, rows), f32),
            pltpu.VMEM((1, rows), f32),
            pltpu.VMEM((vwidth, rows), f32),
            pltpu.VMEM((1, rows), f32),
            pltpu.VMEM((1, rows), f32),
            pltpu.VMEM((vwidth, rows), f32),
            pltpu.VMEM((TILE, heads * vwidth), bf16),
            pltpu.VMEM((groups, heads * vwidth, columns), bf16),
            pltpu.VMEM((groups, TILE, columns), bf16),
            pltpu.VMEM((groups, TILE, columns), bf16),
            pltpu.VMEM((TILE, columns), f32),
            dma((len(inputs),)),
            dma((groups,)),
            dma((n,)),
            dma((n,)),
            dma((n, cap)),
            dma((n, cap)),
            dma((n // 2 + 1,)),
            dma((n // 2,)),
            dma((n // 2,)),
            dma((n // 2,)),
            dma((groups, 2)),
            dma((groups, 2)),
            pltpu.SemaphoreType.REGULAR((2,)),
        ],
        compiler_params=pltpu.CompilerParams(
            collective_id=0, has_side_effects=True, vmem_limit_bytes=60 * 1024 * 1024
        ),
    )(selected, selected, *inputs, out_weight)


def solution(mesh):
    return jax.shard_map(
        shards,
        mesh=mesh,
        in_specs=(
            P("seq", "grp", None),
            P("grp", "seq", None),
            P("grp", "seq", None),
            P("grp", "seq", None),
            P("grp", "seq", None),
            P("seq", None),
            P("grp", None, None),
            P("grp", None),
            P("grp", "seq", None),
        ),
        out_specs=P("seq", "grp"),
        check_vma=False,
    )
```

```python
import functools
import math

import jax
import jax.numpy as jnp
from jax import lax
from jax.experimental import pallas as pl
from jax.experimental.pallas import tpu as pltpu
from jax.sharding import PartitionSpec as P

BLK = 64
SEL = 16
TILE = 128
CSTRIDE = 16
CLEN = 32

NEGATIVE = -1e30
FAR = 1 << 28
MESH = pl.DeviceIdType.MESH
HALF = BLK // 2
UNIT = BLK + HALF + BLK
MARK = 1 << 16
PART = SEL // 4


def pack(keys, values, width):
    tail = keys[:, 128:width]
    folded = jnp.concatenate([tail[:HALF], tail[HALF:]], axis=1)
    return jnp.concatenate([keys[:, :128], folded, values], axis=0)


def unpack(block):
    folded = block[BLK : BLK + HALF]
    low = lax.broadcasted_iota(jnp.int32, folded.shape, 1) < 64
    zero = jnp.zeros_like(folded)
    tails = jnp.concatenate([jnp.where(low, folded, zero), jnp.where(low, zero, folded)], axis=0)
    return jnp.concatenate([block[:BLK], tails], axis=1), block[BLK + HALF :]


def bit_of(index, bit):
    return index // bit % 2 if isinstance(index, int) else lax.rem(index // bit, 2)


def flip(index, step, size):
    shared = 0
    bit = 1
    while bit < size:
        shared = shared + bit_of(index, bit) * bit_of(step, bit) * bit
        bit *= 2
    return index + step - 2 * shared


def exchanges(count):
    found = []
    p = 1
    while p < count:
        k = p
        while k >= 1:
            for j in range(k % p, count - k, 2 * k):
                for i in range(min(k, count - j - k)):
                    if (i + j) // (2 * p) == (i + j + k) // (2 * p):
                        found.append((i + j, i + j + k))
            k //= 2
        p *= 2
    return found


def picks(read, owner, blocks, cap):
    low = owner * blocks
    found = [jnp.int32(-1)] * cap
    count = jnp.int32(0)
    for entry in range(SEL):
        block = read(entry)
        here = (block >= low) & (block < low + blocks)
        for slot in range(cap):
            found[slot] = jnp.where(here & (count == slot), block, found[slot])
        count = count + here.astype(jnp.int32)
    return found


def kernel(
    n,
    groups,
    cap,
    scale,
    own_smem,
    own_table,
    query_hbm,
    key_hbm,
    value_hbm,
    ckey_hbm,
    cvalue_hbm,
    hidden_hbm,
    gate_hbm,
    weight_hbm,
    out_ref,
    query_ref,
    key_ref,
    value_ref,
    ckey_ref,
    cvalue_ref,
    hidden_ref,
    gate_ref,
    packed,
    query_wide,
    tables_smem,
    order_smem,
    outgoing,
    early,
    late,
    coarse,
    keys_wide,
    values_wide,
    picked_top,
    picked_sum,
    picked_out,
    coarse_top,
    coarse_sum,
    coarse_out,
    attended,
    weights,
    partial,
    arrived,
    own_part,
    input_sem,
    weight_sem,
    table_send,
    table_recv,
    slot_send,
    slot_recv,
    coarse_send,
    coarse_recv,
    pass_send,
    pass_recv,
    part_send,
    part_recv,
    hello,
):
    me = lax.axis_index("seq")
    group = lax.axis_index("grp")
    core = lax.rem(me, 2)
    sibling = me + 1 - 2 * core
    heads, width, _ = query_ref.shape
    blocks = value_ref.shape[0]
    columns = out_ref.shape[1]
    context = blocks * BLK * n
    span = 2 * TILE
    half = n // 2
    chips = n // 2
    staged = len(late) > 0
    ready = early.shape[0]
    starts = [ready, ready + 4, ready + 6]
    side = me // half
    outer = (me < half - 2) | (me >= half + 2)

    barrier = pltpu.get_barrier_semaphore()

    def greet(step, carry):
        pl.semaphore_signal(
            barrier, inc=1, device_id={"seq": flip(me, step, n)}, device_id_type=MESH
        )
        return carry

    inner = jnp.logical_not(outer)
    lax.fori_loop(1, half if staged else n, greet, 0)
    if staged:

        @pl.when(inner)
        def _():
            lax.fori_loop(n - 2, n, greet, 0)

    for step in range(1, groups):
        pl.semaphore_signal(
            barrier, inc=1, device_id={"grp": flip(group, step, groups)}, device_id_type=MESH
        )

    loads = [
        pltpu.make_async_copy(source, target, input_sem.at[index])
        for index, (source, target) in enumerate(
            [
                (ckey_hbm, ckey_ref),
                (cvalue_hbm, cvalue_ref),
                (key_hbm, key_ref),
                (value_hbm, value_ref),
                (query_hbm, query_ref),
                (hidden_hbm, hidden_ref),
                (gate_hbm, gate_ref),
            ]
        )
    ]
    for load in loads:
        load.start()

    def weight_copy(step):
        target = flip(group, step, groups)
        return pltpu.make_async_copy(
            weight_hbm.at[:, pl.ds(pl.multiple_of(target * columns, 128), columns)],
            weights.at[step],
            weight_sem.at[step],
        )

    for step in reversed(range(groups)):
        weight_copy(step).start()

    loads[0].wait()
    loads[1].wait()
    coarse[me] = pack(ckey_ref[...], cvalue_ref[...], width)
    loads[2].wait()
    loads[3].wait()
    for pair in range(blocks // 2):
        both = key_ref[:, pair * 128 : (pair + 1) * 128].T
        packed[2 * pair] = pack(both[:BLK], value_ref[2 * pair], width)
        packed[2 * pair + 1] = pack(both[BLK:], value_ref[2 * pair + 1], width)
    if not staged:
        pl.semaphore_wait(barrier, n - 1 + groups - 1)
    else:

        @pl.when(inner)
        def _():
            pl.semaphore_wait(barrier, half + 1 + groups - 1)

        @pl.when(outer)
        def _():
            pl.semaphore_wait(barrier, half - 1 + groups - 1)

    def say(kind, step):
        pl.semaphore_signal(
            hello.at[kind], inc=1, device_id={"seq": flip(me, step, n)}, device_id_type=MESH
        )


    def table_copy(step):
        return pltpu.make_async_remote_copy(
            src_ref=own_table,
            dst_ref=tables_smem.at[step],
            send_sem=table_send.at[step],
            recv_sem=table_recv.at[step],
            device_id={"seq": flip(me, step, n)},
            device_id_type=MESH,
        )

    def coarse_copy(held, bit, index=None):
        unit = coarse.at[flip(me, 2 * held, n)]
        landing = flip(held, bit, chips)
        return pltpu.make_async_remote_copy(
            src_ref=unit,
            dst_ref=unit,
            send_sem=coarse_send.at[landing if index is None else index],
            recv_sem=coarse_recv.at[landing],
            device_id={"seq": flip(me, 2 * bit, n)},
            device_id_type=MESH,
        )

    hops = [(0, 3), (0, 1), (1, 3), (3, 1), (2, 1)]

    def hop(index):
        return coarse_copy(*hops[index], index)

    def coarse_pass(held):
        coarse_wait(held)
        pass_copy(held).start()

    def coarse_wait(held):
        coarse_copy(0, held).wait_recv()

    def pass_copy(step):
        unit = coarse.at[flip(me, 2 * step, n)]
        return pltpu.make_async_remote_copy(
            src_ref=unit,
            dst_ref=unit,
            send_sem=pass_send.at[step],
            recv_sem=pass_recv.at[step],
            device_id={"seq": sibling},
            device_id_type=MESH,
        )

    def bits_below(bit):
        while bit > 1:
            bit //= 2
            yield bit

    def slot_copy(step, slot, late_one):
        if not staged:
            target = early.at[step * cap + slot]
        elif late_one:
            odd = lax.rem(step, 2)
            target = late[0].at[odd * 2 + slot] if slot < 2 else late[slot - 1].at[odd]
        else:
            place = jnp.where(step < half, step, half + lax.rem(step, 2))
            target = early.at[place * cap + slot]
        return pltpu.make_async_remote_copy(
            src_ref=outgoing.at[step, slot],
            dst_ref=target,
            send_sem=slot_send.at[step, slot],
            recv_sem=slot_recv.at[step, slot],
            device_id={"seq": flip(me, step, n)},
            device_id_type=MESH,
        )

    def send_table(step, carry):
        table_copy(step).start()
        return carry

    lax.fori_loop(1, half if staged else n, send_table, 0)

    if staged:

        @pl.when(inner)
        def _():
            say(0, n - 2)
            say(0, 2)
            lax.fori_loop(n - 2, n, send_table, 0)
            hop(0).start()

        hop(1).start()
    else:
        for bit in bits_below(chips):
            coarse_copy(0, bit).start()
    pass_copy(0).start()

    def fill_slots(step):
        table_copy(step).wait_recv()
        wanted = picks(lambda entry: tables_smem[step, 0, 0, entry], me, blocks, cap)
        for slot in range(cap):
            outgoing[step, slot] = packed[jnp.maximum(wanted[slot] - me * blocks, 0)]

    def send_near(step, carry):
        fill_slots(step)
        for slot in range(cap):
            slot_copy(step, slot, False).start()
        return carry

    def far_step(phase, chip):
        return flip(me, half - side + (1 - 2 * side) * (2 * chip + phase), n)

    def useful(owner, tile, slot):
        return (owner * blocks + slot) * BLK < context - TILE * n + (tile + 1) * TILE

    def send_far(phase, first, last):
        def fill_far(chip, carry):
            fill_slots(far_step(phase, chip))
            return carry

        lax.fori_loop(first, last, fill_far, 0)
        if not staged:

            def send_single(index, carry):
                step = far_step(phase, half // 2 - 1 - index)
                for slot in range(cap):
                    slot_copy(step, slot, False).start()
                return carry

            lax.fori_loop(0, half // 2, send_single, 0)
            return
        def send_order(lag, late_one):
            order = [
                (slot + lag * (half // 2 - 1 - chip), chip, slot)
                for chip in range(first, last)
                for slot in range(cap)
            ]
            for _, chip, slot in sorted(order):
                step = far_step(phase, chip)
                copy = slot_copy(step, slot, late_one)
                if slot < 2 or late_one:
                    copy.start()
                else:
                    pl.when(useful(me, flip(me, step, n), slot))(copy.start)

        @pl.when(outer)
        def _():
            send_order(1.5 if phase else -0.1, False)

        @pl.when(inner & (side == 0))
        def _():
            send_order(0.7 if phase else -0.1, True)

        @pl.when(inner & (side == 1))
        def _():
            send_order(2.5 if phase else -0.1, True)

    def send_chip(start, stop):
        lax.fori_loop(start, stop, send_near, 0)

    if staged:

        @pl.when(inner)
        def _():
            @pl.when(side == 0)
            def _():
                send_chip(2, half)

            send_far(0, 0, 1)
            pl.semaphore_wait(hello.at[0], 1)
            say(1, 2)
            lax.fori_loop(half, n - 2, send_table, 0)

            @pl.when(side == 1)
            def _():
                send_chip(2, half)

            coarse_pass(3)
            hop(3).start()
            coarse_pass(1)
            hop(2).start()
            send_far(0, 1, 2)
            coarse_pass(2)
            hop(4).start()

        @pl.when(outer)
        def _():
            pl.semaphore_wait(hello.at[0], 1)
            lax.fori_loop(half, n - 2, send_table, 0)
            pl.semaphore_wait(hello.at[1], 1)
            lax.fori_loop(n - 2, n, send_table, 0)
            send_chip(2, half)
            send_far(0, 0, 2)

        send_chip(1, 2)
        send_far(1, 0, 2)

        @pl.when(outer)
        def _():
            for held in (1, 2, 3):
                coarse_pass(held)
    else:
        for low in bits_below(chips):
            for held in range(low, chips, 2 * low):
                if low > 1:
                    coarse_pass(held)
                    for bit in bits_below(low):
                        coarse_copy(held, bit).start()
        send_chip(1, half)
        send_far(0, 0, half // 2)
        send_far(1, 0, half // 2)
        for held in range(1, chips, 2):
            coarse_pass(held)

    def rank(step, carry):
        owner = flip(me, step, n)
        if not staged:
            for line, value in enumerate([step * cap, step * cap, 1]):
                order_smem[line, owner] = value
        else:
            central = (owner >= half - 2) & (owner < half + 2)
            last = (step >= half) & central
            odd = lax.rem(step, 2)
            place = jnp.where(step < half, step, half + odd) * cap
            order_smem[0, owner] = jnp.where(last, ready + odd * 2, place)
            order_smem[1, owner] = jnp.where(last, ready + odd, place)
            order_smem[2, owner] = jnp.where(last, 2, 1)
        return carry

    lax.fori_loop(0, n, rank, 0)
    newest = (context - TILE * n + me * TILE) // (blocks * BLK)
    entries = [own_smem[0, 0, entry] for entry in range(SEL)]
    owners = [entry // blocks for entry in entries]
    marks = []
    for entry in range(SEL):
        slot = jnp.int32(0)
        for other in range(entry):
            slot = slot + (owners[other] == owners[entry]).astype(jnp.int32)
        place = jnp.where(
            slot < 2,
            order_smem[0, owners[entry]] + slot,
            order_smem[1, owners[entry]] + slot * order_smem[2, owners[entry]],
        )
        place = jnp.where(owners[entry] == newest, place, place + n * cap)
        marks.append(place * MARK + entries[entry])
    for low, high in exchanges(SEL):
        marks[low], marks[high] = (
            jnp.minimum(marks[low], marks[high]),
            jnp.maximum(marks[low], marks[high]),
        )
    for entry in range(SEL):
        order_smem[3, entry] = marks[entry]
    mine = picks(lambda entry: own_smem[0, 0, entry], me, blocks, cap)
    for slot in range(cap):
        early[slot] = packed[jnp.maximum(mine[slot] - me * blocks, 0)]

    loads[4].wait()
    for head in range(heads):
        one = query_ref[head]
        query_wide[:width, head * 128 : (head + 1) * 128] = one
        query_wide[width:, head * 128 : (head + 1) * 128] = one[128:]

    first_pos = context - TILE * n + me * TILE
    row = lax.broadcasted_iota(jnp.int32, (BLK, span), 0)
    query = lax.rem(lax.broadcasted_iota(jnp.int32, (BLK, span), 1), TILE)

    def fill(place, block):
        keys, values = unpack(block)
        keys_wide[place * BLK : (place + 1) * BLK] = keys
        return values

    def gate_row(index, kind):
        first_head = kind * heads + index * (span // TILE)
        return jnp.concatenate(
            [gates[first_head + other : first_head + other + 1] for other in range(span // TILE)],
            axis=1,
        )

    def close(index, picked, total):
        here = slice(index * span, (index + 1) * span)
        mixed = coarse_out[:, here] + picked * (gate_row(index, 1) / total)
        mixed = mixed.astype(jnp.bfloat16)
        for other in range(span // TILE):
            start = index * span + other * TILE
            attended[:, start : start + TILE] = mixed[:, other * TILE : (other + 1) * TILE].T

    def attend(count, bounds, stride, top_ref, sum_ref, out, first, closing=False):
        lag = row * stride - query
        total = heads * TILE // span

        def score(index):
            here = slice(index * span, (index + 1) * span)
            return jnp.dot(
                keys_wide[: count * BLK], query_wide[:, here], preferred_element_type=jnp.float32
            )

        def soft(index, scores):
            here = slice(index * span, (index + 1) * span)
            if bounds is not None:
                scores = jnp.concatenate(
                    [
                        jnp.where(lag <= bounds[block], scores[block * BLK : (block + 1) * BLK], -jnp.inf)
                        for block in range(count)
                    ],
                    axis=0,
                )
            top = jnp.max(scores, axis=0, keepdims=True)
            if first:
                new = jnp.maximum(top, NEGATIVE)
                factor = None
            else:
                old = top_ref[:, here]
                new = jnp.maximum(old, top)
                factor = jnp.exp2((old - new) * scale)
            if not closing:
                top_ref[:, here] = new
            return jnp.exp2((scores - new) * scale).astype(jnp.bfloat16), factor

        def value(index, exponents, factor):
            here = slice(index * span, (index + 1) * span)
            added = jnp.dot(
                values_wide[:, : count * BLK], exponents, preferred_element_type=jnp.float32
            )
            if first:
                out[:, here] = added[:128]
                sum_ref[:, here] = added[128:129]
            elif closing:
                close(
                    index,
                    out[:, here] * factor + added[:128],
                    sum_ref[:, here] * factor + added[128:129],
                )
            else:
                out[:, here] = out[:, here] * factor + added[:128]
                sum_ref[:, here] = sum_ref[:, here] * factor + added[128:129]

        ready = score(0)
        for index in range(total):
            later = score(index + 1) if index + 1 < total else None
            value(index, *soft(index, ready))
            ready = later

    values_wide[128:, :] = jnp.ones_like(values_wide[128:, :])

    def gather(mark, turn):
        place = lax.rem(mark // MARK, n * cap)
        block = early[jnp.where(place < ready, place, 0)]
        for index in range(turn):
            other = late[index]
            start = starts[index]
            block = jnp.where(
                place >= start, other[jnp.clip(place - start, 0, other.shape[0] - 1)], block
            )
        return block

    def attend_picked(turn, start, count, closing=False):
        marks = [order_smem[3, start + index] for index in range(count)]
        values = [fill(index, gather(mark, turn)) for index, mark in enumerate(marks)]
        values_wide[:128, : count * BLK] = jnp.concatenate(values, axis=0).T
        bounds = None
        if start == 0:
            bounds = [first_pos - lax.rem(mark, MARK) * BLK for mark in marks]
        attend(
            count, bounds, 1, picked_top, picked_sum, picked_out, start == 0, closing
        )

    loads[5].wait()
    loads[6].wait()
    gates = jax.nn.sigmoid(
        lax.dot_general(
            gate_ref[...],
            hidden_ref[...],
            (((1,), (1,)), ((), ())),
            preferred_element_type=jnp.float32,
        )
    )

    def passed(step, carry):
        pass_copy(step).wait_recv()
        return carry

    lax.fori_loop(0, n // 2, passed, 0)

    pieces = min(n, 8)

    def coarse_step(index, first):
        values = [fill(piece, coarse[index * pieces + piece]) for piece in range(pieces)]
        values_wide[:128, : pieces * BLK] = jnp.concatenate(values, axis=0).T
        start = first_pos - (CLEN - 1) - index * (pieces * BLK * CSTRIDE)
        bounds = [start - piece * (BLK * CSTRIDE) for piece in range(pieces)]
        attend(pieces, bounds, CSTRIDE, coarse_top, coarse_sum, coarse_out, first)

    coarse_step(0, True)
    if n > pieces:

        def coarse_more(index, carry):
            coarse_step(index, False)
            return carry

        lax.fori_loop(1, n // pieces, coarse_more, 0)

    for index in range(heads * TILE // span):
        here = slice(index * span, (index + 1) * span)
        coarse_out[:, here] = coarse_out[:, here] * (gate_row(index, 0) / coarse_sum[:, here])

    def wait_slots(start, stop, slots, late_one, base=None):
        def wait_one(index, carry):
            step = index if base is None else flip(me, base + index, n)
            for slot in slots:
                copy = slot_copy(step, slot, late_one)
                if base is None or slot < 2 or late_one:
                    copy.wait_recv()
                else:
                    pl.when(useful(flip(me, step, n), me, slot))(copy.wait_recv)
            return carry

        lax.fori_loop(start, stop, wait_one, 0)

    if not staged:
        wait_slots(1, n, range(cap), False)
        for start in range(0, SEL, PART):
            attend_picked(0, start, PART, start + PART == SEL)
    else:
        wait_slots(1, half, range(cap), False)
        wait_slots(0, 2, range(cap), False, (n - 2) * (1 - side))
        for start in range(0, SEL // 2, PART):
            attend_picked(0, start, PART)
        start = SEL // 2
        for turn, slots in enumerate([range(2), range(2, 3), range(3, 4)]):
            wait_slots(0, 2, slots, True, half - 2 * side)
            count = 2 * len(slots)
            attend_picked(turn + 1, start, count, turn == 2)
            start += count

    halves = [(0, columns // 256 * 128), (columns // 256 * 128, columns)]

    def part_copy(step, half_of):
        here = slice(*halves[half_of])
        return pltpu.make_async_remote_copy(
            src_ref=partial.at[step, :, here],
            dst_ref=arrived.at[step, :, here],
            send_sem=part_send.at[step, half_of],
            recv_sem=part_recv.at[step, half_of],
            device_id={"grp": flip(group, step, groups)},
            device_id_type=MESH,
        )

    for step in range(1, groups):
        weight_copy(step).wait()
    last = groups - 1
    turns = [(last, 0), (last - 1, 0), (last, 1)]
    turns += [(step, half_of) for step in range(1, last - 1) for half_of in range(2)]
    turns += [(last - 1, 1)]
    for step, half_of in turns:
        here = slice(*halves[half_of])
        partial[step, :, here] = jnp.dot(
            attended[...], weights[step, :, here], preferred_element_type=jnp.float32
        ).astype(jnp.bfloat16)
        part_copy(step, half_of).start()
    weight_copy(0).wait()
    own_part[...] = jnp.dot(attended[...], weights[0], preferred_element_type=jnp.float32)

    def sent(step, carry):
        table_copy(step).wait_send()
        return carry

    lax.fori_loop(1, n, sent, 0)

    def sent_slots(step, carry):
        for slot in range(cap):
            copy = slot_copy(step, slot, False)
            if slot < 2 or not staged:
                copy.wait_send()
            else:
                pl.when(useful(me, flip(me, step, n), slot))(copy.wait_send)
        return carry

    lax.fori_loop(1, n, sent_slots, 0)
    for held in range(chips):
        if held and not staged:
            coarse_copy(0, held).wait_send()
        pass_copy(held).wait_send()
    if staged:
        hop(1).wait_send()

        @pl.when(inner)
        def _():
            for index in (0, 2, 3, 4):
                hop(index).wait_send()

    total = own_part[...]
    for step in range(1, groups):
        for half_of in range(2):
            part_copy(step, half_of).wait_recv()
        total = total + arrived[step].astype(jnp.float32)
    out_ref[...] = total.astype(out_ref.dtype)
    for step in range(1, groups):
        for half_of in range(2):
            part_copy(step, half_of).wait_send()


def shards(
    queries,
    key_cache,
    group_value_cache,
    coarse_keys,
    coarse_values,
    hidden,
    gate_weight,
    out_weight,
    selected,
):
    n = lax.axis_size("seq")
    groups = lax.axis_size("grp")
    ctx_dev = key_cache.shape[1]
    heads = queries.shape[1]
    width = queries.shape[2]
    vwidth = group_value_cache.shape[2]
    rows = TILE * heads
    blocks = ctx_dev // BLK
    cap = max(1, 2 * SEL // n)
    columns = out_weight.shape[1] // groups
    pieces = min(n, 8)
    wide = max(pieces, PART) * BLK
    staged = n == 8 and cap == 4 and n * TILE <= ctx_dev

    vmem = pl.BlockSpec(memory_space=pltpu.VMEM)
    hbm = pl.BlockSpec(memory_space=pl.ANY)
    dma = pltpu.SemaphoreType.DMA
    bf16, f32 = jnp.bfloat16, jnp.float32
    inputs = (
        queries.transpose(1, 2, 0),
        key_cache[0].T,
        group_value_cache.reshape(blocks, BLK, vwidth),
        coarse_keys[0],
        coarse_values[0],
        hidden,
        gate_weight[0].T,
    )
    return pl.pallas_call(
        functools.partial(kernel, n, groups, cap, width**-0.5 * math.log2(math.e)),
        out_shape=pltpu.VMEM((TILE, columns), bf16),
        in_specs=[pl.BlockSpec(memory_space=pltpu.SMEM), vmem] + [hbm] * (len(inputs) + 1),
        out_specs=vmem,
        scratch_shapes=[pltpu.VMEM(one.shape, bf16) for one in inputs]
        + [
            pltpu.VMEM((blocks, UNIT, 128), bf16),
            pltpu.VMEM((256, rows), bf16),
            pltpu.SMEM((n, 1, 1, SEL), jnp.int32),
            pltpu.SMEM((4, max(n, SEL)), jnp.int32),
            pltpu.VMEM((n, cap, UNIT, 128), bf16),
            pltpu.VMEM(((n - 2 * staged) * cap, UNIT, 128), bf16),
            [pltpu.VMEM((size, UNIT, 128), bf16) for size in ([4, 2, 2] if staged else [])],
            pltpu.VMEM((n, UNIT, 128), bf16),
            pltpu.VMEM((wide, 256), bf16),
            pltpu.VMEM((144, wide), bf16),
            pltpu.VMEM((1, rows), f32),
            pltpu.VMEM((1, rows), f32),
            pltpu.VMEM((vwidth, rows), f32),
            pltpu.VMEM((1, rows), f32),
            pltpu.VMEM((1, rows), f32),
            pltpu.VMEM((vwidth, rows), f32),
            pltpu.VMEM((TILE, heads * vwidth), bf16),
            pltpu.VMEM((groups, heads * vwidth, columns), bf16),
            pltpu.VMEM((groups, TILE, columns), bf16),
            pltpu.VMEM((groups, TILE, columns), bf16),
            pltpu.VMEM((TILE, columns), f32),
            dma((len(inputs),)),
            dma((groups,)),
            dma((n,)),
            dma((n,)),
            dma((n, cap)),
            dma((n, cap)),
            dma((n // 2 + 1,)),
            dma((n // 2,)),
            dma((n // 2,)),
            dma((n // 2,)),
            dma((groups, 2)),
            dma((groups, 2)),
            pltpu.SemaphoreType.REGULAR((2,)),
        ],
        compiler_params=pltpu.CompilerParams(
            collective_id=0, has_side_effects=True, vmem_limit_bytes=60 * 1024 * 1024
        ),
    )(selected, selected, *inputs, out_weight)


def solution(mesh):
    return jax.shard_map(
        shards,
        mesh=mesh,
        in_specs=(
            P("seq", "grp", None),
            P("grp", "seq", None),
            P("grp", "seq", None),
            P("grp", "seq", None),
            P("grp", "seq", None),
            P("seq", None),
            P("grp", None, None),
            P("grp", None),
            P("grp", "seq", None),
        ),
        out_specs=P("seq", "grp"),
        check_vma=False,
    )
```

```python
import functools
import math

import jax
import jax.numpy as jnp
from jax import lax
from jax.experimental import pallas as pl
from jax.experimental.pallas import tpu as pltpu
from jax.sharding import PartitionSpec as P

BLK = 64
SEL = 16
TILE = 128
CSTRIDE = 16
CLEN = 32

NEGATIVE = -1e30
FAR = 1 << 28
MESH = pl.DeviceIdType.MESH
HALF = BLK // 2
UNIT = BLK + HALF + BLK
MARK = 1 << 16
PART = SEL // 4


def pack(keys, values, width):
    tail = keys[:, 128:width]
    folded = jnp.concatenate([tail[:HALF], tail[HALF:]], axis=1)
    return jnp.concatenate([keys[:, :128], folded, values], axis=0)


def unpack(block):
    folded = block[BLK : BLK + HALF]
    low = lax.broadcasted_iota(jnp.int32, folded.shape, 1) < 64
    zero = jnp.zeros_like(folded)
    tails = jnp.concatenate([jnp.where(low, folded, zero), jnp.where(low, zero, folded)], axis=0)
    return jnp.concatenate([block[:BLK], tails], axis=1), block[BLK + HALF :]


def bit_of(index, bit):
    return index // bit % 2 if isinstance(index, int) else lax.rem(index // bit, 2)


def flip(index, step, size):
    shared = 0
    bit = 1
    while bit < size:
        shared = shared + bit_of(index, bit) * bit_of(step, bit) * bit
        bit *= 2
    return index + step - 2 * shared


def exchanges(count):
    found = []
    p = 1
    while p < count:
        k = p
        while k >= 1:
            for j in range(k % p, count - k, 2 * k):
                for i in range(min(k, count - j - k)):
                    if (i + j) // (2 * p) == (i + j + k) // (2 * p):
                        found.append((i + j, i + j + k))
            k //= 2
        p *= 2
    return found


def picks(read, owner, blocks, cap):
    low = owner * blocks
    found = [jnp.int32(-1)] * cap
    count = jnp.int32(0)
    for entry in range(SEL):
        block = read(entry)
        here = (block >= low) & (block < low + blocks)
        for slot in range(cap):
            found[slot] = jnp.where(here & (count == slot), block, found[slot])
        count = count + here.astype(jnp.int32)
    return found


def kernel(
    n,
    groups,
    cap,
    scale,
    own_smem,
    own_table,
    query_hbm,
    key_hbm,
    value_hbm,
    ckey_hbm,
    cvalue_hbm,
    hidden_hbm,
    gate_hbm,
    weight_hbm,
    out_ref,
    query_ref,
    key_ref,
    value_ref,
    ckey_ref,
    cvalue_ref,
    hidden_ref,
    gate_ref,
    packed,
    query_wide,
    tables_smem,
    order_smem,
    outgoing,
    early,
    late,
    coarse,
    keys_wide,
    values_wide,
    picked_top,
    picked_sum,
    picked_out,
    coarse_top,
    coarse_sum,
    coarse_out,
    attended,
    weights,
    partial,
    arrived,
    own_part,
    input_sem,
    weight_sem,
    table_send,
    table_recv,
    slot_send,
    slot_recv,
    coarse_send,
    coarse_recv,
    pass_send,
    pass_recv,
    part_send,
    part_recv,
    hello,
):
    me = lax.axis_index("seq")
    group = lax.axis_index("grp")
    core = lax.rem(me, 2)
    sibling = me + 1 - 2 * core
    heads, width, _ = query_ref.shape
    blocks = value_ref.shape[0]
    columns = out_ref.shape[1]
    context = blocks * BLK * n
    span = 2 * TILE
    half = n // 2
    chips = n // 2
    staged = len(late) > 0
    ready = early.shape[0]
    starts = [ready, ready + 4, ready + 6]
    side = me // half
    outer = (me < half - 2) | (me >= half + 2)

    barrier = pltpu.get_barrier_semaphore()

    def greet(step, carry):
        pl.semaphore_signal(
            barrier, inc=1, device_id={"seq": flip(me, step, n)}, device_id_type=MESH
        )
        return carry

    inner = jnp.logical_not(outer)
    lax.fori_loop(1, half if staged else n, greet, 0)
    if staged:

        @pl.when(inner)
        def _():
            lax.fori_loop(n - 2, n, greet, 0)

    for step in range(1, groups):
        pl.semaphore_signal(
            barrier, inc=1, device_id={"grp": flip(group, step, groups)}, device_id_type=MESH
        )

    loads = [
        pltpu.make_async_copy(source, target, input_sem.at[index])
        for index, (source, target) in enumerate(
            [
                (ckey_hbm, ckey_ref),
                (cvalue_hbm, cvalue_ref),
                (key_hbm, key_ref),
                (value_hbm, value_ref),
                (query_hbm, query_ref),
                (hidden_hbm, hidden_ref),
                (gate_hbm, gate_ref),
            ]
        )
    ]
    for load in loads:
        load.start()

    def weight_copy(step):
        target = flip(group, step, groups)
        return pltpu.make_async_copy(
            weight_hbm.at[:, pl.ds(pl.multiple_of(target * columns, 128), columns)],
            weights.at[step],
            weight_sem.at[step],
        )

    for step in reversed(range(groups)):
        weight_copy(step).start()

    loads[0].wait()
    loads[1].wait()
    coarse[me] = pack(ckey_ref[...], cvalue_ref[...], width)
    loads[2].wait()
    loads[3].wait()
    for pair in range(blocks // 2):
        both = key_ref[:, pair * 128 : (pair + 1) * 128].T
        packed[2 * pair] = pack(both[:BLK], value_ref[2 * pair], width)
        packed[2 * pair + 1] = pack(both[BLK:], value_ref[2 * pair + 1], width)
    if not staged:
        pl.semaphore_wait(barrier, n - 1 + groups - 1)
    else:

        @pl.when(inner)
        def _():
            pl.semaphore_wait(barrier, half + 1 + groups - 1)

        @pl.when(outer)
        def _():
            pl.semaphore_wait(barrier, half - 1 + groups - 1)

    def say(kind, step):
        pl.semaphore_signal(
            hello.at[kind], inc=1, device_id={"seq": flip(me, step, n)}, device_id_type=MESH
        )


    def table_copy(step):
        return pltpu.make_async_remote_copy(
            src_ref=own_table,
            dst_ref=tables_smem.at[step],
            send_sem=table_send.at[step],
            recv_sem=table_recv.at[step],
            device_id={"seq": flip(me, step, n)},
            device_id_type=MESH,
        )

    def coarse_copy(held, bit, index=None):
        unit = coarse.at[flip(me, 2 * held, n)]
        landing = flip(held, bit, chips)
        return pltpu.make_async_remote_copy(
            src_ref=unit,
            dst_ref=unit,
            send_sem=coarse_send.at[landing if index is None else index],
            recv_sem=coarse_recv.at[landing],
            device_id={"seq": flip(me, 2 * bit, n)},
            device_id_type=MESH,
        )

    hops = [(0, 3), (0, 1), (1, 3), (3, 1), (2, 1)]

    def hop(index):
        return coarse_copy(*hops[index], index)

    def coarse_pass(held):
        coarse_wait(held)
        pass_copy(held).start()

    def coarse_wait(held):
        coarse_copy(0, held).wait_recv()

    def pass_copy(step):
        unit = coarse.at[flip(me, 2 * step, n)]
        return pltpu.make_async_remote_copy(
            src_ref=unit,
            dst_ref=unit,
            send_sem=pass_send.at[step],
            recv_sem=pass_recv.at[step],
            device_id={"seq": sibling},
            device_id_type=MESH,
        )

    def bits_below(bit):
        while bit > 1:
            bit //= 2
            yield bit

    def slot_copy(step, slot, late_one):
        if not staged:
            target = early.at[step * cap + slot]
        elif late_one:
            odd = lax.rem(step, 2)
            target = late[0].at[odd * 2 + slot] if slot < 2 else late[slot - 1].at[odd]
        else:
            place = jnp.where(step < half, step, half + lax.rem(step, 2))
            target = early.at[place * cap + slot]
        return pltpu.make_async_remote_copy(
            src_ref=outgoing.at[step, slot],
            dst_ref=target,
            send_sem=slot_send.at[step, slot],
            recv_sem=slot_recv.at[step, slot],
            device_id={"seq": flip(me, step, n)},
            device_id_type=MESH,
        )

    def send_table(step, carry):
        table_copy(step).start()
        return carry

    lax.fori_loop(1, half if staged else n, send_table, 0)

    if staged:

        @pl.when(inner)
        def _():
            say(0, n - 2)
            say(0, 2)
            lax.fori_loop(n - 2, n, send_table, 0)
            hop(0).start()

        hop(1).start()
    else:
        for bit in bits_below(chips):
            coarse_copy(0, bit).start()
    pass_copy(0).start()

    def fill_slots(step):
        table_copy(step).wait_recv()
        wanted = picks(lambda entry: tables_smem[step, 0, 0, entry], me, blocks, cap)
        for slot in range(cap):
            outgoing[step, slot] = packed[jnp.maximum(wanted[slot] - me * blocks, 0)]

    def send_near(step, carry):
        fill_slots(step)
        for slot in range(cap):
            slot_copy(step, slot, False).start()
        return carry

    def far_step(phase, chip):
        return flip(me, half - side + (1 - 2 * side) * (2 * chip + phase), n)

    def useful(owner, tile, slot):
        return (owner * blocks + slot) * BLK < context - TILE * n + (tile + 1) * TILE

    def send_far(phase, first, last):
        def fill_far(chip, carry):
            fill_slots(far_step(phase, chip))
            return carry

        lax.fori_loop(first, last, fill_far, 0)
        if not staged:

            def send_single(index, carry):
                step = far_step(phase, half // 2 - 1 - index)
                for slot in range(cap):
                    slot_copy(step, slot, False).start()
                return carry

            lax.fori_loop(0, half // 2, send_single, 0)
            return
        def send_order(lag, late_one):
            order = [
                (slot + lag * (half // 2 - 1 - chip), chip, slot)
                for chip in range(first, last)
                for slot in range(cap)
            ]
            for _, chip, slot in sorted(order):
                step = far_step(phase, chip)
                copy = slot_copy(step, slot, late_one)
                if slot < 2 or late_one:
                    copy.start()
                else:
                    pl.when(useful(me, flip(me, step, n), slot))(copy.start)

        @pl.when(outer)
        def _():
            send_order(1.5 if phase else -0.1, False)

        @pl.when(inner & (side == 0))
        def _():
            send_order(0.7 if phase else -0.1, True)

        @pl.when(inner & (side == 1))
        def _():
            send_order(2.5 if phase else -0.1, True)

    def send_chip(start, stop):
        lax.fori_loop(start, stop, send_near, 0)

    if staged:

        @pl.when(inner)
        def _():
            @pl.when(side == 0)
            def _():
                send_chip(2, half)

            send_far(0, 0, 1)
            pl.semaphore_wait(hello.at[0], 1)
            say(1, 2)
            lax.fori_loop(half, n - 2, send_table, 0)

            @pl.when(side == 1)
            def _():
                send_chip(2, half)

            coarse_pass(3)
            hop(3).start()
            send_far(0, 1, 2)
            coarse_pass(1)
            hop(2).start()
            coarse_pass(2)
            hop(4).start()

        @pl.when(outer)
        def _():
            pl.semaphore_wait(hello.at[0], 1)
            lax.fori_loop(half, n - 2, send_table, 0)
            pl.semaphore_wait(hello.at[1], 1)
            lax.fori_loop(n - 2, n, send_table, 0)
            send_chip(2, half)
            send_far(0, 0, 2)

        send_chip(1, 2)
        send_far(1, 0, 2)

        @pl.when(outer)
        def _():
            for held in (1, 2, 3):
                coarse_pass(held)
    else:
        for low in bits_below(chips):
            for held in range(low, chips, 2 * low):
                if low > 1:
                    coarse_pass(held)
                    for bit in bits_below(low):
                        coarse_copy(held, bit).start()
        send_chip(1, half)
        send_far(0, 0, half // 2)
        send_far(1, 0, half // 2)
        for held in range(1, chips, 2):
            coarse_pass(held)

    def rank(step, carry):
        owner = flip(me, step, n)
        if not staged:
            for line, value in enumerate([step * cap, step * cap, 1]):
                order_smem[line, owner] = value
        else:
            central = (owner >= half - 2) & (owner < half + 2)
            last = (step >= half) & central
            odd = lax.rem(step, 2)
            place = jnp.where(step < half, step, half + odd) * cap
            order_smem[0, owner] = jnp.where(last, ready + odd * 2, place)
            order_smem[1, owner] = jnp.where(last, ready + odd, place)
            order_smem[2, owner] = jnp.where(last, 2, 1)
        return carry

    lax.fori_loop(0, n, rank, 0)
    newest = (context - TILE * n + me * TILE) // (blocks * BLK)
    entries = [own_smem[0, 0, entry] for entry in range(SEL)]
    owners = [entry // blocks for entry in entries]
    marks = []
    for entry in range(SEL):
        slot = jnp.int32(0)
        for other in range(entry):
            slot = slot + (owners[other] == owners[entry]).astype(jnp.int32)
        place = jnp.where(
            slot < 2,
            order_smem[0, owners[entry]] + slot,
            order_smem[1, owners[entry]] + slot * order_smem[2, owners[entry]],
        )
        place = jnp.where(owners[entry] == newest, place, place + n * cap)
        marks.append(place * MARK + entries[entry])
    for low, high in exchanges(SEL):
        marks[low], marks[high] = (
            jnp.minimum(marks[low], marks[high]),
            jnp.maximum(marks[low], marks[high]),
        )
    for entry in range(SEL):
        order_smem[3, entry] = marks[entry]
    mine = picks(lambda entry: own_smem[0, 0, entry], me, blocks, cap)
    for slot in range(cap):
        early[slot] = packed[jnp.maximum(mine[slot] - me * blocks, 0)]

    loads[4].wait()
    for head in range(heads):
        one = query_ref[head]
        query_wide[:width, head * 128 : (head + 1) * 128] = one
        query_wide[width:, head * 128 : (head + 1) * 128] = one[128:]

    first_pos = context - TILE * n + me * TILE
    row = lax.broadcasted_iota(jnp.int32, (BLK, span), 0)
    query = lax.rem(lax.broadcasted_iota(jnp.int32, (BLK, span), 1), TILE)

    def fill(place, block):
        keys, values = unpack(block)
        keys_wide[place * BLK : (place + 1) * BLK] = keys
        return values

    def gate_row(index, kind):
        first_head = kind * heads + index * (span // TILE)
        return jnp.concatenate(
            [gates[first_head + other : first_head + other + 1] for other in range(span // TILE)],
            axis=1,
        )

    def close(index, picked, total):
        here = slice(index * span, (index + 1) * span)
        mixed = coarse_out[:, here] + picked * (gate_row(index, 1) / total)
        mixed = mixed.astype(jnp.bfloat16)
        for other in range(span // TILE):
            start = index * span + other * TILE
            attended[:, start : start + TILE] = mixed[:, other * TILE : (other + 1) * TILE].T

    def attend(count, bounds, stride, top_ref, sum_ref, out, first, closing=False):
        lag = row * stride - query
        total = heads * TILE // span

        def score(index):
            here = slice(index * span, (index + 1) * span)
            return jnp.dot(
                keys_wide[: count * BLK], query_wide[:, here], preferred_element_type=jnp.float32
            )

        def soft(index, scores):
            here = slice(index * span, (index + 1) * span)
            if bounds is not None:
                scores = jnp.concatenate(
                    [
                        jnp.where(lag <= bounds[block], scores[block * BLK : (block + 1) * BLK], -jnp.inf)
                        for block in range(count)
                    ],
                    axis=0,
                )
            top = jnp.max(scores, axis=0, keepdims=True)
            if first:
                new = jnp.maximum(top, NEGATIVE)
                factor = None
            else:
                old = top_ref[:, here]
                new = jnp.maximum(old, top)
                factor = jnp.exp2((old - new) * scale)
            if not closing:
                top_ref[:, here] = new
            return jnp.exp2((scores - new) * scale).astype(jnp.bfloat16), factor

        def value(index, exponents, factor):
            here = slice(index * span, (index + 1) * span)
            added = jnp.dot(
                values_wide[:, : count * BLK], exponents, preferred_element_type=jnp.float32
            )
            if first:
                out[:, here] = added[:128]
                sum_ref[:, here] = added[128:129]
            elif closing:
                close(
                    index,
                    out[:, here] * factor + added[:128],
                    sum_ref[:, here] * factor + added[128:129],
                )
            else:
                out[:, here] = out[:, here] * factor + added[:128]
                sum_ref[:, here] = sum_ref[:, here] * factor + added[128:129]

        ready = score(0)
        for index in range(total):
            later = score(index + 1) if index + 1 < total else None
            value(index, *soft(index, ready))
            ready = later

    values_wide[128:, :] = jnp.ones_like(values_wide[128:, :])

    def gather(mark, turn):
        place = lax.rem(mark // MARK, n * cap)
        block = early[jnp.where(place < ready, place, 0)]
        for index in range(turn):
            other = late[index]
            start = starts[index]
            block = jnp.where(
                place >= start, other[jnp.clip(place - start, 0, other.shape[0] - 1)], block
            )
        return block

    def attend_picked(turn, start, count, closing=False):
        marks = [order_smem[3, start + index] for index in range(count)]
        values = [fill(index, gather(mark, turn)) for index, mark in enumerate(marks)]
        values_wide[:128, : count * BLK] = jnp.concatenate(values, axis=0).T
        bounds = None
        if start == 0:
            bounds = [first_pos - lax.rem(mark, MARK) * BLK for mark in marks]
        attend(
            count, bounds, 1, picked_top, picked_sum, picked_out, start == 0, closing
        )

    loads[5].wait()
    loads[6].wait()
    gates = jax.nn.sigmoid(
        lax.dot_general(
            gate_ref[...],
            hidden_ref[...],
            (((1,), (1,)), ((), ())),
            preferred_element_type=jnp.float32,
        )
    )

    def passed(step, carry):
        pass_copy(step).wait_recv()
        return carry

    lax.fori_loop(0, n // 2, passed, 0)

    pieces = min(n, 8)

    def coarse_step(index, first):
        values = [fill(piece, coarse[index * pieces + piece]) for piece in range(pieces)]
        values_wide[:128, : pieces * BLK] = jnp.concatenate(values, axis=0).T
        start = first_pos - (CLEN - 1) - index * (pieces * BLK * CSTRIDE)
        bounds = [start - piece * (BLK * CSTRIDE) for piece in range(pieces)]
        attend(pieces, bounds, CSTRIDE, coarse_top, coarse_sum, coarse_out, first)

    coarse_step(0, True)
    if n > pieces:

        def coarse_more(index, carry):
            coarse_step(index, False)
            return carry

        lax.fori_loop(1, n // pieces, coarse_more, 0)

    for index in range(heads * TILE // span):
        here = slice(index * span, (index + 1) * span)
        coarse_out[:, here] = coarse_out[:, here] * (gate_row(index, 0) / coarse_sum[:, here])

    def wait_slots(start, stop, slots, late_one, base=None):
        def wait_one(index, carry):
            step = index if base is None else flip(me, base + index, n)
            for slot in slots:
                copy = slot_copy(step, slot, late_one)
                if base is None or slot < 2 or late_one:
                    copy.wait_recv()
                else:
                    pl.when(useful(flip(me, step, n), me, slot))(copy.wait_recv)
            return carry

        lax.fori_loop(start, stop, wait_one, 0)

    if not staged:
        wait_slots(1, n, range(cap), False)
        for start in range(0, SEL, PART):
            attend_picked(0, start, PART, start + PART == SEL)
    else:
        wait_slots(1, half, range(cap), False)
        wait_slots(0, 2, range(cap), False, (n - 2) * (1 - side))
        for start in range(0, SEL // 2, PART):
            attend_picked(0, start, PART)
        start = SEL // 2
        for turn, slots in enumerate([range(2), range(2, 3), range(3, 4)]):
            wait_slots(0, 2, slots, True, half - 2 * side)
            count = 2 * len(slots)
            attend_picked(turn + 1, start, count, turn == 2)
            start += count

    halves = [(0, columns // 256 * 128), (columns // 256 * 128, columns)]

    def part_copy(step, half_of):
        here = slice(*halves[half_of])
        return pltpu.make_async_remote_copy(
            src_ref=partial.at[step, :, here],
            dst_ref=arrived.at[step, :, here],
            send_sem=part_send.at[step, half_of],
            recv_sem=part_recv.at[step, half_of],
            device_id={"grp": flip(group, step, groups)},
            device_id_type=MESH,
        )

    for step in range(1, groups):
        weight_copy(step).wait()
    last = groups - 1
    turns = [(last, 0), (last - 1, 0), (last, 1)]
    turns += [(step, half_of) for step in range(1, last - 1) for half_of in range(2)]
    turns += [(last - 1, 1)]
    for step, half_of in turns:
        here = slice(*halves[half_of])
        partial[step, :, here] = jnp.dot(
            attended[...], weights[step, :, here], preferred_element_type=jnp.float32
        ).astype(jnp.bfloat16)
        part_copy(step, half_of).start()
    weight_copy(0).wait()
    own_part[...] = jnp.dot(attended[...], weights[0], preferred_element_type=jnp.float32)

    def sent(step, carry):
        table_copy(step).wait_send()
        return carry

    lax.fori_loop(1, n, sent, 0)

    def sent_slots(step, carry):
        for slot in range(cap):
            copy = slot_copy(step, slot, False)
            if slot < 2 or not staged:
                copy.wait_send()
            else:
                pl.when(useful(me, flip(me, step, n), slot))(copy.wait_send)
        return carry

    lax.fori_loop(1, n, sent_slots, 0)
    for held in range(chips):
        if held and not staged:
            coarse_copy(0, held).wait_send()
        pass_copy(held).wait_send()
    if staged:
        hop(1).wait_send()

        @pl.when(inner)
        def _():
            for index in (0, 2, 3, 4):
                hop(index).wait_send()

    total = own_part[...]
    for step in range(1, groups):
        for half_of in range(2):
            part_copy(step, half_of).wait_recv()
        total = total + arrived[step].astype(jnp.float32)
    out_ref[...] = total.astype(out_ref.dtype)
    for step in range(1, groups):
        for half_of in range(2):
            part_copy(step, half_of).wait_send()


def shards(
    queries,
    key_cache,
    group_value_cache,
    coarse_keys,
    coarse_values,
    hidden,
    gate_weight,
    out_weight,
    selected,
):
    n = lax.axis_size("seq")
    groups = lax.axis_size("grp")
    ctx_dev = key_cache.shape[1]
    heads = queries.shape[1]
    width = queries.shape[2]
    vwidth = group_value_cache.shape[2]
    rows = TILE * heads
    blocks = ctx_dev // BLK
    cap = max(1, 2 * SEL // n)
    columns = out_weight.shape[1] // groups
    pieces = min(n, 8)
    wide = max(pieces, PART) * BLK
    staged = n == 8 and cap == 4 and n * TILE <= ctx_dev

    vmem = pl.BlockSpec(memory_space=pltpu.VMEM)
    hbm = pl.BlockSpec(memory_space=pl.ANY)
    dma = pltpu.SemaphoreType.DMA
    bf16, f32 = jnp.bfloat16, jnp.float32
    inputs = (
        queries.transpose(1, 2, 0),
        key_cache[0].T,
        group_value_cache.reshape(blocks, BLK, vwidth),
        coarse_keys[0],
        coarse_values[0],
        hidden,
        gate_weight[0].T,
    )
    return pl.pallas_call(
        functools.partial(kernel, n, groups, cap, width**-0.5 * math.log2(math.e)),
        out_shape=pltpu.VMEM((TILE, columns), bf16),
        in_specs=[pl.BlockSpec(memory_space=pltpu.SMEM), vmem] + [hbm] * (len(inputs) + 1),
        out_specs=vmem,
        scratch_shapes=[pltpu.VMEM(one.shape, bf16) for one in inputs]
        + [
            pltpu.VMEM((blocks, UNIT, 128), bf16),
            pltpu.VMEM((256, rows), bf16),
            pltpu.SMEM((n, 1, 1, SEL), jnp.int32),
            pltpu.SMEM((4, max(n, SEL)), jnp.int32),
            pltpu.VMEM((n, cap, UNIT, 128), bf16),
            pltpu.VMEM(((n - 2 * staged) * cap, UNIT, 128), bf16),
            [pltpu.VMEM((size, UNIT, 128), bf16) for size in ([4, 2, 2] if staged else [])],
            pltpu.VMEM((n, UNIT, 128), bf16),
            pltpu.VMEM((wide, 256), bf16),
            pltpu.VMEM((144, wide), bf16),
            pltpu.VMEM((1, rows), f32),
            pltpu.VMEM((1, rows), f32),
            pltpu.VMEM((vwidth, rows), f32),
            pltpu.VMEM((1, rows), f32),
            pltpu.VMEM((1, rows), f32),
            pltpu.VMEM((vwidth, rows), f32),
            pltpu.VMEM((TILE, heads * vwidth), bf16),
            pltpu.VMEM((groups, heads * vwidth, columns), bf16),
            pltpu.VMEM((groups, TILE, columns), bf16),
            pltpu.VMEM((groups, TILE, columns), bf16),
            pltpu.VMEM((TILE, columns), f32),
            dma((len(inputs),)),
            dma((groups,)),
            dma((n,)),
            dma((n,)),
            dma((n, cap)),
            dma((n, cap)),
            dma((n // 2 + 1,)),
            dma((n // 2,)),
            dma((n // 2,)),
            dma((n // 2,)),
            dma((groups, 2)),
            dma((groups, 2)),
            pltpu.SemaphoreType.REGULAR((2,)),
        ],
        compiler_params=pltpu.CompilerParams(
            collective_id=0, has_side_effects=True, vmem_limit_bytes=60 * 1024 * 1024
        ),
    )(selected, selected, *inputs, out_weight)


def solution(mesh):
    return jax.shard_map(
        shards,
        mesh=mesh,
        in_specs=(
            P("seq", "grp", None),
            P("grp", "seq", None),
            P("grp", "seq", None),
            P("grp", "seq", None),
            P("grp", "seq", None),
            P("seq", None),
            P("grp", None, None),
            P("grp", None),
            P("grp", "seq", None),
        ),
        out_specs=P("seq", "grp"),
        check_vma=False,
    )
```

```python
import functools
import math

import jax
import jax.numpy as jnp
from jax import lax
from jax.experimental import pallas as pl
from jax.experimental.pallas import tpu as pltpu
from jax.sharding import PartitionSpec as P

BLK = 64
SEL = 16
TILE = 128
CSTRIDE = 16
CLEN = 32

NEGATIVE = -1e30
FAR = 1 << 28
MESH = pl.DeviceIdType.MESH
HALF = BLK // 2
UNIT = BLK + HALF + BLK
MARK = 1 << 16
PART = SEL // 4


def pack(keys, values, width):
    tail = keys[:, 128:width]
    folded = jnp.concatenate([tail[:HALF], tail[HALF:]], axis=1)
    return jnp.concatenate([keys[:, :128], folded, values], axis=0)


def unpack(block):
    folded = block[BLK : BLK + HALF]
    low = lax.broadcasted_iota(jnp.int32, folded.shape, 1) < 64
    zero = jnp.zeros_like(folded)
    tails = jnp.concatenate([jnp.where(low, folded, zero), jnp.where(low, zero, folded)], axis=0)
    return jnp.concatenate([block[:BLK], tails], axis=1), block[BLK + HALF :]


def bit_of(index, bit):
    return index // bit % 2 if isinstance(index, int) else lax.rem(index // bit, 2)


def flip(index, step, size):
    shared = 0
    bit = 1
    while bit < size:
        shared = shared + bit_of(index, bit) * bit_of(step, bit) * bit
        bit *= 2
    return index + step - 2 * shared


def exchanges(count):
    found = []
    p = 1
    while p < count:
        k = p
        while k >= 1:
            for j in range(k % p, count - k, 2 * k):
                for i in range(min(k, count - j - k)):
                    if (i + j) // (2 * p) == (i + j + k) // (2 * p):
                        found.append((i + j, i + j + k))
            k //= 2
        p *= 2
    return found


def picks(read, owner, blocks, cap):
    low = owner * blocks
    found = [jnp.int32(-1)] * cap
    count = jnp.int32(0)
    for entry in range(SEL):
        block = read(entry)
        here = (block >= low) & (block < low + blocks)
        for slot in range(cap):
            found[slot] = jnp.where(here & (count == slot), block, found[slot])
        count = count + here.astype(jnp.int32)
    return found


def kernel(
    n,
    groups,
    cap,
    scale,
    own_smem,
    own_table,
    query_hbm,
    key_hbm,
    value_hbm,
    ckey_hbm,
    cvalue_hbm,
    hidden_hbm,
    gate_hbm,
    weight_hbm,
    out_ref,
    query_ref,
    key_ref,
    value_ref,
    ckey_ref,
    cvalue_ref,
    hidden_ref,
    gate_ref,
    packed,
    query_wide,
    tables_smem,
    order_smem,
    outgoing,
    early,
    late,
    coarse,
    keys_wide,
    values_wide,
    picked_top,
    picked_sum,
    picked_out,
    coarse_top,
    coarse_sum,
    coarse_out,
    attended,
    weights,
    partial,
    arrived,
    own_part,
    input_sem,
    weight_sem,
    table_send,
    table_recv,
    slot_send,
    slot_recv,
    coarse_send,
    coarse_recv,
    pass_send,
    pass_recv,
    part_send,
    part_recv,
    hello,
):
    me = lax.axis_index("seq")
    group = lax.axis_index("grp")
    core = lax.rem(me, 2)
    sibling = me + 1 - 2 * core
    heads, width, _ = query_ref.shape
    blocks = value_ref.shape[0]
    columns = out_ref.shape[1]
    context = blocks * BLK * n
    span = 2 * TILE
    half = n // 2
    chips = n // 2
    staged = len(late) > 0
    ready = early.shape[0]
    starts = [ready, ready + 4, ready + 6]
    side = me // half
    outer = (me < half - 2) | (me >= half + 2)

    barrier = pltpu.get_barrier_semaphore()

    def greet(step, carry):
        pl.semaphore_signal(
            barrier, inc=1, device_id={"seq": flip(me, step, n)}, device_id_type=MESH
        )
        return carry

    inner = jnp.logical_not(outer)
    lax.fori_loop(1, half if staged else n, greet, 0)
    if staged:

        @pl.when(inner)
        def _():
            lax.fori_loop(n - 2, n, greet, 0)

    for step in range(1, groups):
        pl.semaphore_signal(
            barrier, inc=1, device_id={"grp": flip(group, step, groups)}, device_id_type=MESH
        )

    loads = [
        pltpu.make_async_copy(source, target, input_sem.at[index])
        for index, (source, target) in enumerate(
            [
                (ckey_hbm, ckey_ref),
                (cvalue_hbm, cvalue_ref),
                (key_hbm, key_ref),
                (value_hbm, value_ref),
                (query_hbm, query_ref),
                (hidden_hbm, hidden_ref),
                (gate_hbm, gate_ref),
            ]
        )
    ]
    for load in loads:
        load.start()

    def weight_copy(step):
        target = flip(group, step, groups)
        return pltpu.make_async_copy(
            weight_hbm.at[:, pl.ds(pl.multiple_of(target * columns, 128), columns)],
            weights.at[step],
            weight_sem.at[step],
        )

    for step in reversed(range(groups)):
        weight_copy(step).start()

    loads[0].wait()
    loads[1].wait()
    coarse[me] = pack(ckey_ref[...], cvalue_ref[...], width)
    loads[2].wait()
    loads[3].wait()
    for pair in range(blocks // 2):
        both = key_ref[:, pair * 128 : (pair + 1) * 128].T
        packed[2 * pair] = pack(both[:BLK], value_ref[2 * pair], width)
        packed[2 * pair + 1] = pack(both[BLK:], value_ref[2 * pair + 1], width)
    if not staged:
        pl.semaphore_wait(barrier, n - 1 + groups - 1)
    else:

        @pl.when(inner)
        def _():
            pl.semaphore_wait(barrier, half + 1 + groups - 1)

        @pl.when(outer)
        def _():
            pl.semaphore_wait(barrier, half - 1 + groups - 1)

    def say(kind, step):
        pl.semaphore_signal(
            hello.at[kind], inc=1, device_id={"seq": flip(me, step, n)}, device_id_type=MESH
        )


    def table_copy(step):
        return pltpu.make_async_remote_copy(
            src_ref=own_table,
            dst_ref=tables_smem.at[step],
            send_sem=table_send.at[step],
            recv_sem=table_recv.at[step],
            device_id={"seq": flip(me, step, n)},
            device_id_type=MESH,
        )

    def coarse_copy(held, bit, index=None):
        unit = coarse.at[flip(me, 2 * held, n)]
        landing = flip(held, bit, chips)
        return pltpu.make_async_remote_copy(
            src_ref=unit,
            dst_ref=unit,
            send_sem=coarse_send.at[landing if index is None else index],
            recv_sem=coarse_recv.at[landing],
            device_id={"seq": flip(me, 2 * bit, n)},
            device_id_type=MESH,
        )

    hops = [(0, 3), (0, 1), (1, 3), (3, 1), (2, 1)]

    def hop(index):
        return coarse_copy(*hops[index], index)

    def coarse_pass(held):
        coarse_wait(held)
        pass_copy(held).start()

    def coarse_wait(held):
        coarse_copy(0, held).wait_recv()

    def pass_copy(step):
        unit = coarse.at[flip(me, 2 * step, n)]
        return pltpu.make_async_remote_copy(
            src_ref=unit,
            dst_ref=unit,
            send_sem=pass_send.at[step],
            recv_sem=pass_recv.at[step],
            device_id={"seq": sibling},
            device_id_type=MESH,
        )

    def bits_below(bit):
        while bit > 1:
            bit //= 2
            yield bit

    def slot_copy(step, slot, late_one):
        if not staged:
            target = early.at[step * cap + slot]
        elif late_one:
            odd = lax.rem(step, 2)
            target = late[0].at[odd * 2 + slot] if slot < 2 else late[slot - 1].at[odd]
        else:
            place = jnp.where(step < half, step, half + lax.rem(step, 2))
            target = early.at[place * cap + slot]
        return pltpu.make_async_remote_copy(
            src_ref=outgoing.at[step, slot],
            dst_ref=target,
            send_sem=slot_send.at[step, slot],
            recv_sem=slot_recv.at[step, slot],
            device_id={"seq": flip(me, step, n)},
            device_id_type=MESH,
        )

    def send_table(step, carry):
        table_copy(step).start()
        return carry

    lax.fori_loop(1, half if staged else n, send_table, 0)

    if staged:

        @pl.when(inner)
        def _():
            say(0, n - 2)
            say(0, 2)
            lax.fori_loop(n - 2, n, send_table, 0)
            hop(0).start()

        hop(1).start()
    else:
        for bit in bits_below(chips):
            coarse_copy(0, bit).start()
    pass_copy(0).start()

    def fill_slots(step):
        table_copy(step).wait_recv()
        wanted = picks(lambda entry: tables_smem[step, 0, 0, entry], me, blocks, cap)
        for slot in range(cap):
            outgoing[step, slot] = packed[jnp.maximum(wanted[slot] - me * blocks, 0)]

    def send_near(step, carry):
        fill_slots(step)
        for slot in range(cap):
            slot_copy(step, slot, False).start()
        return carry

    def far_step(phase, chip):
        return flip(me, half - side + (1 - 2 * side) * (2 * chip + phase), n)

    def useful(owner, tile, slot):
        return (owner * blocks + slot) * BLK < context - TILE * n + (tile + 1) * TILE

    def send_far(phase, first, last):
        def fill_far(chip, carry):
            fill_slots(far_step(phase, chip))
            return carry

        lax.fori_loop(first, last, fill_far, 0)
        if not staged:

            def send_single(index, carry):
                step = far_step(phase, half // 2 - 1 - index)
                for slot in range(cap):
                    slot_copy(step, slot, False).start()
                return carry

            lax.fori_loop(0, half // 2, send_single, 0)
            return
        def send_order(lag, late_one):
            order = [
                (slot + lag * (half // 2 - 1 - chip), chip, slot)
                for chip in range(first, last)
                for slot in range(cap)
            ]
            for _, chip, slot in sorted(order):
                step = far_step(phase, chip)
                copy = slot_copy(step, slot, late_one)
                if slot < 2 or late_one:
                    copy.start()
                else:
                    pl.when(useful(me, flip(me, step, n), slot))(copy.start)

        @pl.when(outer)
        def _():
            send_order(1.5 if phase else -0.1, False)

        @pl.when(inner & (side == 0))
        def _():
            send_order(0.7 if phase else -0.1, True)

        @pl.when(inner & (side == 1))
        def _():
            send_order(2.5 if phase else -0.1, True)

    def send_chip(start, stop):
        lax.fori_loop(start, stop, send_near, 0)

    if staged:

        @pl.when(inner)
        def _():
            @pl.when(side == 0)
            def _():
                send_chip(2, half)

            send_far(0, 0, 1)
            pl.semaphore_wait(hello.at[0], 1)
            say(1, 2)
            lax.fori_loop(half, n - 2, send_table, 0)

            @pl.when(side == 1)
            def _():
                send_chip(2, half)

            send_far(0, 1, 2)
            coarse_pass(3)
            hop(3).start()
            coarse_pass(1)
            hop(2).start()
            coarse_pass(2)
            hop(4).start()

        @pl.when(outer)
        def _():
            pl.semaphore_wait(hello.at[0], 1)
            lax.fori_loop(half, n - 2, send_table, 0)
            pl.semaphore_wait(hello.at[1], 1)
            lax.fori_loop(n - 2, n, send_table, 0)
            send_chip(2, half)
            send_far(0, 0, 2)

        send_chip(1, 2)
        send_far(1, 0, 2)

        @pl.when(outer)
        def _():
            for held in (1, 2, 3):
                coarse_pass(held)
    else:
        for low in bits_below(chips):
            for held in range(low, chips, 2 * low):
                if low > 1:
                    coarse_pass(held)
                    for bit in bits_below(low):
                        coarse_copy(held, bit).start()
        send_chip(1, half)
        send_far(0, 0, half // 2)
        send_far(1, 0, half // 2)
        for held in range(1, chips, 2):
            coarse_pass(held)

    def rank(step, carry):
        owner = flip(me, step, n)
        if not staged:
            for line, value in enumerate([step * cap, step * cap, 1]):
                order_smem[line, owner] = value
        else:
            central = (owner >= half - 2) & (owner < half + 2)
            last = (step >= half) & central
            odd = lax.rem(step, 2)
            place = jnp.where(step < half, step, half + odd) * cap
            order_smem[0, owner] = jnp.where(last, ready + odd * 2, place)
            order_smem[1, owner] = jnp.where(last, ready + odd, place)
            order_smem[2, owner] = jnp.where(last, 2, 1)
        return carry

    lax.fori_loop(0, n, rank, 0)
    newest = (context - TILE * n + me * TILE) // (blocks * BLK)
    entries = [own_smem[0, 0, entry] for entry in range(SEL)]
    owners = [entry // blocks for entry in entries]
    marks = []
    for entry in range(SEL):
        slot = jnp.int32(0)
        for other in range(entry):
            slot = slot + (owners[other] == owners[entry]).astype(jnp.int32)
        place = jnp.where(
            slot < 2,
            order_smem[0, owners[entry]] + slot,
            order_smem[1, owners[entry]] + slot * order_smem[2, owners[entry]],
        )
        place = jnp.where(owners[entry] == newest, place, place + n * cap)
        marks.append(place * MARK + entries[entry])
    for low, high in exchanges(SEL):
        marks[low], marks[high] = (
            jnp.minimum(marks[low], marks[high]),
            jnp.maximum(marks[low], marks[high]),
        )
    for entry in range(SEL):
        order_smem[3, entry] = marks[entry]
    mine = picks(lambda entry: own_smem[0, 0, entry], me, blocks, cap)
    for slot in range(cap):
        early[slot] = packed[jnp.maximum(mine[slot] - me * blocks, 0)]

    loads[4].wait()
    for head in range(heads):
        one = query_ref[head]
        query_wide[:width, head * 128 : (head + 1) * 128] = one
        query_wide[width:, head * 128 : (head + 1) * 128] = one[128:]

    first_pos = context - TILE * n + me * TILE
    row = lax.broadcasted_iota(jnp.int32, (BLK, span), 0)
    query = lax.rem(lax.broadcasted_iota(jnp.int32, (BLK, span), 1), TILE)

    def fill(place, block):
        keys, values = unpack(block)
        keys_wide[place * BLK : (place + 1) * BLK] = keys
        return values

    def gate_row(index, kind):
        first_head = kind * heads + index * (span // TILE)
        return jnp.concatenate(
            [gates[first_head + other : first_head + other + 1] for other in range(span // TILE)],
            axis=1,
        )

    def close(index, picked, total):
        here = slice(index * span, (index + 1) * span)
        mixed = coarse_out[:, here] + picked * (gate_row(index, 1) / total)
        mixed = mixed.astype(jnp.bfloat16)
        for other in range(span // TILE):
            start = index * span + other * TILE
            attended[:, start : start + TILE] = mixed[:, other * TILE : (other + 1) * TILE].T

    def attend(count, bounds, stride, top_ref, sum_ref, out, first, closing=False):
        lag = row * stride - query
        total = heads * TILE // span

        def score(index):
            here = slice(index * span, (index + 1) * span)
            return jnp.dot(
                keys_wide[: count * BLK], query_wide[:, here], preferred_element_type=jnp.float32
            )

        def soft(index, scores):
            here = slice(index * span, (index + 1) * span)
            if bounds is not None:
                scores = jnp.concatenate(
                    [
                        jnp.where(lag <= bounds[block], scores[block * BLK : (block + 1) * BLK], -jnp.inf)
                        for block in range(count)
                    ],
                    axis=0,
                )
            top = jnp.max(scores, axis=0, keepdims=True)
            if first:
                new = jnp.maximum(top, NEGATIVE)
                factor = None
            else:
                old = top_ref[:, here]
                new = jnp.maximum(old, top)
                factor = jnp.exp2((old - new) * scale)
            if not closing:
                top_ref[:, here] = new
            return jnp.exp2((scores - new) * scale).astype(jnp.bfloat16), factor

        def value(index, exponents, factor):
            here = slice(index * span, (index + 1) * span)
            added = jnp.dot(
                values_wide[:, : count * BLK], exponents, preferred_element_type=jnp.float32
            )
            if first:
                out[:, here] = added[:128]
                sum_ref[:, here] = added[128:129]
            elif closing:
                close(
                    index,
                    out[:, here] * factor + added[:128],
                    sum_ref[:, here] * factor + added[128:129],
                )
            else:
                out[:, here] = out[:, here] * factor + added[:128]
                sum_ref[:, here] = sum_ref[:, here] * factor + added[128:129]

        ready = score(0)
        for index in range(total):
            later = score(index + 1) if index + 1 < total else None
            value(index, *soft(index, ready))
            ready = later

    values_wide[128:, :] = jnp.ones_like(values_wide[128:, :])

    def gather(mark, turn):
        place = lax.rem(mark // MARK, n * cap)
        block = early[jnp.where(place < ready, place, 0)]
        for index in range(turn):
            other = late[index]
            start = starts[index]
            block = jnp.where(
                place >= start, other[jnp.clip(place - start, 0, other.shape[0] - 1)], block
            )
        return block

    def attend_picked(turn, start, count, closing=False):
        marks = [order_smem[3, start + index] for index in range(count)]
        values = [fill(index, gather(mark, turn)) for index, mark in enumerate(marks)]
        values_wide[:128, : count * BLK] = jnp.concatenate(values, axis=0).T
        bounds = None
        if start == 0:
            bounds = [first_pos - lax.rem(mark, MARK) * BLK for mark in marks]
        attend(
            count, bounds, 1, picked_top, picked_sum, picked_out, start == 0, closing
        )

    loads[5].wait()
    loads[6].wait()
    gates = jax.nn.sigmoid(
        lax.dot_general(
            gate_ref[...],
            hidden_ref[...],
            (((1,), (1,)), ((), ())),
            preferred_element_type=jnp.float32,
        )
    )

    def passed(step, carry):
        pass_copy(step).wait_recv()
        return carry

    lax.fori_loop(0, n // 2, passed, 0)

    pieces = min(n, 8)

    def coarse_step(index, first):
        values = [fill(piece, coarse[index * pieces + piece]) for piece in range(pieces)]
        values_wide[:128, : pieces * BLK] = jnp.concatenate(values, axis=0).T
        start = first_pos - (CLEN - 1) - index * (pieces * BLK * CSTRIDE)
        bounds = [start - piece * (BLK * CSTRIDE) for piece in range(pieces)]
        attend(pieces, bounds, CSTRIDE, coarse_top, coarse_sum, coarse_out, first)

    coarse_step(0, True)
    if n > pieces:

        def coarse_more(index, carry):
            coarse_step(index, False)
            return carry

        lax.fori_loop(1, n // pieces, coarse_more, 0)

    for index in range(heads * TILE // span):
        here = slice(index * span, (index + 1) * span)
        coarse_out[:, here] = coarse_out[:, here] * (gate_row(index, 0) / coarse_sum[:, here])

    def wait_slots(start, stop, slots, late_one, base=None):
        def wait_one(index, carry):
            step = index if base is None else flip(me, base + index, n)
            for slot in slots:
                copy = slot_copy(step, slot, late_one)
                if base is None or slot < 2 or late_one:
                    copy.wait_recv()
                else:
                    pl.when(useful(flip(me, step, n), me, slot))(copy.wait_recv)
            return carry

        lax.fori_loop(start, stop, wait_one, 0)

    if not staged:
        wait_slots(1, n, range(cap), False)
        for start in range(0, SEL, PART):
            attend_picked(0, start, PART, start + PART == SEL)
    else:
        wait_slots(1, half, range(cap), False)
        wait_slots(0, 2, range(cap), False, (n - 2) * (1 - side))
        for start in range(0, SEL // 2, PART):
            attend_picked(0, start, PART)
        start = SEL // 2
        for turn, slots in enumerate([range(2), range(2, 3), range(3, 4)]):
            wait_slots(0, 2, slots, True, half - 2 * side)
            count = 2 * len(slots)
            attend_picked(turn + 1, start, count, turn == 2)
            start += count

    halves = [(0, columns // 256 * 128), (columns // 256 * 128, columns)]

    def part_copy(step, half_of):
        here = slice(*halves[half_of])
        return pltpu.make_async_remote_copy(
            src_ref=partial.at[step, :, here],
            dst_ref=arrived.at[step, :, here],
            send_sem=part_send.at[step, half_of],
            recv_sem=part_recv.at[step, half_of],
            device_id={"grp": flip(group, step, groups)},
            device_id_type=MESH,
        )

    for step in range(1, groups):
        weight_copy(step).wait()
    last = groups - 1
    turns = [(last, 0), (last - 1, 0), (last, 1)]
    turns += [(step, half_of) for step in range(1, last - 1) for half_of in range(2)]
    turns += [(last - 1, 1)]
    for step, half_of in turns:
        here = slice(*halves[half_of])
        partial[step, :, here] = jnp.dot(
            attended[...], weights[step, :, here], preferred_element_type=jnp.float32
        ).astype(jnp.bfloat16)
        part_copy(step, half_of).start()
    weight_copy(0).wait()
    own_part[...] = jnp.dot(attended[...], weights[0], preferred_element_type=jnp.float32)

    def sent(step, carry):
        table_copy(step).wait_send()
        return carry

    lax.fori_loop(1, n, sent, 0)

    def sent_slots(step, carry):
        for slot in range(cap):
            copy = slot_copy(step, slot, False)
            if slot < 2 or not staged:
                copy.wait_send()
            else:
                pl.when(useful(me, flip(me, step, n), slot))(copy.wait_send)
        return carry

    lax.fori_loop(1, n, sent_slots, 0)
    for held in range(chips):
        if held and not staged:
            coarse_copy(0, held).wait_send()
        pass_copy(held).wait_send()
    if staged:
        hop(1).wait_send()

        @pl.when(inner)
        def _():
            for index in (0, 2, 3, 4):
                hop(index).wait_send()

    total = own_part[...]
    for step in range(1, groups):
        for half_of in range(2):
            part_copy(step, half_of).wait_recv()
        total = total + arrived[step].astype(jnp.float32)
    out_ref[...] = total.astype(out_ref.dtype)
    for step in range(1, groups):
        for half_of in range(2):
            part_copy(step, half_of).wait_send()


def shards(
    queries,
    key_cache,
    group_value_cache,
    coarse_keys,
    coarse_values,
    hidden,
    gate_weight,
    out_weight,
    selected,
):
    n = lax.axis_size("seq")
    groups = lax.axis_size("grp")
    ctx_dev = key_cache.shape[1]
    heads = queries.shape[1]
    width = queries.shape[2]
    vwidth = group_value_cache.shape[2]
    rows = TILE * heads
    blocks = ctx_dev // BLK
    cap = max(1, 2 * SEL // n)
    columns = out_weight.shape[1] // groups
    pieces = min(n, 8)
    wide = max(pieces, PART) * BLK
    staged = n == 8 and cap == 4 and n * TILE <= ctx_dev

    vmem = pl.BlockSpec(memory_space=pltpu.VMEM)
    hbm = pl.BlockSpec(memory_space=pl.ANY)
    dma = pltpu.SemaphoreType.DMA
    bf16, f32 = jnp.bfloat16, jnp.float32
    inputs = (
        queries.transpose(1, 2, 0),
        key_cache[0].T,
        group_value_cache.reshape(blocks, BLK, vwidth),
        coarse_keys[0],
        coarse_values[0],
        hidden,
        gate_weight[0].T,
    )
    return pl.pallas_call(
        functools.partial(kernel, n, groups, cap, width**-0.5 * math.log2(math.e)),
        out_shape=pltpu.VMEM((TILE, columns), bf16),
        in_specs=[pl.BlockSpec(memory_space=pltpu.SMEM), vmem] + [hbm] * (len(inputs) + 1),
        out_specs=vmem,
        scratch_shapes=[pltpu.VMEM(one.shape, bf16) for one in inputs]
        + [
            pltpu.VMEM((blocks, UNIT, 128), bf16),
            pltpu.VMEM((256, rows), bf16),
            pltpu.SMEM((n, 1, 1, SEL), jnp.int32),
            pltpu.SMEM((4, max(n, SEL)), jnp.int32),
            pltpu.VMEM((n, cap, UNIT, 128), bf16),
            pltpu.VMEM(((n - 2 * staged) * cap, UNIT, 128), bf16),
            [pltpu.VMEM((size, UNIT, 128), bf16) for size in ([4, 2, 2] if staged else [])],
            pltpu.VMEM((n, UNIT, 128), bf16),
            pltpu.VMEM((wide, 256), bf16),
            pltpu.VMEM((144, wide), bf16),
            pltpu.VMEM((1, rows), f32),
            pltpu.VMEM((1, rows), f32),
            pltpu.VMEM((vwidth, rows), f32),
            pltpu.VMEM((1, rows), f32),
            pltpu.VMEM((1, rows), f32),
            pltpu.VMEM((vwidth, rows), f32),
            pltpu.VMEM((TILE, heads * vwidth), bf16),
            pltpu.VMEM((groups, heads * vwidth, columns), bf16),
            pltpu.VMEM((groups, TILE, columns), bf16),
            pltpu.VMEM((groups, TILE, columns), bf16),
            pltpu.VMEM((TILE, columns), f32),
            dma((len(inputs),)),
            dma((groups,)),
            dma((n,)),
            dma((n,)),
            dma((n, cap)),
            dma((n, cap)),
            dma((n // 2 + 1,)),
            dma((n // 2,)),
            dma((n // 2,)),
            dma((n // 2,)),
            dma((groups, 2)),
            dma((groups, 2)),
            pltpu.SemaphoreType.REGULAR((2,)),
        ],
        compiler_params=pltpu.CompilerParams(
            collective_id=0, has_side_effects=True, vmem_limit_bytes=60 * 1024 * 1024
        ),
    )(selected, selected, *inputs, out_weight)


def solution(mesh):
    return jax.shard_map(
        shards,
        mesh=mesh,
        in_specs=(
            P("seq", "grp", None),
            P("grp", "seq", None),
            P("grp", "seq", None),
            P("grp", "seq", None),
            P("grp", "seq", None),
            P("seq", None),
            P("grp", None, None),
            P("grp", None),
            P("grp", "seq", None),
        ),
        out_specs=P("seq", "grp"),
        check_vma=False,
    )
```
